128 devices in a mesh: tm: 32 (over z, x, core), cam: 4 (over y).
Axes of the slice: x: 4, y: 4, z: 4, core: 2. Of those that a mesh axis runs over, the one named last changes fastest.
Arguments:
- tokens: bfloat16 [4, 32, 512, 1536], P('cam', 'tm'), may hold values from -6 to 6
- w_query: bfloat16 [1536, 768], replicated, may hold values from -18 to 18
- w_key: bfloat16 [1536, 768], replicated, may hold values from -1 to 1
- w_value: bfloat16 [1536, 768], replicated, may hold values from -0.15625 to 0.15625
- w_out: bfloat16 [768, 1536], replicated, may hold values from -1.75 to 1.75
- grad_update: bfloat16 [4, 32, 512, 1536], P('cam', 'tm'), may hold values from -6 to 6
- memory_offsets: int32 [32, 4], replicated, may hold values from 1 to 31, as said below
- strip_count: int32 [4, 4], replicated, may hold values from 0 to 2, as said below
- strip_index: int32 [4, 4, 2], replicated, may hold values from 0 to 3, as said below
Outputs:
- update: bfloat16 [4, 32, 512, 1536], P('cam', 'tm')
- grad_tokens: bfloat16 [4, 32, 512, 1536], P('cam', 'tm')
The draws below stay inside these ranges and needn't reach their ends.
Inputs may be any that keep to these rules, and one draw needn't show every extreme that they name: `memory_offsets`: every entry of row f is at most max(f, 1). strip_count[c, c] is 0. For every camera c the sum over s of strip_count[s, c] is at most 4; it is exactly 4 for some camera, and some entry is 2. The 2 entries of strip_index[s, c] are different.
All inputs are finite; a program needn't handle non-finite values.
Results may differ from the reference program's by a relative error of at most 0.0085.
The reference program's roundings to bfloat16 on the way count: a program that leaves them out, or rounds other values in their place, can miss the bound.
Values may be sent and summed in bfloat16 or wider, within the bound.
No kernel may reach another device: no remote copies, remote signals or barrier semaphores. Data moves between devices by JAX's collectives and lax.ppermute only.
A program may use at most 128 MiB of HBM per device.

```python
import math
import jax
import jax.numpy as jnp
from jax import lax

D = 1536
HEADS = 12
HDIM = 64
INNER = 768
P_SIZE = 512
STRIP = 128
NSTRIP = 4
MEM = 32
POOL = 16
NOFF = 4
SMAX = 2
RMAX = 4
FRAMES = 32
CAMS = 4


def shared_base(key):
    raw_normal = jax.random.normal(jax.random.fold_in(key, 7), (D, HEADS * HDIM), jnp.float32)
    return jnp.clip(raw_normal, -5.0, 5.0) / math.sqrt(D)


def draw_w_key(key, part):
    return shared_base(key).astype(jnp.bfloat16)


def draw_w_query(key, part):
    fresh_part = jax.random.normal(jax.random.fold_in(key, 11), (D, HEADS * HDIM), jnp.float32)
    fresh_part = jnp.clip(fresh_part, -5.0, 5.0) / math.sqrt(D)
    return fresh_part.astype(jnp.bfloat16)


def draw_tokens(key, part):
    full_shape = (CAMS, FRAMES, P_SIZE, D)
    raw_normal = jax.random.normal(jax.random.fold_in(key, 3), full_shape, jnp.float32)
    return jnp.clip(raw_normal, -6.0, 6.0).astype(jnp.bfloat16)


def draw_memory_offsets(key, part):
    frame_ids = jnp.arange(FRAMES, dtype=jnp.int32)[:, None]
    reach_max = jnp.maximum(frame_ids, 1)
    raw_draw = jax.random.randint(jax.random.fold_in(key, 13), (FRAMES, NOFF), 0, 1 << 20, dtype=jnp.int32)
    offsets = 1 + raw_draw % reach_max
    return offsets.at[FRAMES - 1, 0].set(FRAMES - 1).astype(jnp.int32)


def draw_strip_count(key, part):
    senders = jnp.arange(CAMS, dtype=jnp.int32)
    raw_draw = jax.random.randint(jax.random.fold_in(key, 17), (CAMS, CAMS), 1, SMAX + 1, dtype=jnp.int32)
    off_diagonal = 1 - jnp.eye(CAMS, dtype=jnp.int32)
    wanted = raw_draw * off_diagonal
    capped = jnp.minimum(jnp.cumsum(wanted, axis=0, dtype=jnp.int32), RMAX)
    counts = capped - jnp.concatenate([jnp.zeros((1, CAMS), jnp.int32), capped[:-1]], axis=0)
    busiest = jax.random.randint(jax.random.fold_in(key, 23), (), 0, CAMS, dtype=jnp.int32)
    order_pos = (senders - busiest - 1) % CAMS
    forced = jnp.minimum(SMAX, jnp.maximum(0, RMAX - order_pos * SMAX))
    forced = jnp.where(senders == busiest, 0, forced)
    return jnp.where(senders[None, :] == busiest, forced[:, None], counts).astype(jnp.int32)


def draw_strip_index(key, part):
    raw_draw = jax.random.randint(jax.random.fold_in(key, 29), (CAMS, CAMS, NSTRIP), 0, 1 << 20, dtype=jnp.int32)
    scores_int = raw_draw * NSTRIP + jnp.arange(NSTRIP, dtype=jnp.int32)
    picked = jnp.argsort(scores_int, axis=-1, stable=True)[..., :SMAX].astype(jnp.int32)
    slot_ids = jnp.arange(SMAX, dtype=jnp.int32)
    picked = picked.at[0, 1].set(NSTRIP - 1 - slot_ids)
    picked = picked.at[1, 0].set(slot_ids)
    return picked.astype(jnp.int32)


def steps_of(rng, shape, cuts, least, high):
    def one(axis_at, blocks):
        steps = jax.random.uniform(jax.random.fold_in(jax.random.fold_in(rng, 6), axis_at), (blocks,), jnp.float32, least / len(cuts), high / len(cuts))
        return jnp.repeat(jnp.exp(steps), shape[axis_at] // blocks).reshape((-1,) + (1,) * (len(shape) - axis_at - 1))

    gain = one(*cuts[0])
    for cut in cuts[1:]:
        gain = gain * one(*cut)
    return gain


def noise(stream_key, shape, width, most, shards=(), held_as=jnp.bfloat16):
    drawn = width * jax.random.normal(stream_key, shape, jnp.float32)
    if shards:
        drawn = drawn * steps_of(stream_key, shape, shards, -0.22, 0.18)
    return jnp.clip(drawn, -most, most).astype(held_as)


def setup_inputs(seed: int = 0) -> dict:
    keys = jax.random.split(jax.random.key(seed), 10)
    tokens = draw_tokens(jax.random.fold_in(keys[9], 71), 0)
    w_query = draw_w_query(jax.random.fold_in(keys[9], 71), 0)
    w_key = draw_w_key(jax.random.fold_in(keys[9], 71), 0)
    w_value = noise(keys[3], (D, INNER), D ** -0.5, 0.15625)
    w_out = noise(keys[4], (INNER, D), (max(INNER // 64, 1)) ** -0.5, 1.75)
    grad_update = noise(keys[5], (CAMS, FRAMES, P_SIZE, D), 1.0, 6.0, ((0, 4), (1, 32)))
    memory_offsets = draw_memory_offsets(jax.random.fold_in(keys[9], 71), 0)
    strip_count = draw_strip_count(jax.random.fold_in(keys[9], 71), 0)
    strip_index = draw_strip_index(jax.random.fold_in(keys[9], 71), 0)
    return {"tokens": tokens, "w_query": w_query, "w_key": w_key, "w_value": w_value, "w_out": w_out, "grad_update": grad_update, "memory_offsets": memory_offsets, "strip_count": strip_count, "strip_index": strip_index}


EPS = 1e-05

def normalize(values_in):
    widened = values_in.astype(jnp.float32)
    average = lax.optimization_barrier(jnp.mean(widened, axis=-1, keepdims=True))
    centred = widened - average
    spread = lax.optimization_barrier(jnp.mean(centred * centred, axis=-1, keepdims=True))
    inverse = lax.rsqrt(spread + EPS)
    return (centred * inverse, inverse)

def norm_backward(grad_normed, normed, inverse):
    first_mean = lax.optimization_barrier(jnp.mean(grad_normed, axis=-1, keepdims=True))
    second_mean = lax.optimization_barrier(jnp.mean(grad_normed * normed, axis=-1, keepdims=True))
    return inverse * (grad_normed - first_mean - normed * second_mean)

def head_pass(queries, key_rows, value_rows, key_live, grad_mixed):
    row_count = queries.shape[0]
    key_count = key_rows.shape[0]
    score_scale = 1.0 / math.sqrt(HDIM)
    query_four = queries.astype(jnp.float32).reshape(row_count, HEADS, HDIM)
    key_four = key_rows.astype(jnp.float32).reshape(key_count, HEADS, HDIM)
    value_four = value_rows.astype(jnp.float32).reshape(key_count, HEADS, HDIM)
    grad_four = grad_mixed.astype(jnp.float32).reshape(row_count, HEADS, HDIM)
    scores = jnp.einsum('qhd,khd->hqk', query_four, key_four) * score_scale
    scores = jnp.where(key_live[None, None, :], scores, -jnp.inf)
    highest = lax.optimization_barrier(jnp.max(scores, axis=-1, keepdims=True))
    shifted_exp = jnp.exp(scores - highest)
    weights = shifted_exp / lax.optimization_barrier(jnp.sum(shifted_exp, axis=-1, keepdims=True))
    weights_low = lax.optimization_barrier(weights.astype(jnp.bfloat16)).astype(jnp.float32)
    mixed_rows = jnp.einsum('hqk,khd->qhd', weights_low, value_four)
    mixed_rows = mixed_rows.reshape(row_count, HEADS * HDIM).astype(jnp.bfloat16)
    grad_weights = jnp.einsum('qhd,khd->hqk', grad_four, value_four)
    inner_sum = lax.optimization_barrier(jnp.sum(weights * grad_weights, axis=-1, keepdims=True))
    grad_scores = (weights * (grad_weights - inner_sum) * score_scale).astype(jnp.bfloat16)
    grad_scores = lax.optimization_barrier(grad_scores).astype(jnp.float32)
    grad_query = jnp.einsum('hqk,khd->qhd', grad_scores, key_four)
    grad_query = grad_query.reshape(row_count, HEADS * HDIM).astype(jnp.bfloat16)
    grad_key = jnp.einsum('hqk,qhd->khd', grad_scores, query_four).reshape(key_count, HEADS * HDIM)
    grad_value = jnp.einsum('hqk,qhd->khd', weights_low, grad_four).reshape(key_count, HEADS * HDIM)
    return (mixed_rows, grad_query, grad_key, grad_value)

def gather_back(own_grads, memory_grads, far_grads, source_safe, source_live, strip_count, strip_index):
    own_grid = own_grads.reshape(CAMS, FRAMES, MEM, POOL, INNER)
    memory_grid = memory_grads.reshape(CAMS, FRAMES, NOFF, MEM, INNER)
    memory_grid = memory_grid * source_live[None, :, :, None, None].astype(jnp.float32)
    kept_add = jnp.zeros((CAMS, FRAMES, MEM, INNER), jnp.float32).at[:, source_safe].add(memory_grid)
    own_grid = own_grid.at[:, :, :, 0].add(kept_add)
    far_grid = far_grads.reshape(CAMS, FRAMES, CAMS, SMAX, STRIP, INNER).astype(jnp.float32)
    slot_ids = jnp.arange(SMAX, dtype=jnp.int32)
    far_live = slot_ids[None, None, :] < jnp.transpose(strip_count)[:, :, None]
    far_grid = far_grid * far_live[:, None, :, :, None, None].astype(jnp.float32)
    sender_ids = jnp.arange(CAMS, dtype=jnp.int32)[None, None, :, None]
    frame_ids = jnp.arange(FRAMES, dtype=jnp.int32)[None, :, None, None]
    strip_ids = jnp.transpose(strip_index, (1, 0, 2))[:, None, :, :]
    strip_grid = own_grid.reshape(CAMS, FRAMES, NSTRIP, STRIP, INNER)
    strip_grid = strip_grid.at[sender_ids, frame_ids, strip_ids].add(far_grid)
    return strip_grid.reshape(CAMS, FRAMES, P_SIZE, INNER).astype(jnp.bfloat16)

def reference(tokens, w_query, w_key, w_value, w_out, grad_update, memory_offsets, strip_count, strip_index):
    all_rows = CAMS * FRAMES * P_SIZE
    normed, inverse = normalize(tokens.reshape(all_rows, D))
    normed_low = normed.astype(jnp.bfloat16)

    def project(weight):
        result = jnp.dot(normed_low, weight, preferred_element_type=jnp.float32)
        return result.astype(jnp.bfloat16).reshape(CAMS, FRAMES, P_SIZE, INNER)
    queries = project(w_query)
    keys_all = project(w_key)
    values_all = project(w_value)
    grad_mixed = jnp.dot(grad_update.reshape(all_rows, D), w_out.T, preferred_element_type=jnp.float32)
    grad_mixed = grad_mixed.astype(jnp.bfloat16).reshape(CAMS, FRAMES, P_SIZE, INNER)
    kept_keys = keys_all[:, :, ::POOL]
    kept_values = values_all[:, :, ::POOL]
    frame_ids = jnp.arange(FRAMES, dtype=jnp.int32)
    sources = frame_ids[:, None] - memory_offsets
    source_live = sources >= 0
    source_safe = jnp.maximum(sources, 0).astype(jnp.int32)
    key_strips = keys_all.reshape(CAMS, FRAMES, NSTRIP, STRIP, INNER)
    value_strips = values_all.reshape(CAMS, FRAMES, NSTRIP, STRIP, INNER)
    senders = jnp.arange(CAMS, dtype=jnp.int32)
    slot_ids = jnp.arange(SMAX, dtype=jnp.int32)

    def per_item(item_id):
        camera = item_id // FRAMES
        frame_at = item_id % FRAMES
        picked_frames = source_safe[frame_at]
        memory_keys = kept_keys[camera][picked_frames].reshape(NOFF * MEM, INNER)
        memory_values = kept_values[camera][picked_frames].reshape(NOFF * MEM, INNER)
        memory_live = jnp.repeat(source_live[frame_at], MEM)
        chosen = strip_index[:, camera, :]
        far_keys = key_strips[senders[:, None], frame_at, chosen].reshape(CAMS * SMAX * STRIP, INNER)
        far_values = value_strips[senders[:, None], frame_at, chosen].reshape(CAMS * SMAX * STRIP, INNER)
        far_live = jnp.repeat((slot_ids[None, :] < strip_count[:, camera][:, None]).reshape(-1), STRIP)
        key_rows = jnp.concatenate([keys_all[camera, frame_at], memory_keys, far_keys], axis=0)
        value_rows = jnp.concatenate([values_all[camera, frame_at], memory_values, far_values], axis=0)
        key_live = jnp.concatenate([jnp.ones((P_SIZE,), dtype=bool), memory_live, far_live], axis=0)
        mixed_rows, grad_query, grad_key, grad_value = head_pass(queries[camera, frame_at], key_rows, value_rows, key_live, grad_mixed[camera, frame_at])
        update_rows = jnp.dot(mixed_rows, w_out, preferred_element_type=jnp.float32).astype(jnp.bfloat16)
        split_at = P_SIZE + NOFF * MEM
        return (update_rows, grad_query, grad_key[:P_SIZE], grad_value[:P_SIZE], grad_key[P_SIZE:split_at], grad_value[P_SIZE:split_at], grad_key[split_at:].astype(jnp.bfloat16), grad_value[split_at:].astype(jnp.bfloat16))
    results = lax.map(per_item, jnp.arange(CAMS * FRAMES, dtype=jnp.int32))
    update = results[0].reshape(CAMS, FRAMES, P_SIZE, D)
    grad_query = results[1].reshape(all_rows, INNER)
    total_keys = gather_back(results[2], results[4], results[6], source_safe, source_live, strip_count, strip_index)
    total_values = gather_back(results[3], results[5], results[7], source_safe, source_live, strip_count, strip_index)
    grad_normed = jnp.dot(grad_query, w_query.T, preferred_element_type=jnp.float32)
    grad_normed = grad_normed + jnp.dot(total_keys.reshape(all_rows, INNER), w_key.T, preferred_element_type=jnp.float32)
    grad_normed = grad_normed + jnp.dot(total_values.reshape(all_rows, INNER), w_value.T, preferred_element_type=jnp.float32)
    grad_tokens = norm_backward(grad_normed, normed, inverse).astype(jnp.bfloat16).reshape(CAMS, FRAMES, P_SIZE, D)
    return (update, grad_tokens)
```

```python
import functools

import jax
import jax.numpy as jnp
from jax import lax
from jax.experimental import pallas as pl
from jax.experimental.pallas import tpu as pltpu
from jax.sharding import PartitionSpec as P


LOW = jnp.bfloat16
WIDE = jnp.float32
ROWS = 512
MODEL = 1536
INNER = 768
STRIP = 128
MEM = 32
READS = 4
SLOTS = 6
LIVE_MAX = 4
MEM_AT = ROWS
FAR_AT = ROWS + READS * MEM
KEYS = FAR_AT + LIVE_MAX * STRIP
PAIR = 128
CHUNK = 128
EPS = 1e-05
MASKED = -1e30
NT = (((1,), (1,)), ((), ()))
GROUPS = ((0, 3), (3, 3))


def dot(left, right):
    return jnp.dot(left, right, preferred_element_type=WIDE)


def dot_t(left, right):
    return lax.dot_general(left, right, NT, preferred_element_type=WIDE)


def whole(shape):
    return pl.BlockSpec(shape, lambda *_: (0,) * len(shape))


def call(kernel, name, grid, scalars, in_specs, out_specs, out_shape, scratch, flops, moved):
    return pl.pallas_call(
        kernel,
        grid_spec=pltpu.PrefetchScalarGridSpec(
            num_scalar_prefetch=scalars,
            grid=(grid,),
            in_specs=in_specs,
            out_specs=out_specs,
            scratch_shapes=scratch,
        ),
        out_shape=out_shape,
        compiler_params=pltpu.CompilerParams(
            dimension_semantics=("arbitrary",), vmem_limit_bytes=60 << 20
        ),
        cost_estimate=pl.CostEstimate(flops=flops, bytes_accessed=moved, transcendentals=0),
        name=name,
    )


def array(shape, dtype):
    return jax.ShapeDtypeStruct(shape, dtype)


def normalize(rows):
    widened = rows.astype(WIDE)
    average = jnp.mean(widened, axis=-1, keepdims=True)
    centred = widened - average
    spread = jnp.mean(centred * centred, axis=-1, keepdims=True)
    inverse = lax.rsqrt(spread + EPS)
    return centred * inverse, inverse


def project_keys_kernel(ids, index, tokens, w_key, w_value, low, keys, values, *rest):
    sends, normed_low = rest[:3], rest[3]
    camera = ids[0]

    @pl.when(pl.program_id(0) == 0)
    def _():
        for start in range(0, ROWS, STRIP):
            at = slice(start, start + STRIP)
            normed_low[at, :] = normalize(tokens[at, :])[0].astype(LOW)
        low[...] = normed_low[...]

    keys[...] = dot(normed_low[...], w_key[...]).astype(LOW)
    values[...] = dot(normed_low[...], w_value[...]).astype(LOW)
    for shift in (1, 2, 3):
        for slot in range(2):
            strip = index[camera, lax.rem(camera + shift, 4), slot]
            at = pl.ds(pl.multiple_of(strip * STRIP, STRIP), STRIP)
            sends[shift - 1][0, slot] = keys[at, :]
            sends[shift - 1][1, slot] = values[at, :]


def project_keys(ids, index, tokens, w_key, w_value):
    width = 256
    weight = pl.BlockSpec((MODEL, width), lambda j, *_: (0, j))
    out = pl.BlockSpec((ROWS, width), lambda j, *_: (0, j))
    send = pl.BlockSpec((2, 2, STRIP, width), lambda j, *_: (0, 0, 0, j))
    return call(
        project_keys_kernel,
        "project_keys",
        INNER // width,
        2,
        [whole((ROWS, MODEL)), weight, weight],
        [whole((ROWS, MODEL)), out, out, send, send, send],
        [array((ROWS, MODEL), LOW), array((ROWS, INNER), LOW), array((ROWS, INNER), LOW)]
        + [array((2, 2, STRIP, INNER), LOW)] * 3,
        [pltpu.VMEM((ROWS, MODEL), LOW)],
        4 * ROWS * MODEL * INNER,
        12 << 20,
    )(ids, index, tokens, w_key, w_value)


def project_queries_kernel(low, grad_update, w_query, w_out, queries, grad_mixed):
    product = dot(low[...], w_query[...]).astype(LOW)
    queries[...] = product * jnp.asarray(0.125, LOW)
    grad_mixed[...] = dot_t(grad_update[...], w_out[...]).astype(LOW)


def project_queries(low, grad_update, w_query, w_out):
    width = 256
    out = pl.BlockSpec((ROWS, width), lambda j: (0, j))
    return call(
        project_queries_kernel,
        "project_queries",
        INNER // width,
        0,
        [
            whole((ROWS, MODEL)),
            whole((ROWS, MODEL)),
            pl.BlockSpec((MODEL, width), lambda j: (0, j)),
            pl.BlockSpec((width, MODEL), lambda j: (j, 0)),
        ],
        [out, out],
        [array((ROWS, INNER), LOW)] * 2,
        [],
        4 * ROWS * MODEL * INNER,
        10 << 20,
    )(low, grad_update, w_query, w_out)


def parts_of(frame):
    return frame // 8, lax.rem(frame // 2, 4), lax.rem(frame, 2)


def source_of(offsets, frame, read):
    source = frame - offsets[frame, read]
    return jnp.maximum(source, 0), source >= 0


def pick_kernel(ids, offsets, held_0, held_1, held_2, held_3, picked):
    frame = ids[1]
    z_here, x_here, core_here = parts_of(frame)
    partner = frame + 1 - 2 * core_here
    held = (held_0, held_1, held_2, held_3)
    for read in range(READS):
        source, live = source_of(offsets, partner, read)
        z_at, x_at, core_at = parts_of(source)
        back_z, back_x = lax.rem(z_here - z_at + 4, 4), lax.rem(x_here - x_at + 4, 4)
        wanted = jnp.logical_and(live, core_at == core_here)
        for shift in range(4):

            @pl.when(jnp.logical_and(wanted, back_x == shift))
            def _():
                picked[read] = held[shift][back_z]

        @pl.when(jnp.logical_not(wanted))
        def _():
            picked[read] = jnp.zeros((MEM, MODEL), LOW)


def pick(ids, offsets, held):
    return call(
        pick_kernel,
        "pick",
        1,
        2,
        [whole((4, MEM, MODEL))] * 4,
        whole((READS, MEM, MODEL)),
        array((READS, MEM, MODEL), LOW),
        [],
        0,
        2 << 20,
    )(ids, offsets, *held)


def project_memory_kernel(ids, offsets, held_0, held_1, held_2, held_3, given, w_key, w_value, keys, values, rows, low):
    frame = ids[1]
    z_here, x_here, core_here = parts_of(frame)
    held = (held_0, held_1, held_2, held_3)

    @pl.when(pl.program_id(0) == 0)
    def _():
        for read in range(READS):
            source, live = source_of(offsets, frame, read)
            z_at, x_at, core_at = parts_of(source)
            back_z, back_x = lax.rem(z_here - z_at + 4, 4), lax.rem(x_here - x_at + 4, 4)
            mine = jnp.logical_and(live, core_at == core_here)
            at = slice(read * MEM, (read + 1) * MEM)
            for shift in range(4):

                @pl.when(jnp.logical_and(mine, back_x == shift))
                def _():
                    rows[at, :] = held[shift][back_z]

            @pl.when(jnp.logical_not(mine))
            def _():
                rows[at, :] = given[read]

        low[...] = normalize(rows[...])[0].astype(LOW)

    keys[...] = dot(low[...], w_key[...]).astype(LOW)
    values[...] = dot(low[...], w_value[...]).astype(LOW)


def project_memory(ids, offsets, held, given, w_key, w_value):
    width = 256
    weight = pl.BlockSpec((MODEL, width), lambda j, *_: (0, j))
    out = pl.BlockSpec((READS * MEM, width), lambda j, *_: (0, j))
    return call(
        project_memory_kernel,
        "project_memory",
        INNER // width,
        2,
        [whole((4, MEM, MODEL))] * 4 + [whole((READS, MEM, MODEL)), weight, weight],
        [out, out],
        [array((READS * MEM, INNER), LOW)] * 2,
        [pltpu.VMEM((READS * MEM, MODEL), LOW)] * 2,
        4 * READS * MEM * MODEL * INNER,
        7 << 20,
    )(ids, offsets, *held, given, w_key, w_value)


def shift_z(by):
    return [(f, (f + 8 * by) % 32) for f in range(32)]


def shift_x(by):
    return [(f, f // 8 * 8 + (f % 8 + 2 * by) % 8) for f in range(32)]


SWAP_CORE = [(f, f ^ 1) for f in range(32)]


def shift_cam(by):
    return [(s, (s + by) % 4) for s in range(4)]


def attention_kernel(ids, offsets, count, queries, grads, keys_own, values_own, keys_mem, values_mem, *rest):
    far_in, rest = rest[:3], rest[3:]
    mixed, grad_query, grad_keys, grad_values, grad_mem, grad_mem_low = rest[:6]
    far_out, rest = rest[6:9], rest[9:]
    keys, values, keys_t, values_t, scores, grad_w, weights, grad_s, two_q, two_g, rest_k, rest_v = rest
    camera, frame = ids[0], ids[1]

    slot_live, slot_at, live_total = [], [], 0
    for slot in range(SLOTS):
        sender = lax.rem(camera + 4 - (slot // 2 + 1), 4)
        live = count[sender, camera] > slot % 2
        slot_live.append(jnp.logical_and(live, live_total < LIVE_MAX))
        slot_at.append(jnp.minimum(live_total, LIVE_MAX - 1))
        live_total = live_total + live.astype(jnp.int32)

    keys[0:ROWS, :] = keys_own[...]
    values[0:ROWS, :] = values_own[...]
    keys[MEM_AT:FAR_AT, :] = keys_mem[...]
    values[MEM_AT:FAR_AT, :] = values_mem[...]
    for place in range(LIVE_MAX):

        @pl.when(live_total <= place)
        def _():
            at = slice(FAR_AT + place * STRIP, FAR_AT + (place + 1) * STRIP)
            keys[at, :] = jnp.zeros((STRIP, PAIR), LOW)
            values[at, :] = jnp.zeros((STRIP, PAIR), LOW)

    for slot in range(SLOTS):

        @pl.when(slot_live[slot])
        def _():
            at = pl.ds(pl.multiple_of(FAR_AT + slot_at[slot] * STRIP, STRIP), STRIP)
            keys[at, :] = far_in[slot // 2][0, slot % 2]
            values[at, :] = far_in[slot // 2][1, slot % 2]

    keys_t[...] = keys[...].T
    values_t[...] = values[...].T
    lane = lax.broadcasted_iota(jnp.int32, (ROWS, PAIR), 1)
    for head in range(2):
        keep = (lane >= 64) if head else (lane < 64)
        at = slice(head * ROWS, (head + 1) * ROWS)
        two_q[at, :] = jnp.where(keep, queries[...], jnp.zeros((ROWS, PAIR), LOW))
        two_g[at, :] = jnp.where(keep, grads[...], jnp.zeros((ROWS, PAIR), LOW))

    def masked(block, base):
        if base < ROWS:
            return block
        if base < FAR_AT:
            pieces = []
            for read in range(READS):
                live = offsets[frame, read] <= frame
                pieces.append(jnp.where(live, block[read * MEM : (read + 1) * MEM], MASKED))
            return jnp.concatenate(pieces, axis=0)
        return jnp.where((base - FAR_AT) // STRIP < live_total, block, MASKED)

    def folded(block):
        return block.reshape(CHUNK // 8, 8, ROWS)

    for head in range(2):
        cols = slice(head * ROWS, (head + 1) * ROWS)
        highest = jnp.full((8, ROWS), MASKED, WIDE)
        for base in range(0, KEYS, CHUNK):
            at = slice(base, base + CHUNK)
            block = masked(dot_t(keys[at, :], two_q[cols, :]), base)
            scores[head, at, :] = block
            highest = jnp.maximum(highest, jnp.max(folded(block), axis=0))
        highest = jnp.max(highest, axis=0, keepdims=True)
        total = jnp.zeros((8, ROWS), WIDE)
        inner = jnp.zeros((8, ROWS), WIDE)
        for base in range(0, KEYS, CHUNK):
            at = slice(base, base + CHUNK)
            block = dot_t(values[at, :], two_g[cols, :])
            lifted = jnp.exp(scores[head, at, :] - highest)
            scores[head, at, :] = lifted
            grad_w[head, at, :] = block
            total = total + jnp.sum(folded(lifted), axis=0)
            inner = inner + jnp.sum(folded(lifted * block), axis=0)
        share = 1.0 / jnp.sum(total, axis=0, keepdims=True)
        inner = jnp.sum(inner, axis=0, keepdims=True) * share
        for base in range(0, KEYS, CHUNK):
            at = slice(base, base + CHUNK)
            part = scores[head, at, :] * share
            weights[at, cols] = part.astype(LOW)
            grad_s[at, cols] = (part * (grad_w[head, at, :] - inner)).astype(LOW)

    mixed_t, grad_query_t = [], []
    for head in range(2):
        cols = slice(head * ROWS, (head + 1) * ROWS)
        dims = slice(head * 64, (head + 1) * 64)
        mixed_t.append(dot(values_t[dims, :], weights[:, cols]))
        grad_query_t.append(dot(keys_t[dims, :], grad_s[:, cols]))
    mixed[...] = jnp.concatenate(mixed_t, axis=0).T.astype(LOW)
    grad_query[...] = (jnp.concatenate(grad_query_t, axis=0).T * 0.125).astype(LOW)

    for base in range(0, KEYS, CHUNK):
        at = slice(base, base + CHUNK)
        for_value = dot(weights[at, :], two_g[...])
        for_key = dot(grad_s[at, :], two_q[...])
        if base < ROWS:
            grad_keys[at, :] = for_key
            grad_values[at, :] = for_value
        else:
            rest_k[base - ROWS : base - ROWS + CHUNK, :] = for_key
            rest_v[base - ROWS : base - ROWS + CHUNK, :] = for_value
    grad_mem[0] = rest_k[0 : READS * MEM, :]
    grad_mem[1] = rest_v[0 : READS * MEM, :]
    grad_mem_low[0] = rest_k[0 : READS * MEM, :].astype(LOW)
    grad_mem_low[1] = rest_v[0 : READS * MEM, :].astype(LOW)
    for slot in range(SLOTS):

        @pl.when(slot_live[slot])
        def _():
            start = FAR_AT - ROWS + slot_at[slot] * STRIP
            at = pl.ds(pl.multiple_of(start, STRIP), STRIP)
            far_out[slot // 2][0, slot % 2] = rest_k[at, :].astype(LOW)
            far_out[slot // 2][1, slot % 2] = rest_v[at, :].astype(LOW)


def attention(group, ids, offsets, count, queries, grads, keys_own, values_own, keys_mem, values_mem, far):
    first, pairs = group
    width = pairs * PAIR

    def taken(rows):
        return pl.BlockSpec((rows, PAIR), lambda p, *_: (0, first + p))

    def made(rows):
        return pl.BlockSpec((rows, PAIR), lambda p, *_: (0, p))

    far_in = pl.BlockSpec((2, 2, STRIP, PAIR), lambda p, *_: (0, 0, 0, first + p))
    far_out = pl.BlockSpec((2, 2, STRIP, PAIR), lambda p, *_: (0, 0, 0, p))
    mem_out = pl.BlockSpec((2, READS * MEM, PAIR), lambda p, *_: (0, 0, p))
    return call(
        attention_kernel,
        "attention",
        pairs,
        3,
        [taken(ROWS)] * 4 + [taken(READS * MEM)] * 2 + [far_in] * 3,
        [made(ROWS)] * 4 + [mem_out] * 2 + [far_out] * 3,
        [array((ROWS, width), LOW)] * 2
        + [array((ROWS, width), WIDE)] * 2
        + [array((2, READS * MEM, width), WIDE), array((2, READS * MEM, width), LOW)]
        + [array((2, 2, STRIP, width), LOW)] * 3,
        [pltpu.VMEM((KEYS, PAIR), LOW)] * 2
        + [pltpu.VMEM((PAIR, KEYS), LOW)] * 2
        + [pltpu.VMEM((2, KEYS, ROWS), WIDE)] * 2
        + [pltpu.VMEM((KEYS, 2 * ROWS), LOW)] * 2
        + [pltpu.VMEM((2 * ROWS, PAIR), LOW)] * 2
        + [pltpu.VMEM((KEYS - ROWS, PAIR), WIDE)] * 2,
        pairs * 12 * KEYS * 2 * ROWS * 256,
        pairs * (3 << 20),
    )(ids, offsets, count, queries, grads, keys_own, values_own, keys_mem, values_mem, *far)


def sort_kernel(ids, offsets, *rest):
    count = len(GROUPS)
    own, given = rest[:count], rest[count : 2 * count]
    outs, total = rest[2 * count : 2 * count + 4], rest[2 * count + 4]
    frame = ids[1]
    z_here, x_here, core_here = parts_of(frame)
    partner = frame + 1 - 2 * core_here
    total[...] = jnp.zeros_like(total)
    for reader, arrays in ((frame, own), (partner, given)):
        for read in range(READS):
            source, live = source_of(offsets, reader, read)
            z_at, x_at, core_at = parts_of(source)
            to = lax.rem(x_at - x_here + 4, 4) * 4 + lax.rem(z_at - z_here + 4, 4)

            @pl.when(jnp.logical_and(live, core_at == core_here))
            def _():
                for (first, pairs), part in zip(GROUPS, arrays):
                    cols = slice(first * PAIR, (first + pairs) * PAIR)
                    for kind in range(2):
                        added = part[kind, read * MEM : (read + 1) * MEM, :].astype(WIDE)
                        total[to, kind, :, cols] = total[to, kind, :, cols] + added

    for shift in range(4):
        outs[shift][...] = total[4 * shift : 4 * shift + 4].astype(LOW)


def sort_reads(ids, offsets, own, given):
    shapes = [(2, READS * MEM, pairs * PAIR) for _, pairs in GROUPS]
    return call(
        sort_kernel,
        "sort_reads",
        1,
        2,
        [whole(s) for s in shapes] * 2,
        [whole((4, 2, MEM, INNER))] * 4,
        [array((4, 2, MEM, INNER), LOW)] * 4,
        [pltpu.VMEM((16, 2, MEM, INNER), WIDE)],
        0,
        3 << 20,
    )(ids, offsets, *own, *given)


def add_kernel(part_0, part_1, part_2, part_3, *outs):
    for shift in range(4):
        total = part_0[shift].astype(WIDE) + part_1[shift].astype(WIDE)
        total = total + part_2[shift].astype(WIDE) + part_3[shift].astype(WIDE)
        outs[shift][...] = total.astype(LOW)


def add_reads(parts):
    return call(
        add_kernel,
        "add_reads",
        1,
        0,
        [whole((4, 2, MEM, INNER))] * 4,
        [whole((2, MEM, INNER))] * 4,
        [array((2, MEM, INNER), LOW)] * 4,
        [],
        0,
        2 << 20,
    )(*parts)


def outward_kernel(*refs):
    count = len(GROUPS)
    mixed, grad_query = refs[:count], refs[count : 2 * count]
    w_out, w_query, update, grad_normed = refs[2 * count :]
    total, part = 0.0, 0.0
    for (first, pairs), mixed_ref, grad_ref in zip(GROUPS, mixed, grad_query):
        cols = slice(first * PAIR, (first + pairs) * PAIR)
        total = total + dot(mixed_ref[...], w_out[cols, :])
        part = part + dot_t(grad_ref[...], w_query[:, cols])
    update[...] = total.astype(LOW)
    grad_normed[...] = part


def outward(mixed, grad_query, w_out, w_query):
    width = 256
    out = pl.BlockSpec((ROWS, width), lambda j: (0, j))
    parts = [whole((ROWS, pairs * PAIR)) for _, pairs in GROUPS]
    return call(
        outward_kernel,
        "outward",
        MODEL // width,
        0,
        parts
        + parts
        + [
            pl.BlockSpec((INNER, width), lambda j: (0, j)),
            pl.BlockSpec((width, INNER), lambda j: (j, 0)),
        ],
        [out, out],
        [array((ROWS, MODEL), LOW), array((ROWS, MODEL), WIDE)],
        [],
        4 * ROWS * MODEL * INNER,
        11 << 20,
    )(*mixed, *grad_query, w_out, w_query)


def token_grads_kernel(ids, count, index, *refs):
    groups = len(GROUPS)
    own_keys, own_values = refs[:groups], refs[groups : 2 * groups]
    back = refs[2 * groups : 5 * groups]
    kept = refs[5 * groups : 5 * groups + 4]
    tokens, grad_part, w_key, w_value, grad_tokens = refs[5 * groups + 4 : 5 * groups + 9]
    total_keys, total_values, grad_normed, wide = refs[5 * groups + 9 :]
    camera = ids[0]
    step = pl.program_id(0)

    @pl.when(step == 0)
    def _():
        row = lax.broadcasted_iota(jnp.int32, (ROWS, 4 * MEM), 0)
        col = lax.broadcasted_iota(jnp.int32, (ROWS, 4 * MEM), 1)
        hit = row == (col % MEM) * (ROWS // MEM)
        spread = jnp.where(hit, 1.0, 0.0).astype(LOW)
        for kind, (own, total) in enumerate(((own_keys, total_keys), (own_values, total_values))):
            stacked = jnp.concatenate([part[kind] for part in kept], axis=0)
            wide[...] = dot(spread, stacked)
            for (first, pairs), part in zip(GROUPS, own):
                cols = slice(first * PAIR, (first + pairs) * PAIR)
                wide[:, cols] = wide[:, cols] + part[...]
            for shift in (1, 2, 3):
                other = lax.rem(camera + shift, 4)
                for slot in range(2):

                    @pl.when(slot < count[camera, other])
                    def _():
                        start = index[camera, other, slot] * STRIP
                        at = pl.ds(pl.multiple_of(start, STRIP), STRIP)
                        for group, (first, pairs) in enumerate(GROUPS):
                            cols = slice(first * PAIR, (first + pairs) * PAIR)
                            given = back[3 * group + shift - 1][kind, slot]
                            wide[at, cols] = wide[at, cols] + given.astype(WIDE)

            total[...] = wide[...].astype(LOW)

    width = w_key.shape[0]
    cols = pl.ds(pl.multiple_of(step * width, width), width)
    grad_normed[:, cols] = (
        grad_part[...]
        + dot_t(total_keys[...], w_key[...])
        + dot_t(total_values[...], w_value[...])
    )

    @pl.when(step == pl.num_programs(0) - 1)
    def _():
        for start in range(0, ROWS, 64):
            at = slice(start, start + 64)
            normed, inverse = normalize(tokens[at, :])
            grad = grad_normed[at, :]
            first_mean = jnp.mean(grad, axis=-1, keepdims=True)
            second_mean = jnp.mean(grad * normed, axis=-1, keepdims=True)
            grad_tokens[at, :] = (inverse * (grad - first_mean - normed * second_mean)).astype(LOW)


def token_grads(ids, count, index, own_keys, own_values, back, kept, tokens, grad_part, w_key, w_value):
    width = 256
    weight = pl.BlockSpec((width, INNER), lambda j, *_: (j, 0))
    parts = [whole((ROWS, pairs * PAIR)) for _, pairs in GROUPS]
    far = [whole((2, 2, STRIP, pairs * PAIR)) for _, pairs in GROUPS for _ in range(3)]
    return call(
        token_grads_kernel,
        "token_grads",
        MODEL // width,
        3,
        parts
        + parts
        + far
        + [whole((2, MEM, INNER))] * 4
        + [whole((ROWS, MODEL)), pl.BlockSpec((ROWS, width), lambda j, *_: (0, j)), weight, weight],
        whole((ROWS, MODEL)),
        array((ROWS, MODEL), LOW),
        [pltpu.VMEM((ROWS, INNER), LOW)] * 2
        + [pltpu.VMEM((ROWS, MODEL), WIDE), pltpu.VMEM((ROWS, INNER), WIDE)],
        4 * ROWS * MODEL * INNER,
        16 << 20,
    )(ids, count, index, *own_keys, *own_values, *back, *kept, tokens, grad_part, w_key, w_value)


def local(tokens, w_query, w_key, w_value, w_out, grad_update, offsets, count, index):
    tokens = tokens.reshape(ROWS, MODEL)
    grad_update = grad_update.reshape(ROWS, MODEL)
    ids = jnp.stack([lax.axis_index("cam"), lax.axis_index("tm")]).astype(jnp.int32)

    kept = tokens.reshape(MEM, ROWS // MEM, MODEL)[:, 0]
    along_z = jnp.stack([kept] + [lax.ppermute(kept, "tm", shift_z(k)) for k in (1, 2, 3)])

    low, keys, values, *sends = project_keys(ids, index, tokens, w_key, w_value)
    far = [lax.ppermute(sends[k - 1], "cam", shift_cam(k)) for k in (1, 2, 3)]

    held = [along_z] + [lax.ppermute(along_z, "tm", shift_x(k)) for k in (1, 2, 3)]
    queries, grads = project_queries(low, grad_update, w_query, w_out)
    given = lax.ppermute(pick(ids, offsets, held), "tm", SWAP_CORE)
    keys_mem, values_mem = project_memory(ids, offsets, held, given, w_key, w_value)

    mixed, grad_query, own_keys, own_values, mem, mem_given, back = [], [], [], [], [], [], []
    for group in GROUPS:
        made = attention(
            group, ids, offsets, count, queries, grads, keys, values, keys_mem, values_mem, far
        )
        mixed.append(made[0])
        grad_query.append(made[1])
        own_keys.append(made[2])
        own_values.append(made[3])
        mem.append(made[4])
        mem_given.append(lax.ppermute(made[5], "tm", SWAP_CORE))
        back += [lax.ppermute(made[5 + k], "cam", shift_cam(-k)) for k in (1, 2, 3)]

    sorted_x = sort_reads(ids, offsets, mem, mem_given)
    parts = [sorted_x[0]] + [lax.ppermute(sorted_x[k], "tm", shift_x(k)) for k in (1, 2, 3)]
    sorted_z = add_reads(parts)
    kept_grads = [sorted_z[0]] + [lax.ppermute(sorted_z[k], "tm", shift_z(k)) for k in (1, 2, 3)]

    update, grad_part = outward(mixed, grad_query, w_out, w_query)
    grad_tokens = token_grads(
        ids, count, index, own_keys, own_values, back, kept_grads, tokens, grad_part, w_key, w_value
    )
    shape = (1, 1, ROWS, MODEL)
    return update.reshape(shape), grad_tokens.reshape(shape)


def solution(mesh):
    frames = P("cam", "tm", None, None)
    return jax.shard_map(
        local,
        mesh=mesh,
        in_specs=(frames, P(), P(), P(), P(), frames, P(), P(), P()),
        out_specs=(frames, frames),
        check_vma=False,
    )
```

```python
import jax
import jax.numpy as jnp
from jax import lax
from jax.experimental import pallas as pl
from jax.experimental.pallas import tpu as pltpu
from jax.sharding import PartitionSpec as P


LOW = jnp.bfloat16
WIDE = jnp.float32
ROWS = 512
MODEL = 1536
INNER = 768
STRIP = 128
MEM = 32
READS = 4
SLOTS = 6
LIVE_MAX = 4
MEM_AT = ROWS
FAR_AT = ROWS + READS * MEM
KEYS = FAR_AT + LIVE_MAX * STRIP
PAIR = 128
CHUNK = 384
EPS = 1e-05
MASKED = -1e30
NT = (((1,), (1,)), ((), ()))
GROUPS = ((0, 3), (3, 3))


def dot(left, right):
    return jnp.dot(left, right, preferred_element_type=WIDE)


def dot_t(left, right):
    return lax.dot_general(left, right, NT, preferred_element_type=WIDE)


def whole(shape):
    return pl.BlockSpec(shape, lambda *_: (0,) * len(shape))


def call(kernel, grid, scalars, in_specs, out_specs, out_shape, scratch, flops, moved, vmem=24):
    return pl.pallas_call(
        kernel,
        grid_spec=pltpu.PrefetchScalarGridSpec(
            num_scalar_prefetch=scalars,
            grid=(grid,),
            in_specs=in_specs,
            out_specs=out_specs,
            scratch_shapes=scratch,
        ),
        out_shape=out_shape,
        compiler_params=pltpu.CompilerParams(
            dimension_semantics=("arbitrary",), vmem_limit_bytes=vmem << 20
        ),
        cost_estimate=pl.CostEstimate(flops=flops, bytes_accessed=moved, transcendentals=0),
    )


IN_PLACE = pl.BlockSpec(memory_space=pl.ANY)


def array(shape, dtype):
    return jax.ShapeDtypeStruct(shape, dtype)


def normalize(rows):
    widened = rows.astype(WIDE)
    average = jnp.mean(widened, axis=-1, keepdims=True)
    centred = widened - average
    spread = jnp.mean(centred * centred, axis=-1, keepdims=True)
    inverse = lax.rsqrt(spread + EPS)
    return centred * inverse, inverse


def project_keys_kernel(ids, index, tokens, w_key, w_value, low, keys, values, *rest):
    sends, (rows, key_w, value_w, normed_low, made, in_sem, out_sem, send_sem) = rest[:3], rest[3:]
    camera = ids[0]
    loads = []
    for step, start in enumerate(range(0, ROWS, STRIP)):
        at = pl.ds(start, STRIP)
        loads.append(pltpu.make_async_copy(tokens.at[at], rows.at[at], in_sem.at[step]))
    loads.append(pltpu.make_async_copy(w_key, key_w, in_sem.at[4]))
    loads.append(pltpu.make_async_copy(w_value, value_w, in_sem.at[5]))
    for load in loads:
        load.start()
    for step, start in enumerate(range(0, ROWS, STRIP)):
        at = slice(start, start + STRIP)
        loads[step].wait()
        normed_low[at, :] = normalize(rows[at, :])[0].astype(LOW)
    stores = [pltpu.make_async_copy(normed_low, low, out_sem.at[0])]
    stores[0].start()
    for kind, (weight, out) in enumerate(((key_w, keys), (value_w, values))):
        loads[4 + kind].wait()
        for start in range(0, INNER, 256):
            cols = slice(start, start + 256)
            made[kind, :, cols] = dot(normed_low[...], weight[:, cols]).astype(LOW)
        for shift in (1, 2, 3):
            for slot in range(2):
                strip = index[camera, lax.rem(camera + shift, 4), slot]
                at = pl.ds(pl.multiple_of(strip * STRIP, STRIP), STRIP)
                stores.append(
                    pltpu.make_async_copy(
                        made.at[kind, at],
                        sends[shift - 1].at[kind, slot],
                        send_sem.at[kind * SLOTS + 2 * (shift - 1) + slot],
                    )
                )
                stores[-1].start()
        stores.append(pltpu.make_async_copy(made.at[kind], out, out_sem.at[1 + kind]))
        stores[-1].start()
    for store in stores:
        store.wait()


def project_keys(ids, index, tokens, w_key, w_value):
    return call(
        project_keys_kernel,
        1,
        2,
        [IN_PLACE] * 3,
        [IN_PLACE] * 6,
        [array((ROWS, MODEL), LOW), array((ROWS, INNER), LOW), array((ROWS, INNER), LOW)]
        + [array((2, 2, STRIP, INNER), LOW)] * 3,
        [
            pltpu.VMEM((ROWS, MODEL), LOW),
            pltpu.VMEM((MODEL, INNER), LOW),
            pltpu.VMEM((MODEL, INNER), LOW),
            pltpu.VMEM((ROWS, MODEL), LOW),
            pltpu.VMEM((2, ROWS, INNER), LOW),
            pltpu.SemaphoreType.DMA((6,)),
            pltpu.SemaphoreType.DMA((3,)),
            pltpu.SemaphoreType.DMA((2 * SLOTS,)),
        ],
        4 * ROWS * MODEL * INNER,
        12 << 20,
        vmem=16,
    )(ids, index, tokens, w_key, w_value)


def project_queries_kernel(low, grad_update, w_query, w_out, queries, grad_mixed):
    product = dot(low[...], w_query[...]).astype(LOW)
    queries[...] = product * jnp.asarray(0.125, LOW)
    grad_mixed[...] = dot_t(grad_update[...], w_out[...]).astype(LOW)


def project_queries(low, grad_update, w_query, w_out):
    width = 384
    out = pl.BlockSpec((ROWS, width), lambda j: (0, j))
    return call(
        project_queries_kernel,
        INNER // width,
        0,
        [
            whole((ROWS, MODEL)),
            whole((ROWS, MODEL)),
            pl.BlockSpec((MODEL, width), lambda j: (0, j)),
            pl.BlockSpec((width, MODEL), lambda j: (j, 0)),
        ],
        [out, out],
        [array((ROWS, INNER), LOW)] * 2,
        [],
        4 * ROWS * MODEL * INNER,
        10 << 20,
    )(low, grad_update, w_query, w_out)


def parts_of(frame):
    return frame // 8, lax.rem(frame // 2, 4), lax.rem(frame, 2)


def source_of(offsets, frame, read):
    source = frame - offsets[frame, read]
    return jnp.maximum(source, 0), source >= 0


def back_to(frame, source):
    z_here, x_here, core_here = parts_of(frame)
    z_at, x_at, core_at = parts_of(source)
    return lax.rem(z_here - z_at + 4, 4), lax.rem(x_here - x_at + 4, 4), core_at == core_here


def pick_kernel(ids, offsets, held_0, held_1, held_2, held_3, picked, sem):
    frame = ids[1]
    partner = frame + 1 - 2 * lax.rem(frame, 2)
    held = (held_0, held_1, held_2, held_3)
    wanted = []
    for read in range(READS):
        source, live = source_of(offsets, partner, read)
        back_z, back_x, same = back_to(frame, source)
        wanted.append(jnp.logical_and(live, same))
        for shift in range(4):

            @pl.when(jnp.logical_and(wanted[read], back_x == shift))
            def _():
                pltpu.make_async_copy(held[shift].at[back_z], picked.at[read], sem.at[read]).start()

        @pl.when(jnp.logical_not(wanted[read]))
        def _():
            picked[read] = jnp.zeros((MEM, MODEL), LOW)

    for read in range(READS):

        @pl.when(wanted[read])
        def _():
            pltpu.make_async_copy(held_0.at[0], picked.at[read], sem.at[read]).wait()


def pick(ids, offsets, held):
    return call(
        pick_kernel,
        1,
        2,
        [IN_PLACE] * 4,
        whole((READS, MEM, MODEL)),
        array((READS, MEM, MODEL), LOW),
        [pltpu.SemaphoreType.DMA((READS,))],
        0,
        1 << 20,
        vmem=2,
    )(ids, offsets, *held)


def project_memory_kernel(ids, offsets, held_0, held_1, held_2, held_3, given, w_key, w_value, keys, values, *rest):
    rows, low, key_w, value_w, sem, w_sem = rest
    frame = ids[1]
    held = (held_0, held_1, held_2, held_3)
    loads = [
        pltpu.make_async_copy(w_key, key_w, w_sem.at[0]),
        pltpu.make_async_copy(w_value, value_w, w_sem.at[1]),
    ]
    for read in range(READS):
        source, live = source_of(offsets, frame, read)
        back_z, back_x, same = back_to(frame, source)
        mine = jnp.logical_and(live, same)
        for shift in range(4):

            @pl.when(jnp.logical_and(mine, back_x == shift))
            def _():
                pltpu.make_async_copy(held[shift].at[back_z], rows.at[read], sem.at[read]).start()

        @pl.when(jnp.logical_not(mine))
        def _():
            pltpu.make_async_copy(given.at[read], rows.at[read], sem.at[read]).start()

    for load in loads:
        load.start()
    for read in range(READS):
        pltpu.make_async_copy(given.at[read], rows.at[read], sem.at[read]).wait()
        low[read * MEM : (read + 1) * MEM, :] = normalize(rows[read])[0].astype(LOW)
    for load, weight, out in zip(loads, (key_w, value_w), (keys, values)):
        load.wait()
        for start in range(0, INNER, 256):
            cols = slice(start, start + 256)
            out[:, cols] = dot(low[...], weight[:, cols]).astype(LOW)


def project_memory(ids, offsets, held, given, w_key, w_value):
    return call(
        project_memory_kernel,
        1,
        2,
        [IN_PLACE] * 7,
        [whole((READS * MEM, INNER))] * 2,
        [array((READS * MEM, INNER), LOW)] * 2,
        [
            pltpu.VMEM((READS, MEM, MODEL), LOW),
            pltpu.VMEM((READS * MEM, MODEL), LOW),
            pltpu.VMEM((MODEL, INNER), LOW),
            pltpu.VMEM((MODEL, INNER), LOW),
            pltpu.SemaphoreType.DMA((READS,)),
            pltpu.SemaphoreType.DMA((2,)),
        ],
        4 * READS * MEM * MODEL * INNER,
        6 << 20,
        vmem=10,
    )(ids, offsets, *held, given, w_key, w_value)


def shift_z(by):
    return [(f, (f + 8 * by) % 32) for f in range(32)]


def shift_x(by):
    return [(f, f // 8 * 8 + (f % 8 + 2 * by) % 8) for f in range(32)]


SWAP_CORE = [(f, f ^ 1) for f in range(32)]


def shift_cam(by):
    return [(s, (s + by) % 4) for s in range(4)]


def attention_kernel(ids, offsets, count, queries, grads, keys_own, values_own, keys_mem, values_mem, *rest):
    far_in, rest = rest[:3], rest[3:]
    mixed, grad_query, grad_keys, grad_values, grad_mem, grad_mem_low = rest[:6]
    far_out, rest = rest[6:9], rest[9:]
    keys, values, keys_t, values_t, scores, grad_w, weights, grad_s, two_q, two_g, rest_k, rest_v = rest
    camera, frame = ids[0], ids[1]

    slot_live, slot_at, live_total = [], [], 0
    for slot in range(SLOTS):
        sender = lax.rem(camera + 4 - (slot // 2 + 1), 4)
        live = count[sender, camera] > slot % 2
        slot_live.append(jnp.logical_and(live, live_total < LIVE_MAX))
        slot_at.append(jnp.minimum(live_total, LIVE_MAX - 1))
        live_total = live_total + live.astype(jnp.int32)

    keys[0:ROWS, :] = keys_own[...]
    values[0:ROWS, :] = values_own[...]
    keys[MEM_AT:FAR_AT, :] = keys_mem[...]
    values[MEM_AT:FAR_AT, :] = values_mem[...]
    for place in range(LIVE_MAX):

        @pl.when(live_total <= place)
        def _():
            at = slice(FAR_AT + place * STRIP, FAR_AT + (place + 1) * STRIP)
            keys[at, :] = jnp.zeros((STRIP, PAIR), LOW)
            values[at, :] = jnp.zeros((STRIP, PAIR), LOW)

    for slot in range(SLOTS):

        @pl.when(slot_live[slot])
        def _():
            at = pl.ds(pl.multiple_of(FAR_AT + slot_at[slot] * STRIP, STRIP), STRIP)
            keys[at, :] = far_in[slot // 2][0, slot % 2]
            values[at, :] = far_in[slot // 2][1, slot % 2]

    keys_t[...] = keys[...].T
    values_t[...] = values[...].T
    lane = lax.broadcasted_iota(jnp.int32, (ROWS, PAIR), 1)
    for head in range(2):
        keep = (lane >= 64) if head else (lane < 64)
        at = slice(head * ROWS, (head + 1) * ROWS)
        two_q[at, :] = jnp.where(keep, queries[...], jnp.zeros((ROWS, PAIR), LOW))
        two_g[at, :] = jnp.where(keep, grads[...], jnp.zeros((ROWS, PAIR), LOW))

    pieces = [(0, ROWS, None)]
    for read in range(READS):
        start = MEM_AT + read * MEM
        pieces.append((start, start + MEM, offsets[frame, read] <= frame))
    for place in range(LIVE_MAX):
        start = FAR_AT + place * STRIP
        pieces.append((start, start + STRIP, place < live_total))

    def pieces_of(base):
        for start, end, live in pieces:
            low, high = max(start, base), min(end, base + CHUNK)
            if low < high:
                yield low, high, live

    def folded(block):
        return block.reshape(block.shape[0] // 8, 8, ROWS)

    bases = range(0, KEYS, CHUNK)
    highest = [jnp.full((8, ROWS), MASKED, WIDE)] * 2
    total, inner = [jnp.zeros((8, ROWS), WIDE)] * 2, [jnp.zeros((8, ROWS), WIDE)] * 2
    share = [None, None]

    def score(head, base):
        cols = slice(head * ROWS, (head + 1) * ROWS)
        block = dot_t(keys[base : base + CHUNK, :], two_q[cols, :])
        scores[head, base : base + CHUNK, :] = block
        for low, high, live in pieces_of(base):
            top = jnp.max(folded(block[low - base : high - base]), axis=0)
            top = jnp.maximum(highest[head], top)
            highest[head] = top if live is None else jnp.where(live, top, highest[head])
        if base == bases[-1]:
            highest[head] = jnp.max(highest[head], axis=0, keepdims=True)

    def lift(head, base):
        cols = slice(head * ROWS, (head + 1) * ROWS)
        block = dot_t(values[base : base + CHUNK, :], two_g[cols, :])
        grad_w[head, base : base + CHUNK, :] = block
        for low, high, live in pieces_of(base):
            top = highest[head] if live is None else jnp.where(live, highest[head], -MASKED)
            lifted = jnp.exp(scores[head, low:high, :] - top)
            scores[head, low:high, :] = lifted
            total[head] = total[head] + jnp.sum(folded(lifted), axis=0)
            inner[head] = inner[head] + jnp.sum(folded(lifted * block[low - base : high - base]), axis=0)
        if base == bases[-1]:
            share[head] = 1.0 / jnp.sum(total[head], axis=0, keepdims=True)
            inner[head] = jnp.sum(inner[head], axis=0, keepdims=True) * share[head]

    def settle(head, base):
        cols, at = slice(head * ROWS, (head + 1) * ROWS), slice(base, base + CHUNK)
        part = scores[head, at, :] * share[head]
        weights[at, cols] = part.astype(LOW)
        grad_s[at, cols] = (part * (grad_w[head, at, :] - inner[head])).astype(LOW)

    def row_grads(head, base):
        cols, at = slice(head * ROWS, (head + 1) * ROWS), slice(base, base + CHUNK)
        for_value = dot(weights[at, cols], two_g[cols, :])
        for_key = dot(grad_s[at, cols], two_q[cols, :])
        for made, own, far in ((for_key, grad_keys, rest_k), (for_value, grad_values, rest_v)):
            for start, end, ref, shift in ((0, ROWS, own, 0), (ROWS, KEYS, far, ROWS)):
                first, last = max(start, base), min(end, base + CHUNK)
                if first < last:
                    there = slice(first - shift, last - shift)
                    block = made[first - base : last - base]
                    ref[there, :] = block if head == 0 else ref[there, :] + block

    mixed_t, grad_query_t = [None, None], [None, None]

    def query_side(head):
        cols, dims = slice(head * ROWS, (head + 1) * ROWS), slice(head * 64, (head + 1) * 64)
        mixed_t[head] = dot(values_t[dims, :], weights[:, cols])
        grad_query_t[head] = dot(keys_t[dims, :], grad_s[:, cols])

    for base in bases:
        score(0, base)
    for base in bases:
        lift(0, base)
        score(1, base)
    for base in bases:
        settle(0, base)
        lift(1, base)
    for base in bases:
        row_grads(0, base)
        settle(1, base)
    query_side(0)
    for base in bases:
        row_grads(1, base)
    query_side(1)
    mixed[...] = jnp.concatenate(mixed_t, axis=0).T.astype(LOW)
    grad_query[...] = (jnp.concatenate(grad_query_t, axis=0).T * 0.125).astype(LOW)

    grad_mem[0] = rest_k[0 : READS * MEM, :]
    grad_mem[1] = rest_v[0 : READS * MEM, :]
    grad_mem_low[0] = rest_k[0 : READS * MEM, :].astype(LOW)
    grad_mem_low[1] = rest_v[0 : READS * MEM, :].astype(LOW)
    for slot in range(SLOTS):

        @pl.when(slot_live[slot])
        def _():
            start = FAR_AT - ROWS + slot_at[slot] * STRIP
            at = pl.ds(pl.multiple_of(start, STRIP), STRIP)
            far_out[slot // 2][0, slot % 2] = rest_k[at, :].astype(LOW)
            far_out[slot // 2][1, slot % 2] = rest_v[at, :].astype(LOW)


def attention(group, ids, offsets, count, queries, grads, keys_own, values_own, keys_mem, values_mem, far):
    first, pairs = group
    width = pairs * PAIR

    def taken(rows):
        return pl.BlockSpec((rows, PAIR), lambda p, *_: (0, first + p))

    def made(rows):
        return pl.BlockSpec((rows, PAIR), lambda p, *_: (0, p))

    far_in = pl.BlockSpec((2, 2, STRIP, PAIR), lambda p, *_: (0, 0, 0, first + p))
    far_out = pl.BlockSpec((2, 2, STRIP, PAIR), lambda p, *_: (0, 0, 0, p))
    mem_out = pl.BlockSpec((2, READS * MEM, PAIR), lambda p, *_: (0, 0, p))
    return call(
        attention_kernel,
        pairs,
        3,
        [taken(ROWS)] * 4 + [taken(READS * MEM)] * 2 + [far_in] * 3,
        [made(ROWS)] * 4 + [mem_out] * 2 + [far_out] * 3,
        [array((ROWS, width), LOW)] * 2
        + [array((ROWS, width), WIDE)] * 2
        + [array((2, READS * MEM, width), WIDE), array((2, READS * MEM, width), LOW)]
        + [array((2, 2, STRIP, width), LOW)] * 3,
        [pltpu.VMEM((KEYS, PAIR), LOW)] * 2
        + [pltpu.VMEM((PAIR, KEYS), LOW)] * 2
        + [pltpu.VMEM((2, KEYS, ROWS), WIDE)] * 2
        + [pltpu.VMEM((KEYS, 2 * ROWS), LOW)] * 2
        + [pltpu.VMEM((2 * ROWS, PAIR), LOW)] * 2
        + [pltpu.VMEM((KEYS - ROWS, PAIR), WIDE)] * 2,
        pairs * 12 * KEYS * 2 * ROWS * 256,
        pairs * (3 << 20),
    )(ids, offsets, count, queries, grads, keys_own, values_own, keys_mem, values_mem, *far)


def sort_kernel(ids, offsets, *rest):
    count = len(GROUPS)
    own, given = rest[:count], rest[count : 2 * count]
    outs, total = rest[2 * count : 2 * count + 4], rest[2 * count + 4]
    frame = ids[1]
    z_here, x_here, core_here = parts_of(frame)
    partner = frame + 1 - 2 * core_here
    total[...] = jnp.zeros_like(total)
    for reader, arrays in ((frame, own), (partner, given)):
        for read in range(READS):
            source, live = source_of(offsets, reader, read)
            z_at, x_at, core_at = parts_of(source)
            to = lax.rem(x_at - x_here + 4, 4) * 4 + lax.rem(z_at - z_here + 4, 4)

            @pl.when(jnp.logical_and(live, core_at == core_here))
            def _():
                for (first, pairs), part in zip(GROUPS, arrays):
                    cols = slice(first * PAIR, (first + pairs) * PAIR)
                    for kind in range(2):
                        added = part[kind, read * MEM : (read + 1) * MEM, :].astype(WIDE)
                        total[to, kind, :, cols] = total[to, kind, :, cols] + added

    for shift in range(4):
        outs[shift][...] = total[4 * shift : 4 * shift + 4].astype(LOW)


def sort_reads(ids, offsets, own, given):
    shapes = [(2, READS * MEM, pairs * PAIR) for _, pairs in GROUPS]
    return call(
        sort_kernel,
        1,
        2,
        [whole(s) for s in shapes] * 2,
        [whole((4, 2, MEM, INNER))] * 4,
        [array((4, 2, MEM, INNER), LOW)] * 4,
        [pltpu.VMEM((16, 2, MEM, INNER), WIDE)],
        0,
        3 << 20,
    )(ids, offsets, *own, *given)


def add_kernel(part_0, part_1, part_2, part_3, *outs):
    for shift in range(4):
        total = part_0[shift].astype(WIDE) + part_1[shift].astype(WIDE)
        total = total + part_2[shift].astype(WIDE) + part_3[shift].astype(WIDE)
        outs[shift][...] = total.astype(LOW)


def add_reads(parts):
    return call(
        add_kernel,
        1,
        0,
        [whole((4, 2, MEM, INNER))] * 4,
        [whole((2, MEM, INNER))] * 4,
        [array((2, MEM, INNER), LOW)] * 4,
        [],
        0,
        2 << 20,
    )(*parts)


def outward_kernel(*refs):
    count = len(GROUPS)
    mixed, grad_query = refs[:count], refs[count : 2 * count]
    w_out, w_query, update, grad_normed = refs[2 * count :]
    total, part = 0.0, 0.0
    for (first, pairs), mixed_ref, grad_ref in zip(GROUPS, mixed, grad_query):
        cols = slice(first * PAIR, (first + pairs) * PAIR)
        total = total + dot(mixed_ref[...], w_out[cols, :])
        part = part + dot_t(grad_ref[...], w_query[:, cols])
    update[...] = total.astype(LOW)
    grad_normed[...] = part


def outward(mixed, grad_query, w_out, w_query):
    width = 512
    out = pl.BlockSpec((ROWS, width), lambda j: (0, j))
    parts = [whole((ROWS, pairs * PAIR)) for _, pairs in GROUPS]
    return call(
        outward_kernel,
        MODEL // width,
        0,
        parts
        + parts
        + [
            pl.BlockSpec((INNER, width), lambda j: (0, j)),
            pl.BlockSpec((width, INNER), lambda j: (j, 0)),
        ],
        [out, out],
        [array((ROWS, MODEL), LOW), array((ROWS, MODEL), WIDE)],
        [],
        4 * ROWS * MODEL * INNER,
        11 << 20,
    )(*mixed, *grad_query, w_out, w_query)


def token_grads_kernel(ids, count, index, *refs):
    groups = len(GROUPS)
    own = (refs[:groups], refs[groups : 2 * groups])
    back, refs = refs[2 * groups : 5 * groups], refs[5 * groups :]
    kept, (tokens, grad_part, w_key, w_value, grad_tokens), refs = refs[:4], refs[4:9], refs[9:]
    total, far, near, rows, grad_normed, key_w, value_w, low, made = refs[:9]
    own_sem, far_sem, near_sem, in_sem, out_sem = refs[9:]
    camera = ids[0]

    near_loads = [pltpu.make_async_copy(kept[k], near.at[k], near_sem.at[k]) for k in range(4)]
    own_loads, far_loads = [], []
    for group, (first, pairs) in enumerate(GROUPS):
        cols = pl.ds(first * PAIR, pairs * PAIR)
        for kind in range(2):
            own_loads.append(
                pltpu.make_async_copy(
                    own[kind][group], total.at[kind, :, cols], own_sem.at[2 * group + kind]
                )
            )
        for k in range(3):
            far_loads.append(
                pltpu.make_async_copy(
                    back[3 * group + k], far.at[k, :, :, :, cols], far_sem.at[3 * group + k]
                )
            )
    pairs_of_refs = ((w_key, key_w), (w_value, value_w), (grad_part, grad_normed), (tokens, rows))
    loads = [
        pltpu.make_async_copy(source, target, in_sem.at[k])
        for k, (source, target) in enumerate(pairs_of_refs)
    ]
    for load in own_loads + far_loads + near_loads + loads:
        load.start()
    for load in own_loads + far_loads:
        load.wait()
    for shift in (1, 2, 3):
        other = lax.rem(camera + shift, 4)
        for slot in range(2):

            @pl.when(slot < count[camera, other])
            def _():
                start = index[camera, other, slot] * STRIP
                at = pl.ds(pl.multiple_of(start, STRIP), STRIP)
                for kind in range(2):
                    total[kind, at, :] = total[kind, at, :] + far[shift - 1, kind, slot].astype(WIDE)

    for load in near_loads:
        load.wait()
    half = ROWS // 2
    row = lax.broadcasted_iota(jnp.int32, (half, 4 * MEM), 0)
    col = lax.broadcasted_iota(jnp.int32, (half, 4 * MEM), 1)
    stacked = [jnp.concatenate([near[k, kind] for k in range(4)], axis=0) for kind in range(2)]
    for load in loads:
        load.wait()
    stores = []
    for start in range(0, ROWS, half):
        at = slice(start, start + half)
        hit = row + start == (col % MEM) * (ROWS // MEM)
        spread = jnp.where(hit, 1.0, 0.0).astype(LOW)
        for kind in range(2):
            low[kind, at, :] = (total[kind, at, :] + dot(spread, stacked[kind])).astype(LOW)
        for first in range(0, MODEL, 512):
            cols = slice(first, first + 512)
            grad_normed[at, cols] = (
                grad_normed[at, cols]
                + dot_t(low[0, at, :], key_w[cols, :])
                + dot_t(low[1, at, :], value_w[cols, :])
            )
        for begin in range(start, start + half, 64):
            at = slice(begin, begin + 64)
            normed, inverse = normalize(rows[at, :])
            grad = grad_normed[at, :]
            first_mean = jnp.mean(grad, axis=-1, keepdims=True)
            second_mean = jnp.mean(grad * normed, axis=-1, keepdims=True)
            made[at, :] = (inverse * (grad - first_mean - normed * second_mean)).astype(LOW)
        block = pl.ds(start, half)
        stores.append(
            pltpu.make_async_copy(made.at[block], grad_tokens.at[block], out_sem.at[start // half])
        )
        stores[-1].start()
    for store in stores:
        store.wait()


def token_grads(ids, count, index, own_keys, own_values, back, kept, tokens, grad_part, w_key, w_value):
    groups = len(GROUPS)
    return call(
        token_grads_kernel,
        1,
        3,
        [IN_PLACE] * (5 * groups + 8),
        IN_PLACE,
        array((ROWS, MODEL), LOW),
        [
            pltpu.VMEM((2, ROWS, INNER), WIDE),
            pltpu.VMEM((3, 2, 2, STRIP, INNER), LOW),
            pltpu.VMEM((4, 2, MEM, INNER), LOW),
            pltpu.VMEM((ROWS, MODEL), LOW),
            pltpu.VMEM((ROWS, MODEL), WIDE),
            pltpu.VMEM((MODEL, INNER), LOW),
            pltpu.VMEM((MODEL, INNER), LOW),
            pltpu.VMEM((2, ROWS, INNER), LOW),
            pltpu.VMEM((ROWS, MODEL), LOW),
            pltpu.SemaphoreType.DMA((2 * groups,)),
            pltpu.SemaphoreType.DMA((3 * groups,)),
            pltpu.SemaphoreType.DMA((4,)),
            pltpu.SemaphoreType.DMA((4,)),
            pltpu.SemaphoreType.DMA((2,)),
        ],
        4 * ROWS * MODEL * INNER,
        16 << 20,
        vmem=26,
    )(ids, count, index, *own_keys, *own_values, *back, *kept, tokens, grad_part, w_key, w_value)


def send(value, axis, pairs):
    return lax.ppermute(value, axis, pairs)


def local(tokens, w_query, w_key, w_value, w_out, grad_update, offsets, count, index):
    tokens = tokens.reshape(ROWS, MODEL)
    grad_update = grad_update.reshape(ROWS, MODEL)
    ids = jnp.stack([lax.axis_index("cam"), lax.axis_index("tm")]).astype(jnp.int32)
    others = (1, 2, 3)

    kept = tokens.reshape(MEM, ROWS // MEM, MODEL)[:, 0]
    along_z = jnp.stack([kept] + [send(kept, "tm", shift_z(k)) for k in others])
    low, keys, values, *sends = project_keys(ids, index, tokens, w_key, w_value)
    far = [send(sends[k - 1], "cam", shift_cam(k)) for k in others]
    held = [along_z] + [send(along_z, "tm", shift_x(k)) for k in others]
    queries, grads = project_queries(low, grad_update, w_query, w_out)
    given = send(pick(ids, offsets, held), "tm", SWAP_CORE)
    keys_mem, values_mem = project_memory(ids, offsets, held, given, w_key, w_value)

    made, mem_given, back = [], [], []
    for group in GROUPS:
        args = (queries, grads, keys, values, keys_mem, values_mem, far)
        made.append(attention(group, ids, offsets, count, *args))
        mem_given.append(send(made[-1][5], "tm", SWAP_CORE))
        back += [send(made[-1][5 + k], "cam", shift_cam(-k)) for k in others]
    mixed, grad_query, own_keys, own_values, mem = [[m[k] for m in made] for k in range(5)]

    sorted_x = sort_reads(ids, offsets, mem, mem_given)
    parts = [sorted_x[0]] + [send(sorted_x[k], "tm", shift_x(k)) for k in others]
    update, grad_part = outward(mixed, grad_query, w_out, w_query)
    sorted_z = add_reads(parts)
    kept_grads = [sorted_z[0]] + [send(sorted_z[k], "tm", shift_z(k)) for k in others]
    args = (own_keys, own_values, back, kept_grads, tokens, grad_part, w_key, w_value)
    grad_tokens = token_grads(ids, count, index, *args)
    shape = (1, 1, ROWS, MODEL)
    return update.reshape(shape), grad_tokens.reshape(shape)


def solution(mesh):
    frames = P("cam", "tm", None, None)
    return jax.shard_map(
        local,
        mesh=mesh,
        in_specs=(frames, P(), P(), P(), P(), frames, P(), P(), P()),
        out_specs=(frames, frames),
        check_vma=False,
    )
```

```python
import jax
import jax.numpy as jnp
from jax import lax
from jax.experimental import pallas as pl
from jax.experimental.pallas import tpu as pltpu
from jax.sharding import PartitionSpec as P


LOW = jnp.bfloat16
WIDE = jnp.float32
ROWS = 512
MODEL = 1536
INNER = 768
STRIP = 128
MEM = 32
READS = 4
SLOTS = 6
LIVE_MAX = 4
MEM_AT = ROWS
FAR_AT = ROWS + READS * MEM
KEYS = FAR_AT + LIVE_MAX * STRIP
PAIR = 128
CHUNK = 384
EPS = 1e-05
MASKED = -1e30
NT = (((1,), (1,)), ((), ()))
GROUPS = ((0, 3), (3, 3))


def dot(left, right):
    return jnp.dot(left, right, preferred_element_type=WIDE)


def dot_t(left, right):
    return lax.dot_general(left, right, NT, preferred_element_type=WIDE)


def whole(shape):
    return pl.BlockSpec(shape, lambda *_: (0,) * len(shape))


def call(kernel, grid, scalars, in_specs, out_specs, out_shape, scratch, flops, moved, vmem=24):
    return pl.pallas_call(
        kernel,
        grid_spec=pltpu.PrefetchScalarGridSpec(
            num_scalar_prefetch=scalars,
            grid=(grid,),
            in_specs=in_specs,
            out_specs=out_specs,
            scratch_shapes=scratch,
        ),
        out_shape=out_shape,
        compiler_params=pltpu.CompilerParams(
            dimension_semantics=("arbitrary",), vmem_limit_bytes=vmem << 20
        ),
        cost_estimate=pl.CostEstimate(flops=flops, bytes_accessed=moved, transcendentals=0),
    )


IN_PLACE = pl.BlockSpec(memory_space=pl.ANY)
IN_HBM = pl.BlockSpec(memory_space=pltpu.HBM)


def array(shape, dtype):
    return jax.ShapeDtypeStruct(shape, dtype)


def normalize(rows):
    widened = rows.astype(WIDE)
    average = jnp.mean(widened, axis=-1, keepdims=True)
    centred = widened - average
    spread = jnp.mean(centred * centred, axis=-1, keepdims=True)
    inverse = lax.rsqrt(spread + EPS)
    return centred * inverse, inverse


def project_keys_kernel(ids, index, tokens, w_key, w_value, low, keys, values, *rest):
    sends, (rows, key_w, value_w, normed_low, made, in_sem, out_sem, send_sem) = rest[:3], rest[3:]
    camera = ids[0]
    loads = []
    for step, start in enumerate(range(0, ROWS, STRIP)):
        at = pl.ds(start, STRIP)
        loads.append(pltpu.make_async_copy(tokens.at[at], rows.at[at], in_sem.at[step]))
    loads.append(pltpu.make_async_copy(w_key, key_w, in_sem.at[4]))
    loads.append(pltpu.make_async_copy(w_value, value_w, in_sem.at[5]))
    for load in loads:
        load.start()

    def norm(first, last):
        for start in range(first, last, 64):
            at = slice(start, start + 64)
            normed_low[at, :] = normalize(rows[at, :])[0].astype(LOW)

    def product(kind, weight, first, last):
        for start in range(0, INNER, 256):
            cols = slice(start, start + 256)
            made[kind, first:last, cols] = dot(normed_low[first:last, :], weight[:, cols]).astype(LOW)

    stores = []

    def store(source, target, sem):
        stores.append(pltpu.make_async_copy(source, target, sem))
        stores[-1].start()

    def publish(kind, out):
        for shift in (1, 2, 3):
            for slot in range(2):
                strip = index[camera, lax.rem(camera + shift, 4), slot]
                at = pl.ds(pl.multiple_of(strip * STRIP, STRIP), STRIP)
                sem = send_sem.at[kind * SLOTS + 2 * (shift - 1) + slot]
                store(made.at[kind, at], sends[shift - 1].at[kind, slot], sem)
        store(made.at[kind], out, out_sem.at[1 + kind])

    half = ROWS // 2
    loads[0].wait()
    loads[1].wait()
    norm(0, half)
    for load in loads[2:5]:
        load.wait()
    product(0, key_w, 0, half)
    norm(half, ROWS)
    store(normed_low, low, out_sem.at[0])
    product(0, key_w, half, ROWS)
    publish(0, keys)
    loads[5].wait()
    product(1, value_w, 0, ROWS)
    publish(1, values)
    for copy in stores:
        copy.wait()


def project_keys(ids, index, tokens, w_key, w_value):
    return call(
        project_keys_kernel,
        1,
        2,
        [IN_HBM] * 3,
        [IN_PLACE] * 6,
        [array((ROWS, MODEL), LOW), array((ROWS, INNER), LOW), array((ROWS, INNER), LOW)]
        + [array((2, 2, STRIP, INNER), LOW)] * 3,
        [
            pltpu.VMEM((ROWS, MODEL), LOW),
            pltpu.VMEM((MODEL, INNER), LOW),
            pltpu.VMEM((MODEL, INNER), LOW),
            pltpu.VMEM((ROWS, MODEL), LOW),
            pltpu.VMEM((2, ROWS, INNER), LOW),
            pltpu.SemaphoreType.DMA((6,)),
            pltpu.SemaphoreType.DMA((3,)),
            pltpu.SemaphoreType.DMA((2 * SLOTS,)),
        ],
        4 * ROWS * MODEL * INNER,
        12 << 20,
        vmem=60,
    )(ids, index, tokens, w_key, w_value)


def project_queries_kernel(low, grad_update, w_query, w_out, queries, grad_mixed):
    product = dot(low[...], w_query[...]).astype(LOW)
    queries[...] = product * jnp.asarray(0.125, LOW)
    grad_mixed[...] = dot_t(grad_update[...], w_out[...]).astype(LOW)


def project_queries(low, grad_update, w_query, w_out):
    width = 384
    out = pl.BlockSpec((ROWS, width), lambda j: (0, j))
    return call(
        project_queries_kernel,
        INNER // width,
        0,
        [
            whole((ROWS, MODEL)),
            whole((ROWS, MODEL)),
            pl.BlockSpec((MODEL, width), lambda j: (0, j)),
            pl.BlockSpec((width, MODEL), lambda j: (j, 0)),
        ],
        [out, out],
        [array((ROWS, INNER), LOW)] * 2,
        [],
        4 * ROWS * MODEL * INNER,
        10 << 20,
    )(low, grad_update, w_query, w_out)


def parts_of(frame):
    return frame // 8, lax.rem(frame // 2, 4), lax.rem(frame, 2)


def source_of(offsets, frame, read):
    source = frame - offsets[frame, read]
    return jnp.maximum(source, 0), source >= 0


def back_to(frame, source):
    z_here, x_here, core_here = parts_of(frame)
    z_at, x_at, core_at = parts_of(source)
    return lax.rem(z_here - z_at + 4, 4), lax.rem(x_here - x_at + 4, 4), core_at == core_here


def pick_kernel(ids, offsets, held_0, held_1, held_2, held_3, picked, sem):
    frame = ids[1]
    partner = frame + 1 - 2 * lax.rem(frame, 2)
    held = (held_0, held_1, held_2, held_3)
    wanted = []
    for read in range(READS):
        source, live = source_of(offsets, partner, read)
        back_z, back_x, same = back_to(frame, source)
        wanted.append(jnp.logical_and(live, same))
        for shift in range(4):

            @pl.when(jnp.logical_and(wanted[read], back_x == shift))
            def _():
                pltpu.make_async_copy(held[shift].at[back_z], picked.at[read], sem.at[read]).start()

        @pl.when(jnp.logical_not(wanted[read]))
        def _():
            picked[read] = jnp.zeros((MEM, MODEL), LOW)

    for read in range(READS):

        @pl.when(wanted[read])
        def _():
            pltpu.make_async_copy(held_0.at[0], picked.at[read], sem.at[read]).wait()


def pick(ids, offsets, held):
    return call(
        pick_kernel,
        1,
        2,
        [IN_PLACE] * 4,
        whole((READS, MEM, MODEL)),
        array((READS, MEM, MODEL), LOW),
        [pltpu.SemaphoreType.DMA((READS,))],
        0,
        1 << 20,
        vmem=2,
    )(ids, offsets, *held)


def project_memory_kernel(ids, offsets, held_0, held_1, held_2, held_3, given, w_key, w_value, keys, values, *rest):
    rows, low, key_w, value_w, sem, w_sem = rest
    frame = ids[1]
    held = (held_0, held_1, held_2, held_3)
    loads = [
        pltpu.make_async_copy(w_key, key_w, w_sem.at[0]),
        pltpu.make_async_copy(w_value, value_w, w_sem.at[1]),
    ]
    for read in range(READS):
        source, live = source_of(offsets, frame, read)
        back_z, back_x, same = back_to(frame, source)
        mine = jnp.logical_and(live, same)
        for shift in range(4):

            @pl.when(jnp.logical_and(mine, back_x == shift))
            def _():
                pltpu.make_async_copy(held[shift].at[back_z], rows.at[read], sem.at[read]).start()

        @pl.when(jnp.logical_not(mine))
        def _():
            pltpu.make_async_copy(given.at[read], rows.at[read], sem.at[read]).start()

    for load in loads:
        load.start()
    for read in range(READS):
        pltpu.make_async_copy(given.at[read], rows.at[read], sem.at[read]).wait()
        low[read * MEM : (read + 1) * MEM, :] = normalize(rows[read])[0].astype(LOW)
    for load, weight, out in zip(loads, (key_w, value_w), (keys, values)):
        load.wait()
        for start in range(0, INNER, 256):
            cols = slice(start, start + 256)
            out[:, cols] = dot(low[...], weight[:, cols]).astype(LOW)


def project_memory(ids, offsets, held, given, w_key, w_value):
    return call(
        project_memory_kernel,
        1,
        2,
        [IN_PLACE] * 5 + [IN_HBM] * 2,
        [whole((READS * MEM, INNER))] * 2,
        [array((READS * MEM, INNER), LOW)] * 2,
        [
            pltpu.VMEM((READS, MEM, MODEL), LOW),
            pltpu.VMEM((READS * MEM, MODEL), LOW),
            pltpu.VMEM((MODEL, INNER), LOW),
            pltpu.VMEM((MODEL, INNER), LOW),
            pltpu.SemaphoreType.DMA((READS,)),
            pltpu.SemaphoreType.DMA((2,)),
        ],
        4 * READS * MEM * MODEL * INNER,
        6 << 20,
        vmem=10,
    )(ids, offsets, *held, given, w_key, w_value)


def shift_z(by):
    return [(f, (f + 8 * by) % 32) for f in range(32)]


def shift_x(by):
    return [(f, f // 8 * 8 + (f % 8 + 2 * by) % 8) for f in range(32)]


SWAP_CORE = [(f, f ^ 1) for f in range(32)]


def shift_cam(by):
    return [(s, (s + by) % 4) for s in range(4)]


def attention_kernel(ids, offsets, count, queries, grads, keys_own, values_own, keys_mem, values_mem, *rest):
    far_in, rest = rest[:3], rest[3:]
    mixed, grad_query, grad_keys, grad_values, grad_mem, grad_mem_low = rest[:6]
    far_out, rest = rest[6:9], rest[9:]
    keys, values, keys_t, values_t, scores, grad_w, weights, grad_s, two_q, two_g, rest_k, rest_v = rest
    camera, frame = ids[0], ids[1]

    slot_live, slot_at, live_total = [], [], 0
    for slot in range(SLOTS):
        sender = lax.rem(camera + 4 - (slot // 2 + 1), 4)
        live = count[sender, camera] > slot % 2
        slot_live.append(jnp.logical_and(live, live_total < LIVE_MAX))
        slot_at.append(jnp.minimum(live_total, LIVE_MAX - 1))
        live_total = live_total + live.astype(jnp.int32)

    keys[0:ROWS, :] = keys_own[...]
    values[0:ROWS, :] = values_own[...]
    keys[MEM_AT:FAR_AT, :] = keys_mem[...]
    values[MEM_AT:FAR_AT, :] = values_mem[...]
    for place in range(LIVE_MAX):

        @pl.when(live_total <= place)
        def _():
            at = slice(FAR_AT + place * STRIP, FAR_AT + (place + 1) * STRIP)
            keys[at, :] = jnp.zeros((STRIP, PAIR), LOW)
            values[at, :] = jnp.zeros((STRIP, PAIR), LOW)

    for slot in range(SLOTS):

        @pl.when(slot_live[slot])
        def _():
            at = pl.ds(pl.multiple_of(FAR_AT + slot_at[slot] * STRIP, STRIP), STRIP)
            keys[at, :] = far_in[slot // 2][0, slot % 2]
            values[at, :] = far_in[slot // 2][1, slot % 2]

    keys_t[...] = keys[...].T
    values_t[...] = values[...].T
    lane = lax.broadcasted_iota(jnp.int32, (ROWS, PAIR), 1)
    for head in range(2):
        keep = (lane >= 64) if head else (lane < 64)
        at = slice(head * ROWS, (head + 1) * ROWS)
        two_q[at, :] = jnp.where(keep, queries[...], jnp.zeros((ROWS, PAIR), LOW))
        two_g[at, :] = jnp.where(keep, grads[...], jnp.zeros((ROWS, PAIR), LOW))

    pieces = [(0, ROWS, None)]
    for read in range(READS):
        start = MEM_AT + read * MEM
        pieces.append((start, start + MEM, offsets[frame, read] <= frame))
    for place in range(LIVE_MAX):
        start = FAR_AT + place * STRIP
        pieces.append((start, start + STRIP, place < live_total))

    def pieces_of(base):
        for start, end, live in pieces:
            low, high = max(start, base), min(end, base + CHUNK)
            if low < high:
                yield low, high, live

    def folded(block):
        return block.reshape(block.shape[0] // 8, 8, ROWS)

    bases = range(0, KEYS, CHUNK)
    highest = [jnp.full((8, ROWS), MASKED, WIDE)] * 2
    total, inner = [jnp.zeros((8, ROWS), WIDE)] * 2, [jnp.zeros((8, ROWS), WIDE)] * 2
    share = [None, None]

    def score(head, base):
        cols = slice(head * ROWS, (head + 1) * ROWS)
        block = dot_t(keys[base : base + CHUNK, :], two_q[cols, :])
        scores[head, base : base + CHUNK, :] = block
        for low, high, live in pieces_of(base):
            top = jnp.max(folded(block[low - base : high - base]), axis=0)
            top = jnp.maximum(highest[head], top)
            highest[head] = top if live is None else jnp.where(live, top, highest[head])
        if base == bases[-1]:
            highest[head] = jnp.max(highest[head], axis=0, keepdims=True)

    def lift(head, base):
        cols = slice(head * ROWS, (head + 1) * ROWS)
        block = dot_t(values[base : base + CHUNK, :], two_g[cols, :])
        grad_w[head, base : base + CHUNK, :] = block
        for low, high, live in pieces_of(base):
            top = highest[head] if live is None else jnp.where(live, highest[head], -MASKED)
            lifted = jnp.exp(scores[head, low:high, :] - top)
            scores[head, low:high, :] = lifted
            total[head] = total[head] + jnp.sum(folded(lifted), axis=0)
            inner[head] = inner[head] + jnp.sum(folded(lifted * block[low - base : high - base]), axis=0)
        if base == bases[-1]:
            share[head] = 1.0 / jnp.sum(total[head], axis=0, keepdims=True)
            inner[head] = jnp.sum(inner[head], axis=0, keepdims=True) * share[head]

    def settle(head, base):
        cols, at = slice(head * ROWS, (head + 1) * ROWS), slice(base, base + CHUNK)
        part = scores[head, at, :] * share[head]
        weights[at, cols] = part.astype(LOW)
        grad_s[at, cols] = (part * (grad_w[head, at, :] - inner[head])).astype(LOW)

    def row_grads(head, base):
        cols, at = slice(head * ROWS, (head + 1) * ROWS), slice(base, base + CHUNK)
        for_value = dot(weights[at, cols], two_g[cols, :])
        for_key = dot(grad_s[at, cols], two_q[cols, :])
        for made, own, far in ((for_key, grad_keys, rest_k), (for_value, grad_values, rest_v)):
            for start, end, ref, shift in ((0, ROWS, own, 0), (ROWS, KEYS, far, ROWS)):
                first, last = max(start, base), min(end, base + CHUNK)
                if first < last:
                    there = slice(first - shift, last - shift)
                    block = made[first - base : last - base]
                    ref[there, :] = block if head == 0 else ref[there, :] + block

    mixed_t, grad_query_t = [None, None], [None, None]

    def query_side(head):
        cols, dims = slice(head * ROWS, (head + 1) * ROWS), slice(head * 64, (head + 1) * 64)
        mixed_t[head] = dot(values_t[dims, :], weights[:, cols])
        grad_query_t[head] = dot(keys_t[dims, :], grad_s[:, cols])

    for base in bases:
        score(0, base)
    for base in bases:
        lift(0, base)
        score(1, base)
    for base in bases:
        settle(0, base)
        lift(1, base)
    for base in bases:
        row_grads(0, base)
        settle(1, base)
    query_side(0)
    for base in bases:
        row_grads(1, base)
    query_side(1)
    mixed[...] = jnp.concatenate(mixed_t, axis=0).T.astype(LOW)
    grad_query[...] = (jnp.concatenate(grad_query_t, axis=0).T * 0.125).astype(LOW)

    grad_mem[0] = rest_k[0 : READS * MEM, :]
    grad_mem[1] = rest_v[0 : READS * MEM, :]
    grad_mem_low[0] = rest_k[0 : READS * MEM, :].astype(LOW)
    grad_mem_low[1] = rest_v[0 : READS * MEM, :].astype(LOW)
    for slot in range(SLOTS):

        @pl.when(slot_live[slot])
        def _():
            start = FAR_AT - ROWS + slot_at[slot] * STRIP
            at = pl.ds(pl.multiple_of(start, STRIP), STRIP)
            far_out[slot // 2][0, slot % 2] = rest_k[at, :].astype(LOW)
            far_out[slot // 2][1, slot % 2] = rest_v[at, :].astype(LOW)


def attention(group, ids, offsets, count, queries, grads, keys_own, values_own, keys_mem, values_mem, far):
    first, pairs = group
    width = pairs * PAIR

    def taken(rows):
        return pl.BlockSpec((rows, PAIR), lambda p, *_: (0, first + p))

    def made(rows):
        return pl.BlockSpec((rows, PAIR), lambda p, *_: (0, p))

    far_in = pl.BlockSpec((2, 2, STRIP, PAIR), lambda p, *_: (0, 0, 0, first + p))
    far_out = pl.BlockSpec((2, 2, STRIP, PAIR), lambda p, *_: (0, 0, 0, p))
    mem_out = pl.BlockSpec((2, READS * MEM, PAIR), lambda p, *_: (0, 0, p))
    return call(
        attention_kernel,
        pairs,
        3,
        [taken(ROWS)] * 4 + [taken(READS * MEM)] * 2 + [far_in] * 3,
        [made(ROWS)] * 4 + [mem_out] * 2 + [far_out] * 3,
        [array((ROWS, width), LOW)] * 2
        + [array((ROWS, width), WIDE)] * 2
        + [array((2, READS * MEM, width), WIDE), array((2, READS * MEM, width), LOW)]
        + [array((2, 2, STRIP, width), LOW)] * 3,
        [pltpu.VMEM((KEYS, PAIR), LOW)] * 2
        + [pltpu.VMEM((PAIR, KEYS), LOW)] * 2
        + [pltpu.VMEM((2, KEYS, ROWS), WIDE)] * 2
        + [pltpu.VMEM((KEYS, 2 * ROWS), LOW)] * 2
        + [pltpu.VMEM((2 * ROWS, PAIR), LOW)] * 2
        + [pltpu.VMEM((KEYS - ROWS, PAIR), WIDE)] * 2,
        pairs * 12 * KEYS * 2 * ROWS * 256,
        pairs * (3 << 20),
    )(ids, offsets, count, queries, grads, keys_own, values_own, keys_mem, values_mem, *far)


def sort_kernel(ids, offsets, *rest):
    count = len(GROUPS)
    own, given = rest[:count], rest[count : 2 * count]
    outs, total = rest[2 * count : 2 * count + 4], rest[2 * count + 4]
    frame = ids[1]
    z_here, x_here, core_here = parts_of(frame)
    partner = frame + 1 - 2 * core_here
    total[...] = jnp.zeros_like(total)
    for reader, arrays in ((frame, own), (partner, given)):
        for read in range(READS):
            source, live = source_of(offsets, reader, read)
            z_at, x_at, core_at = parts_of(source)
            to = lax.rem(x_at - x_here + 4, 4) * 4 + lax.rem(z_at - z_here + 4, 4)

            @pl.when(jnp.logical_and(live, core_at == core_here))
            def _():
                for (first, pairs), part in zip(GROUPS, arrays):
                    cols = slice(first * PAIR, (first + pairs) * PAIR)
                    for kind in range(2):
                        added = part[kind, read * MEM : (read + 1) * MEM, :].astype(WIDE)
                        total[to, kind, :, cols] = total[to, kind, :, cols] + added

    for shift in range(4):
        outs[shift][...] = total[4 * shift : 4 * shift + 4].astype(LOW)


def sort_reads(ids, offsets, own, given):
    shapes = [(2, READS * MEM, pairs * PAIR) for _, pairs in GROUPS]
    return call(
        sort_kernel,
        1,
        2,
        [whole(s) for s in shapes] * 2,
        [whole((4, 2, MEM, INNER))] * 4,
        [array((4, 2, MEM, INNER), LOW)] * 4,
        [pltpu.VMEM((16, 2, MEM, INNER), WIDE)],
        0,
        3 << 20,
    )(ids, offsets, *own, *given)


def add_kernel(part_0, part_1, part_2, part_3, *outs):
    for shift in range(4):
        total = part_0[shift].astype(WIDE) + part_1[shift].astype(WIDE)
        total = total + part_2[shift].astype(WIDE) + part_3[shift].astype(WIDE)
        outs[shift][...] = total.astype(LOW)


def add_reads(parts):
    return call(
        add_kernel,
        1,
        0,
        [whole((4, 2, MEM, INNER))] * 4,
        [whole((2, MEM, INNER))] * 4,
        [array((2, MEM, INNER), LOW)] * 4,
        [],
        0,
        2 << 20,
    )(*parts)


def outward_kernel(*refs):
    count = len(GROUPS)
    mixed, grad_query = refs[:count], refs[count : 2 * count]
    w_out, w_query, update, grad_normed = refs[2 * count :]
    total, part = 0.0, 0.0
    for (first, pairs), mixed_ref, grad_ref in zip(GROUPS, mixed, grad_query):
        cols = slice(first * PAIR, (first + pairs) * PAIR)
        total = total + dot(mixed_ref[...], w_out[cols, :])
        part = part + dot_t(grad_ref[...], w_query[:, cols])
    update[...] = total.astype(LOW)
    grad_normed[...] = part


def outward(mixed, grad_query, w_out, w_query):
    width = 512
    out = pl.BlockSpec((ROWS, width), lambda j: (0, j))
    parts = [whole((ROWS, pairs * PAIR)) for _, pairs in GROUPS]
    return call(
        outward_kernel,
        MODEL // width,
        0,
        parts
        + parts
        + [
            pl.BlockSpec((INNER, width), lambda j: (0, j)),
            pl.BlockSpec((width, INNER), lambda j: (j, 0)),
        ],
        [out, out],
        [array((ROWS, MODEL), LOW), array((ROWS, MODEL), WIDE)],
        [],
        4 * ROWS * MODEL * INNER,
        11 << 20,
    )(*mixed, *grad_query, w_out, w_query)


def token_grads_kernel(ids, count, index, *refs):
    groups = len(GROUPS)
    own = (refs[:groups], refs[groups : 2 * groups])
    back, refs = refs[2 * groups : 5 * groups], refs[5 * groups :]
    kept, (tokens, grad_part, w_key, w_value, grad_tokens), refs = refs[:4], refs[4:9], refs[9:]
    total, far, near, rows, grad_normed, key_w, value_w, low, made = refs[:9]
    own_sem, far_sem, near_sem, in_sem, out_sem = refs[9:]
    camera = ids[0]

    near_loads = [pltpu.make_async_copy(kept[k], near.at[k], near_sem.at[k]) for k in range(4)]
    own_loads, far_loads = [], []
    for group, (first, pairs) in enumerate(GROUPS):
        cols = pl.ds(first * PAIR, pairs * PAIR)
        for kind in range(2):
            own_loads.append(
                pltpu.make_async_copy(
                    own[kind][group], total.at[kind, :, cols], own_sem.at[2 * group + kind]
                )
            )
        for k in range(3):
            far_loads.append(
                pltpu.make_async_copy(
                    back[3 * group + k], far.at[k, :, :, :, cols], far_sem.at[3 * group + k]
                )
            )
    pairs_of_refs = ((w_key, key_w), (w_value, value_w), (grad_part, grad_normed), (tokens, rows))
    loads = [
        pltpu.make_async_copy(source, target, in_sem.at[k])
        for k, (source, target) in enumerate(pairs_of_refs)
    ]
    for load in own_loads + far_loads + near_loads + loads:
        load.start()
    for load in own_loads + far_loads:
        load.wait()
    for shift in (1, 2, 3):
        other = lax.rem(camera + shift, 4)
        for slot in range(2):

            @pl.when(slot < count[camera, other])
            def _():
                start = index[camera, other, slot] * STRIP
                at = pl.ds(pl.multiple_of(start, STRIP), STRIP)
                for kind in range(2):
                    total[kind, at, :] = total[kind, at, :] + far[shift - 1, kind, slot].astype(WIDE)

    for load in near_loads:
        load.wait()
    half = ROWS // 2
    row = lax.broadcasted_iota(jnp.int32, (half, 4 * MEM), 0)
    col = lax.broadcasted_iota(jnp.int32, (half, 4 * MEM), 1)
    stacked = [jnp.concatenate([near[k, kind] for k in range(4)], axis=0) for kind in range(2)]
    for load in loads:
        load.wait()
    stores = []
    for start in range(0, ROWS, half):
        at = slice(start, start + half)
        hit = row + start == (col % MEM) * (ROWS // MEM)
        spread = jnp.where(hit, 1.0, 0.0).astype(LOW)
        for kind in range(2):
            low[kind, at, :] = (total[kind, at, :] + dot(spread, stacked[kind])).astype(LOW)
        for first in range(0, MODEL, 512):
            cols = slice(first, first + 512)
            grad_normed[at, cols] = (
                grad_normed[at, cols]
                + dot_t(low[0, at, :], key_w[cols, :])
                + dot_t(low[1, at, :], value_w[cols, :])
            )
        for begin in range(start, start + half, 64):
            at = slice(begin, begin + 64)
            normed, inverse = normalize(rows[at, :])
            grad = grad_normed[at, :]
            first_mean = jnp.mean(grad, axis=-1, keepdims=True)
            second_mean = jnp.mean(grad * normed, axis=-1, keepdims=True)
            made[at, :] = (inverse * (grad - first_mean - normed * second_mean)).astype(LOW)
        block = pl.ds(start, half)
        stores.append(
            pltpu.make_async_copy(made.at[block], grad_tokens.at[block], out_sem.at[start // half])
        )
        stores[-1].start()
    for store in stores:
        store.wait()


def token_grads(ids, count, index, own_keys, own_values, back, kept, tokens, grad_part, w_key, w_value):
    groups = len(GROUPS)
    return call(
        token_grads_kernel,
        1,
        3,
        [IN_PLACE] * (5 * groups + 8),
        IN_PLACE,
        array((ROWS, MODEL), LOW),
        [
            pltpu.VMEM((2, ROWS, INNER), WIDE),
            pltpu.VMEM((3, 2, 2, STRIP, INNER), LOW),
            pltpu.VMEM((4, 2, MEM, INNER), LOW),
            pltpu.VMEM((ROWS, MODEL), LOW),
            pltpu.VMEM((ROWS, MODEL), WIDE),
            pltpu.VMEM((MODEL, INNER), LOW),
            pltpu.VMEM((MODEL, INNER), LOW),
            pltpu.VMEM((2, ROWS, INNER), LOW),
            pltpu.VMEM((ROWS, MODEL), LOW),
            pltpu.SemaphoreType.DMA((2 * groups,)),
            pltpu.SemaphoreType.DMA((3 * groups,)),
            pltpu.SemaphoreType.DMA((4,)),
            pltpu.SemaphoreType.DMA((4,)),
            pltpu.SemaphoreType.DMA((2,)),
        ],
        4 * ROWS * MODEL * INNER,
        16 << 20,
        vmem=26,
    )(ids, count, index, *own_keys, *own_values, *back, *kept, tokens, grad_part, w_key, w_value)


def send(value, axis, pairs):
    return lax.ppermute(value, axis, pairs)


def local(tokens, w_query, w_key, w_value, w_out, grad_update, offsets, count, index):
    tokens = tokens.reshape(ROWS, MODEL)
    grad_update = grad_update.reshape(ROWS, MODEL)
    ids = jnp.stack([lax.axis_index("cam"), lax.axis_index("tm")]).astype(jnp.int32)
    others = (1, 2, 3)

    kept = tokens.reshape(MEM, ROWS // MEM, MODEL)[:, 0]
    along_z = jnp.stack([kept] + [send(kept, "tm", shift_z(k)) for k in others])
    low, keys, values, *sends = project_keys(ids, index, tokens, w_key, w_value)
    far = [send(sends[k - 1], "cam", shift_cam(k)) for k in others]
    held = [along_z] + [send(along_z, "tm", shift_x(k)) for k in others]
    queries, grads = project_queries(low, grad_update, w_query, w_out)
    given = send(pick(ids, offsets, held), "tm", SWAP_CORE)
    keys_mem, values_mem = project_memory(ids, offsets, held, given, w_key, w_value)

    made, mem_given, back = [], [], []
    for group in GROUPS:
        args = (queries, grads, keys, values, keys_mem, values_mem, far)
        made.append(attention(group, ids, offsets, count, *args))
        mem_given.append(send(made[-1][5], "tm", SWAP_CORE))
        back += [send(made[-1][5 + k], "cam", shift_cam(-k)) for k in others]
    mixed, grad_query, own_keys, own_values, mem = [[m[k] for m in made] for k in range(5)]

    sorted_x = sort_reads(ids, offsets, mem, mem_given)
    parts = [sorted_x[0]] + [send(sorted_x[k], "tm", shift_x(k)) for k in others]
    update, grad_part = outward(mixed, grad_query, w_out, w_query)
    sorted_z = add_reads(parts)
    kept_grads = [sorted_z[0]] + [send(sorted_z[k], "tm", shift_z(k)) for k in others]
    args = (own_keys, own_values, back, kept_grads, tokens, grad_part, w_key, w_value)
    grad_tokens = token_grads(ids, count, index, *args)
    shape = (1, 1, ROWS, MODEL)
    return update.reshape(shape), grad_tokens.reshape(shape)


def solution(mesh):
    frames = P("cam", "tm", None, None)
    return jax.shard_map(
        local,
        mesh=mesh,
        in_specs=(frames, P(), P(), P(), P(), frames, P(), P(), P()),
        out_specs=(frames, frames),
        check_vma=False,
    )
```

```python
import jax
import jax.numpy as jnp
from jax import lax
from jax.experimental import pallas as pl
from jax.experimental.pallas import tpu as pltpu
from jax.sharding import PartitionSpec as P


LOW = jnp.bfloat16
WIDE = jnp.float32
ROWS = 512
MODEL = 1536
INNER = 768
STRIP = 128
MEM = 32
READS = 4
SLOTS = 6
LIVE_MAX = 4
MEM_AT = ROWS
FAR_AT = ROWS + READS * MEM
KEYS = FAR_AT + LIVE_MAX * STRIP
PAIR = 128
CHUNK = 384
EPS = 1e-05
MASKED = -1e30
NT = (((1,), (1,)), ((), ()))
GROUPS = ((0, 4), (4, 2))


def dot(left, right):
    return jnp.dot(left, right, preferred_element_type=WIDE)


def dot_t(left, right):
    return lax.dot_general(left, right, NT, preferred_element_type=WIDE)


def whole(shape):
    return pl.BlockSpec(shape, lambda *_: (0,) * len(shape))


def call(kernel, grid, scalars, in_specs, out_specs, out_shape, scratch, flops, moved, vmem=24):
    return pl.pallas_call(
        kernel,
        grid_spec=pltpu.PrefetchScalarGridSpec(
            num_scalar_prefetch=scalars,
            grid=(grid,),
            in_specs=in_specs,
            out_specs=out_specs,
            scratch_shapes=scratch,
        ),
        out_shape=out_shape,
        compiler_params=pltpu.CompilerParams(
            dimension_semantics=("arbitrary",), vmem_limit_bytes=vmem << 20
        ),
        cost_estimate=pl.CostEstimate(flops=flops, bytes_accessed=moved, transcendentals=0),
    )


IN_PLACE = pl.BlockSpec(memory_space=pl.ANY)
IN_HBM = pl.BlockSpec(memory_space=pltpu.HBM)


def array(shape, dtype):
    return jax.ShapeDtypeStruct(shape, dtype)


def normalize(rows):
    widened = rows.astype(WIDE)
    average = jnp.mean(widened, axis=-1, keepdims=True)
    centred = widened - average
    spread = jnp.mean(centred * centred, axis=-1, keepdims=True)
    inverse = lax.rsqrt(spread + EPS)
    return centred * inverse, inverse


def project_keys_kernel(ids, index, tokens, w_key, w_value, low, keys, values, *rest):
    sends, (rows, key_w, value_w, normed_low, made, in_sem, out_sem, send_sem) = rest[:3], rest[3:]
    camera = ids[0]
    loads = []
    for step, start in enumerate(range(0, ROWS, STRIP)):
        at = pl.ds(start, STRIP)
        loads.append(pltpu.make_async_copy(tokens.at[at], rows.at[at], in_sem.at[step]))
    loads.append(pltpu.make_async_copy(w_key, key_w, in_sem.at[4]))
    loads.append(pltpu.make_async_copy(w_value, value_w, in_sem.at[5]))
    for load in loads:
        load.start()

    def norm(first, last):
        for start in range(first, last, 64):
            at = slice(start, start + 64)
            normed_low[at, :] = normalize(rows[at, :])[0].astype(LOW)

    def product(kind, weight, first, last):
        for start in range(0, INNER, 256):
            cols = slice(start, start + 256)
            made[kind, first:last, cols] = dot(normed_low[first:last, :], weight[:, cols]).astype(LOW)

    stores = []

    def store(source, target, sem):
        stores.append(pltpu.make_async_copy(source, target, sem))
        stores[-1].start()

    def publish(kind, out):
        for shift in (1, 2, 3):
            for slot in range(2):
                strip = index[camera, slot, lax.rem(camera + shift, 4)]
                at = pl.ds(pl.multiple_of(strip * STRIP, STRIP), STRIP)
                sem = send_sem.at[kind * SLOTS + 2 * (shift - 1) + slot]
                store(made.at[kind, at], sends[shift - 1].at[kind, slot], sem)
        store(made.at[kind], out, out_sem.at[1 + kind])

    half = ROWS // 2
    loads[0].wait()
    loads[1].wait()
    norm(0, half)
    for load in loads[2:5]:
        load.wait()
    product(0, key_w, 0, half)
    norm(half, ROWS)
    store(normed_low, low, out_sem.at[0])
    product(0, key_w, half, ROWS)
    publish(0, keys)
    loads[5].wait()
    product(1, value_w, 0, ROWS)
    publish(1, values)
    for copy in stores:
        copy.wait()


def project_keys(ids, index, tokens, w_key, w_value):
    return call(
        project_keys_kernel,
        1,
        2,
        [IN_HBM] * 3,
        [IN_PLACE] * 6,
        [array((ROWS, MODEL), LOW), array((ROWS, INNER), LOW), array((ROWS, INNER), LOW)]
        + [array((2, 2, STRIP, INNER), LOW)] * 3,
        [
            pltpu.VMEM((ROWS, MODEL), LOW),
            pltpu.VMEM((MODEL, INNER), LOW),
            pltpu.VMEM((MODEL, INNER), LOW),
            pltpu.VMEM((ROWS, MODEL), LOW),
            pltpu.VMEM((2, ROWS, INNER), LOW),
            pltpu.SemaphoreType.DMA((6,)),
            pltpu.SemaphoreType.DMA((3,)),
            pltpu.SemaphoreType.DMA((2 * SLOTS,)),
        ],
        4 * ROWS * MODEL * INNER,
        12 << 20,
        vmem=60,
    )(ids, index, tokens, w_key, w_value)


def project_queries_kernel(low, grad_update, w_query, w_out, queries, grad_mixed):
    product = dot(low[...], w_query[...]).astype(LOW)
    queries[...] = product * jnp.asarray(0.125, LOW)
    grad_mixed[...] = dot_t(grad_update[...], w_out[...]).astype(LOW)


def project_queries(low, grad_update, w_query, w_out):
    width = 384
    out = pl.BlockSpec((ROWS, width), lambda j: (0, j))
    return call(
        project_queries_kernel,
        INNER // width,
        0,
        [
            whole((ROWS, MODEL)),
            whole((ROWS, MODEL)),
            pl.BlockSpec((MODEL, width), lambda j: (0, j)),
            pl.BlockSpec((width, MODEL), lambda j: (j, 0)),
        ],
        [out, out],
        [array((ROWS, INNER), LOW)] * 2,
        [],
        4 * ROWS * MODEL * INNER,
        10 << 20,
    )(low, grad_update, w_query, w_out)


def parts_of(frame):
    return frame // 8, lax.rem(frame // 2, 4), lax.rem(frame, 2)


def source_of(offsets, frame, read):
    source = frame - offsets[read, frame]
    return jnp.maximum(source, 0), source >= 0


def back_to(frame, source):
    z_here, x_here, core_here = parts_of(frame)
    z_at, x_at, core_at = parts_of(source)
    return lax.rem(z_here - z_at + 4, 4), lax.rem(x_here - x_at + 4, 4), core_at == core_here


def pick_kernel(ids, offsets, held_0, held_1, held_2, held_3, picked, sem):
    frame = ids[1]
    partner = frame + 1 - 2 * lax.rem(frame, 2)
    held = (held_0, held_1, held_2, held_3)
    wanted = []
    for read in range(READS):
        source, live = source_of(offsets, partner, read)
        back_z, back_x, same = back_to(frame, source)
        wanted.append(jnp.logical_and(live, same))
        for shift in range(4):

            @pl.when(jnp.logical_and(wanted[read], back_x == shift))
            def _():
                pltpu.make_async_copy(held[shift].at[back_z], picked.at[read], sem.at[read]).start()

        @pl.when(jnp.logical_not(wanted[read]))
        def _():
            picked[read] = jnp.zeros((MEM, MODEL), LOW)

    for read in range(READS):

        @pl.when(wanted[read])
        def _():
            pltpu.make_async_copy(held_0.at[0], picked.at[read], sem.at[read]).wait()


def pick(ids, offsets, held):
    return call(
        pick_kernel,
        1,
        2,
        [IN_PLACE] * 4,
        whole((READS, MEM, MODEL)),
        array((READS, MEM, MODEL), LOW),
        [pltpu.SemaphoreType.DMA((READS,))],
        0,
        1 << 20,
        vmem=2,
    )(ids, offsets, *held)


def project_memory_kernel(ids, offsets, held_0, held_1, held_2, held_3, given, w_key, w_value, keys, values, *rest):
    rows, low, key_w, value_w, sem, w_sem = rest
    frame = ids[1]
    held = (held_0, held_1, held_2, held_3)
    loads = [
        pltpu.make_async_copy(w_key, key_w, w_sem.at[0]),
        pltpu.make_async_copy(w_value, value_w, w_sem.at[1]),
    ]
    for read in range(READS):
        source, live = source_of(offsets, frame, read)
        back_z, back_x, same = back_to(frame, source)
        mine = jnp.logical_and(live, same)
        for shift in range(4):

            @pl.when(jnp.logical_and(mine, back_x == shift))
            def _():
                pltpu.make_async_copy(held[shift].at[back_z], rows.at[read], sem.at[read]).start()

        @pl.when(jnp.logical_not(mine))
        def _():
            pltpu.make_async_copy(given.at[read], rows.at[read], sem.at[read]).start()

    for load in loads:
        load.start()
    for read in range(READS):
        pltpu.make_async_copy(given.at[read], rows.at[read], sem.at[read]).wait()
        low[read * MEM : (read + 1) * MEM, :] = normalize(rows[read])[0].astype(LOW)
    for load, weight, out in zip(loads, (key_w, value_w), (keys, values)):
        load.wait()
        for start in range(0, INNER, 256):
            cols = slice(start, start + 256)
            out[:, cols] = dot(low[...], weight[:, cols]).astype(LOW)


def project_memory(ids, offsets, held, given, w_key, w_value):
    return call(
        project_memory_kernel,
        1,
        2,
        [IN_PLACE] * 5 + [IN_HBM] * 2,
        [whole((READS * MEM, INNER))] * 2,
        [array((READS * MEM, INNER), LOW)] * 2,
        [
            pltpu.VMEM((READS, MEM, MODEL), LOW),
            pltpu.VMEM((READS * MEM, MODEL), LOW),
            pltpu.VMEM((MODEL, INNER), LOW),
            pltpu.VMEM((MODEL, INNER), LOW),
            pltpu.SemaphoreType.DMA((READS,)),
            pltpu.SemaphoreType.DMA((2,)),
        ],
        4 * READS * MEM * MODEL * INNER,
        6 << 20,
        vmem=10,
    )(ids, offsets, *held, given, w_key, w_value)


def shift_z(by):
    return [(f, (f + 8 * by) % 32) for f in range(32)]


def shift_x(by):
    return [(f, f // 8 * 8 + (f % 8 + 2 * by) % 8) for f in range(32)]


SWAP_CORE = [(f, f ^ 1) for f in range(32)]


def shift_cam(by):
    return [(s, (s + by) % 4) for s in range(4)]


def attention_kernel(ids, offsets, count, queries, grads, keys_own, values_own, keys_mem, values_mem, *rest):
    far_in, rest = rest[:3], rest[3:]
    mixed, grad_query, grad_keys, grad_values, grad_mem, grad_mem_low = rest[:6]
    far_out, rest = rest[6:9], rest[9:]
    keys, values, keys_t, values_t, scores, grad_w, weights, grad_s, two_q, two_g, rest_k, rest_v = rest
    camera, frame = ids[0], ids[1]

    slot_live, slot_at, live_total = [], [], 0
    for slot in range(SLOTS):
        sender = lax.rem(camera + 4 - (slot // 2 + 1), 4)
        live = count[sender, camera] > slot % 2
        slot_live.append(jnp.logical_and(live, live_total < LIVE_MAX))
        slot_at.append(jnp.minimum(live_total, LIVE_MAX - 1))
        live_total = live_total + live.astype(jnp.int32)

    keys[0:ROWS, :] = keys_own[...]
    values[0:ROWS, :] = values_own[...]
    keys[MEM_AT:FAR_AT, :] = keys_mem[...]
    values[MEM_AT:FAR_AT, :] = values_mem[...]
    for place in range(LIVE_MAX):

        @pl.when(live_total <= place)
        def _():
            at = slice(FAR_AT + place * STRIP, FAR_AT + (place + 1) * STRIP)
            keys[at, :] = jnp.zeros((STRIP, PAIR), LOW)
            values[at, :] = jnp.zeros((STRIP, PAIR), LOW)

    for slot in range(SLOTS):

        @pl.when(slot_live[slot])
        def _():
            at = pl.ds(pl.multiple_of(FAR_AT + slot_at[slot] * STRIP, STRIP), STRIP)
            keys[at, :] = far_in[slot // 2][0, slot % 2]
            values[at, :] = far_in[slot // 2][1, slot % 2]

    keys_t[...] = keys[...].T
    values_t[...] = values[...].T
    lane = lax.broadcasted_iota(jnp.int32, (ROWS, PAIR), 1)
    for head in range(2):
        keep = (lane >= 64) if head else (lane < 64)
        at = slice(head * ROWS, (head + 1) * ROWS)
        two_q[at, :] = jnp.where(keep, queries[...], jnp.zeros((ROWS, PAIR), LOW))
        two_g[at, :] = jnp.where(keep, grads[...], jnp.zeros((ROWS, PAIR), LOW))

    pieces = [(0, ROWS, None)]
    for read in range(READS):
        start = MEM_AT + read * MEM
        pieces.append((start, start + MEM, offsets[read, frame] <= frame))
    for place in range(LIVE_MAX):
        start = FAR_AT + place * STRIP
        pieces.append((start, start + STRIP, place < live_total))

    def pieces_of(base):
        for start, end, live in pieces:
            low, high = max(start, base), min(end, base + CHUNK)
            if low < high:
                yield low, high, live

    def folded(block):
        return block.reshape(block.shape[0] // 8, 8, ROWS)

    bases = range(0, KEYS, CHUNK)
    highest = [jnp.full((8, ROWS), MASKED, WIDE)] * 2
    total, inner = [jnp.zeros((8, ROWS), WIDE)] * 2, [jnp.zeros((8, ROWS), WIDE)] * 2
    share = [None, None]

    def score(head, base):
        cols = slice(head * ROWS, (head + 1) * ROWS)
        block = dot_t(keys[base : base + CHUNK, :], two_q[cols, :])
        scores[head, base : base + CHUNK, :] = block
        for low, high, live in pieces_of(base):
            top = jnp.max(folded(block[low - base : high - base]), axis=0)
            top = jnp.maximum(highest[head], top)
            highest[head] = top if live is None else jnp.where(live, top, highest[head])
        if base == bases[-1]:
            highest[head] = jnp.max(highest[head], axis=0, keepdims=True)

    def lift(head, base):
        cols = slice(head * ROWS, (head + 1) * ROWS)
        block = dot_t(values[base : base + CHUNK, :], two_g[cols, :])
        grad_w[head, base : base + CHUNK, :] = block
        for low, high, live in pieces_of(base):
            top = highest[head] if live is None else jnp.where(live, highest[head], -MASKED)
            lifted = jnp.exp(scores[head, low:high, :] - top)
            scores[head, low:high, :] = lifted
            total[head] = total[head] + jnp.sum(folded(lifted), axis=0)
            inner[head] = inner[head] + jnp.sum(folded(lifted * block[low - base : high - base]), axis=0)
        if base == bases[-1]:
            share[head] = 1.0 / jnp.sum(total[head], axis=0, keepdims=True)
            inner[head] = jnp.sum(inner[head], axis=0, keepdims=True) * share[head]

    def settle(head, base):
        cols, at = slice(head * ROWS, (head + 1) * ROWS), slice(base, base + CHUNK)
        part = scores[head, at, :] * share[head]
        weights[at, cols] = part.astype(LOW)
        grad_s[at, cols] = (part * (grad_w[head, at, :] - inner[head])).astype(LOW)

    def row_grads(head, base):
        cols, at = slice(head * ROWS, (head + 1) * ROWS), slice(base, base + CHUNK)
        for_value = dot(weights[at, cols], two_g[cols, :])
        for_key = dot(grad_s[at, cols], two_q[cols, :])
        for made, own, far in ((for_key, grad_keys, rest_k), (for_value, grad_values, rest_v)):
            for start, end, ref, shift in ((0, ROWS, own, 0), (ROWS, KEYS, far, ROWS)):
                first, last = max(start, base), min(end, base + CHUNK)
                if first < last:
                    there = slice(first - shift, last - shift)
                    block = made[first - base : last - base]
                    ref[there, :] = block if head == 0 else ref[there, :] + block

    mixed_t, grad_query_t = [None, None], [None, None]

    def query_side(head):
        cols, dims = slice(head * ROWS, (head + 1) * ROWS), slice(head * 64, (head + 1) * 64)
        mixed_t[head] = dot(values_t[dims, :], weights[:, cols])
        grad_query_t[head] = dot(keys_t[dims, :], grad_s[:, cols])

    for base in bases:
        score(0, base)
    for base in bases:
        lift(0, base)
        score(1, base)
    for base in bases:
        settle(0, base)
        lift(1, base)
    for base in bases:
        row_grads(0, base)
        settle(1, base)
    query_side(0)
    for base in bases:
        row_grads(1, base)
    query_side(1)
    mixed[...] = jnp.concatenate(mixed_t, axis=0).T.astype(LOW)
    grad_query[...] = (jnp.concatenate(grad_query_t, axis=0).T * 0.125).astype(LOW)

    grad_mem[0] = rest_k[0 : READS * MEM, :]
    grad_mem[1] = rest_v[0 : READS * MEM, :]
    grad_mem_low[0] = rest_k[0 : READS * MEM, :].astype(LOW)
    grad_mem_low[1] = rest_v[0 : READS * MEM, :].astype(LOW)
    for slot in range(SLOTS):

        @pl.when(slot_live[slot])
        def _():
            start = FAR_AT - ROWS + slot_at[slot] * STRIP
            at = pl.ds(pl.multiple_of(start, STRIP), STRIP)
            far_out[slot // 2][0, slot % 2] = rest_k[at, :].astype(LOW)
            far_out[slot // 2][1, slot % 2] = rest_v[at, :].astype(LOW)


def attention(group, ids, offsets, count, queries, grads, keys_own, values_own, keys_mem, values_mem, far):
    first, pairs = group
    width = pairs * PAIR

    def taken(rows):
        return pl.BlockSpec((rows, PAIR), lambda p, *_: (0, first + p))

    def made(rows):
        return pl.BlockSpec((rows, PAIR), lambda p, *_: (0, p))

    far_in = pl.BlockSpec((2, 2, STRIP, PAIR), lambda p, *_: (0, 0, 0, first + p))
    far_out = pl.BlockSpec((2, 2, STRIP, PAIR), lambda p, *_: (0, 0, 0, p))
    mem_out = pl.BlockSpec((2, READS * MEM, PAIR), lambda p, *_: (0, 0, p))
    return call(
        attention_kernel,
        pairs,
        3,
        [taken(ROWS)] * 4 + [taken(READS * MEM)] * 2 + [far_in] * 3,
        [made(ROWS)] * 4 + [mem_out] * 2 + [far_out] * 3,
        [array((ROWS, width), LOW)] * 2
        + [array((ROWS, width), WIDE)] * 2
        + [array((2, READS * MEM, width), WIDE), array((2, READS * MEM, width), LOW)]
        + [array((2, 2, STRIP, width), LOW)] * 3,
        [pltpu.VMEM((KEYS, PAIR), LOW)] * 2
        + [pltpu.VMEM((PAIR, KEYS), LOW)] * 2
        + [pltpu.VMEM((2, KEYS, ROWS), WIDE)] * 2
        + [pltpu.VMEM((KEYS, 2 * ROWS), LOW)] * 2
        + [pltpu.VMEM((2 * ROWS, PAIR), LOW)] * 2
        + [pltpu.VMEM((KEYS - ROWS, PAIR), WIDE)] * 2,
        pairs * 12 * KEYS * 2 * ROWS * 256,
        pairs * (3 << 20),
    )(ids, offsets, count, queries, grads, keys_own, values_own, keys_mem, values_mem, *far)


def sort_kernel(ids, offsets, own, given, out_0, out_1, out_2, out_3, total):
    outs = (out_0, out_1, out_2, out_3)
    frame = ids[1]
    z_here, x_here, core_here = parts_of(frame)
    partner = frame + 1 - 2 * core_here
    total[...] = jnp.zeros_like(total)
    for reader, part in ((frame, own), (partner, given)):
        for read in range(READS):
            source, live = source_of(offsets, reader, read)
            z_at, x_at, core_at = parts_of(source)
            to = lax.rem(x_at - x_here + 4, 4) * 4 + lax.rem(z_at - z_here + 4, 4)

            @pl.when(jnp.logical_and(live, core_at == core_here))
            def _():
                for kind in range(2):
                    added = part[kind, read * MEM : (read + 1) * MEM, :].astype(WIDE)
                    total[to, kind] = total[to, kind] + added

    for shift in range(4):
        outs[shift][...] = total[4 * shift : 4 * shift + 4].astype(LOW)


def sort_reads(ids, offsets, own, given):
    width = own.shape[2]
    shape = (4, 2, MEM, width)
    return call(
        sort_kernel,
        1,
        2,
        [whole(own.shape)] * 2,
        [whole(shape)] * 4,
        [array(shape, LOW)] * 4,
        [pltpu.VMEM((16, 2, MEM, width), WIDE)],
        0,
        2 << 20,
        vmem=12,
    )(ids, offsets, own, given)


def add_kernel(*refs):
    for group, (first, pairs) in enumerate(GROUPS):
        parts, cols = refs[4 * group : 4 * group + 4], slice(first * PAIR, (first + pairs) * PAIR)
        for shift in range(4):
            total = parts[0][shift].astype(WIDE) + parts[1][shift].astype(WIDE)
            total = total + parts[2][shift].astype(WIDE) + parts[3][shift].astype(WIDE)
            refs[4 * len(GROUPS) + shift][:, :, cols] = total.astype(LOW)


def add_reads(parts):
    return call(
        add_kernel,
        1,
        0,
        [whole(part.shape) for part in parts],
        [whole((2, MEM, INNER))] * 4,
        [array((2, MEM, INNER), LOW)] * 4,
        [],
        0,
        2 << 20,
        vmem=8,
    )(*parts)


def outward_kernel(*refs):
    count = len(GROUPS)
    mixed, grad_query = refs[:count], refs[count : 2 * count]
    w_out, w_query, update, grad_normed = refs[2 * count :]
    total, part = 0.0, 0.0
    for (first, pairs), mixed_ref, grad_ref in zip(GROUPS, mixed, grad_query):
        cols = slice(first * PAIR, (first + pairs) * PAIR)
        total = total + dot(mixed_ref[...], w_out[cols, :])
        part = part + dot_t(grad_ref[...], w_query[:, cols])
    update[...] = total.astype(LOW)
    grad_normed[...] = part


def outward(mixed, grad_query, w_out, w_query):
    width = 512
    out = pl.BlockSpec((ROWS, width), lambda j: (0, j))
    parts = [whole((ROWS, pairs * PAIR)) for _, pairs in GROUPS]
    return call(
        outward_kernel,
        MODEL // width,
        0,
        parts
        + parts
        + [
            pl.BlockSpec((INNER, width), lambda j: (0, j)),
            pl.BlockSpec((width, INNER), lambda j: (j, 0)),
        ],
        [out, out],
        [array((ROWS, MODEL), LOW), array((ROWS, MODEL), WIDE)],
        [],
        4 * ROWS * MODEL * INNER,
        11 << 20,
    )(*mixed, *grad_query, w_out, w_query)


def token_grads_kernel(ids, count, index, *refs):
    groups = len(GROUPS)
    own = (refs[:groups], refs[groups : 2 * groups])
    back, refs = refs[2 * groups : 5 * groups], refs[5 * groups :]
    kept, (tokens, grad_part, w_key, w_value, grad_tokens), refs = refs[:4], refs[4:9], refs[9:]
    total, far, near, rows, grad_normed, key_w, value_w, low, made = refs[:9]
    own_sem, far_sem, near_sem, in_sem, out_sem = refs[9:]
    camera = ids[0]

    near_loads = [pltpu.make_async_copy(kept[k], near.at[k], near_sem.at[k]) for k in range(4)]
    own_loads, far_loads = [], []
    for group, (first, pairs) in enumerate(GROUPS):
        cols = pl.ds(first * PAIR, pairs * PAIR)
        for kind in range(2):
            own_loads.append(
                pltpu.make_async_copy(
                    own[kind][group], total.at[kind, :, cols], own_sem.at[2 * group + kind]
                )
            )
        for k in range(3):
            far_loads.append(
                pltpu.make_async_copy(
                    back[3 * group + k], far.at[k, :, :, :, cols], far_sem.at[3 * group + k]
                )
            )
    pairs_of_refs = ((w_key, key_w), (w_value, value_w), (grad_part, grad_normed), (tokens, rows))
    loads = [
        pltpu.make_async_copy(source, target, in_sem.at[k])
        for k, (source, target) in enumerate(pairs_of_refs)
    ]
    for load in own_loads + far_loads + near_loads + loads:
        load.start()
    for load in own_loads + far_loads:
        load.wait()
    for shift in (1, 2, 3):
        other = lax.rem(camera + shift, 4)
        for slot in range(2):

            @pl.when(slot < count[camera, other])
            def _():
                start = index[camera, slot, other] * STRIP
                at = pl.ds(pl.multiple_of(start, STRIP), STRIP)
                for kind in range(2):
                    total[kind, at, :] = total[kind, at, :] + far[shift - 1, kind, slot].astype(WIDE)

    for load in near_loads:
        load.wait()
    half = ROWS // 2
    row = lax.broadcasted_iota(jnp.int32, (half, 4 * MEM), 0)
    col = lax.broadcasted_iota(jnp.int32, (half, 4 * MEM), 1)
    stacked = [jnp.concatenate([near[k, kind] for k in range(4)], axis=0) for kind in range(2)]
    for load in loads:
        load.wait()
    stores = []
    for start in range(0, ROWS, half):
        at = slice(start, start + half)
        hit = row + start == (col % MEM) * (ROWS // MEM)
        spread = jnp.where(hit, 1.0, 0.0).astype(LOW)
        for kind in range(2):
            low[kind, at, :] = (total[kind, at, :] + dot(spread, stacked[kind])).astype(LOW)
        for first in range(0, MODEL, 512):
            cols = slice(first, first + 512)
            grad_normed[at, cols] = (
                grad_normed[at, cols]
                + dot_t(low[0, at, :], key_w[cols, :])
                + dot_t(low[1, at, :], value_w[cols, :])
            )
        for begin in range(start, start + half, 64):
            at = slice(begin, begin + 64)
            normed, inverse = normalize(rows[at, :])
            grad = grad_normed[at, :]
            first_mean = jnp.mean(grad, axis=-1, keepdims=True)
            second_mean = jnp.mean(grad * normed, axis=-1, keepdims=True)
            made[at, :] = (inverse * (grad - first_mean - normed * second_mean)).astype(LOW)
        block = pl.ds(start, half)
        stores.append(
            pltpu.make_async_copy(made.at[block], grad_tokens.at[block], out_sem.at[start // half])
        )
        stores[-1].start()
    for store in stores:
        store.wait()


def token_grads(ids, count, index, own_keys, own_values, back, kept, tokens, grad_part, w_key, w_value):
    groups = len(GROUPS)
    return call(
        token_grads_kernel,
        1,
        3,
        [IN_PLACE] * (5 * groups + 8),
        IN_PLACE,
        array((ROWS, MODEL), LOW),
        [
            pltpu.VMEM((2, ROWS, INNER), WIDE),
            pltpu.VMEM((3, 2, 2, STRIP, INNER), LOW),
            pltpu.VMEM((4, 2, MEM, INNER), LOW),
            pltpu.VMEM((ROWS, MODEL), LOW),
            pltpu.VMEM((ROWS, MODEL), WIDE),
            pltpu.VMEM((MODEL, INNER), LOW),
            pltpu.VMEM((MODEL, INNER), LOW),
            pltpu.VMEM((2, ROWS, INNER), LOW),
            pltpu.VMEM((ROWS, MODEL), LOW),
            pltpu.SemaphoreType.DMA((2 * groups,)),
            pltpu.SemaphoreType.DMA((3 * groups,)),
            pltpu.SemaphoreType.DMA((4,)),
            pltpu.SemaphoreType.DMA((4,)),
            pltpu.SemaphoreType.DMA((2,)),
        ],
        4 * ROWS * MODEL * INNER,
        16 << 20,
        vmem=26,
    )(ids, count, index, *own_keys, *own_values, *back, *kept, tokens, grad_part, w_key, w_value)


def send(value, axis, pairs):
    return lax.ppermute(value, axis, pairs)


def local(tokens, w_query, w_key, w_value, w_out, grad_update, offsets, count, index):
    tokens = tokens.reshape(ROWS, MODEL)
    grad_update = grad_update.reshape(ROWS, MODEL)
    ids = jnp.stack([lax.axis_index("cam"), lax.axis_index("tm")]).astype(jnp.int32)
    index, offsets = jnp.transpose(index, (0, 2, 1)), offsets.T
    others = (1, 2, 3)

    low, keys, values, *sends = project_keys(ids, index, tokens, w_key, w_value)
    far = [send(sends[k - 1], "cam", shift_cam(k)) for k in others]
    kept = tokens.reshape(MEM, ROWS // MEM, MODEL)[:, 0]
    along_z = jnp.stack([kept] + [send(kept, "tm", shift_z(k)) for k in others])
    held = [along_z] + [send(along_z, "tm", shift_x(k)) for k in others]
    queries, grads = project_queries(low, grad_update, w_query, w_out)
    given = send(pick(ids, offsets, held), "tm", SWAP_CORE)
    keys_mem, values_mem = project_memory(ids, offsets, held, given, w_key, w_value)

    made, back, parts = [], [], []
    for group in GROUPS:
        args = (queries, grads, keys, values, keys_mem, values_mem, far)
        made.append(attention(group, ids, offsets, count, *args))
        back += [send(made[-1][5 + k], "cam", shift_cam(-k)) for k in others]
        mem_given = send(made[-1][5], "tm", SWAP_CORE)
        to_x = sort_reads(ids, offsets, made[-1][4], mem_given)
        parts += [to_x[0]] + [send(to_x[k], "tm", shift_x(k)) for k in others]
    mixed, grad_query, own_keys, own_values = [[m[k] for m in made] for k in range(4)]

    update, grad_part = outward(mixed, grad_query, w_out, w_query)
    sorted_z = add_reads(parts)
    kept_grads = [sorted_z[0]] + [send(sorted_z[k], "tm", shift_z(k)) for k in others]
    args = (own_keys, own_values, back, kept_grads, tokens, grad_part, w_key, w_value)
    grad_tokens = token_grads(ids, count, index, *args)
    shape = (1, 1, ROWS, MODEL)
    return update.reshape(shape), grad_tokens.reshape(shape)


def solution(mesh):
    frames = P("cam", "tm", None, None)
    return jax.shard_map(
        local,
        mesh=mesh,
        in_specs=(frames, P(), P(), P(), P(), frames, P(), P(), P()),
        out_specs=(frames, frames),
        check_vma=False,
    )
```

```python
import jax
import jax.numpy as jnp
from jax import lax
from jax.experimental import pallas as pl
from jax.experimental.pallas import tpu as pltpu
from jax.sharding import PartitionSpec as P


LOW = jnp.bfloat16
WIDE = jnp.float32
ROWS = 512
MODEL = 1536
INNER = 768
STRIP = 128
MEM = 32
READS = 4
SLOTS = 6
LIVE_MAX = 4
MEM_AT = ROWS
FAR_AT = ROWS + READS * MEM
KEYS = FAR_AT + LIVE_MAX * STRIP
PAIR = 128
CHUNK = 384
EPS = 1e-05
MASKED = -1e30
NT = (((1,), (1,)), ((), ()))
GROUPS = ((0, 5), (5, 1))


def dot(left, right):
    return jnp.dot(left, right, preferred_element_type=WIDE)


def dot_t(left, right):
    return lax.dot_general(left, right, NT, preferred_element_type=WIDE)


def whole(shape):
    return pl.BlockSpec(shape, lambda *_: (0,) * len(shape))


def call(kernel, grid, scalars, in_specs, out_specs, out_shape, scratch, flops, moved, vmem=24):
    return pl.pallas_call(
        kernel,
        grid_spec=pltpu.PrefetchScalarGridSpec(
            num_scalar_prefetch=scalars,
            grid=(grid,),
            in_specs=in_specs,
            out_specs=out_specs,
            scratch_shapes=scratch,
        ),
        out_shape=out_shape,
        compiler_params=pltpu.CompilerParams(
            dimension_semantics=("arbitrary",), vmem_limit_bytes=vmem << 20
        ),
        cost_estimate=pl.CostEstimate(flops=flops, bytes_accessed=moved, transcendentals=0),
    )


IN_PLACE = pl.BlockSpec(memory_space=pl.ANY)
IN_HBM = pl.BlockSpec(memory_space=pltpu.HBM)


def array(shape, dtype):
    return jax.ShapeDtypeStruct(shape, dtype)


def normalize(rows):
    widened = rows.astype(WIDE)
    average = jnp.mean(widened, axis=-1, keepdims=True)
    centred = widened - average
    spread = jnp.mean(centred * centred, axis=-1, keepdims=True)
    inverse = lax.rsqrt(spread + EPS)
    return centred * inverse, inverse


def project_keys_kernel(ids, index, tokens, w_key, w_value, low, keys, values, kept, *rest):
    sends, (rows, key_w, value_w, normed_low, made, in_sem, out_sem, send_sem) = rest[:3], rest[3:]
    camera = ids[0]
    loads = []
    for step, start in enumerate(range(0, ROWS, STRIP)):
        at = pl.ds(start, STRIP)
        loads.append(pltpu.make_async_copy(tokens.at[at], rows.at[at], in_sem.at[step]))
    loads.append(pltpu.make_async_copy(w_key, key_w, in_sem.at[4]))
    loads.append(pltpu.make_async_copy(w_value, value_w, in_sem.at[5]))
    for load in loads:
        load.start()

    def norm(first, last):
        for start in range(first, last, 64):
            at = slice(start, start + 64)
            normed_low[at, :] = normalize(rows[at, :])[0].astype(LOW)

    def product(kind, weight, first, last):
        for start in range(0, INNER, 256):
            cols = slice(start, start + 256)
            made[kind, first:last, cols] = dot(normed_low[first:last, :], weight[:, cols]).astype(LOW)

    stores = []

    def store(source, target, sem):
        stores.append(pltpu.make_async_copy(source, target, sem))
        stores[-1].start()

    def publish(kind, out):
        for shift in (1, 2, 3):
            for slot in range(2):
                strip = index[camera, slot, lax.rem(camera + shift, 4)]
                at = pl.ds(pl.multiple_of(strip * STRIP, STRIP), STRIP)
                sem = send_sem.at[kind * SLOTS + 2 * (shift - 1) + slot]
                store(made.at[kind, at], sends[shift - 1].at[kind, slot], sem)
        store(made.at[kind], out, out_sem.at[1 + kind])
        row = lax.broadcasted_iota(jnp.int32, (MEM, ROWS), 1)
        hit = row == lax.broadcasted_iota(jnp.int32, (MEM, ROWS), 0) * (ROWS // MEM)
        choice = jnp.where(hit, 1.0, 0.0).astype(LOW)
        kept[:, kind * INNER : (kind + 1) * INNER] = dot(choice, made[kind]).astype(LOW)

    half = ROWS // 2
    loads[0].wait()
    loads[1].wait()
    norm(0, half)
    for load in loads[2:5]:
        load.wait()
    product(0, key_w, 0, half)
    norm(half, ROWS)
    store(normed_low, low, out_sem.at[0])
    product(0, key_w, half, ROWS)
    publish(0, keys)
    loads[5].wait()
    product(1, value_w, 0, ROWS)
    publish(1, values)
    for copy in stores:
        copy.wait()


def project_keys(ids, index, tokens, w_key, w_value):
    return call(
        project_keys_kernel,
        1,
        2,
        [IN_HBM] * 3,
        [IN_PLACE] * 3 + [whole((MEM, 2 * INNER))] + [IN_PLACE] * 3,
        [array((ROWS, MODEL), LOW), array((ROWS, INNER), LOW), array((ROWS, INNER), LOW)]
        + [array((MEM, 2 * INNER), LOW)]
        + [array((2, 2, STRIP, INNER), LOW)] * 3,
        [
            pltpu.VMEM((ROWS, MODEL), LOW),
            pltpu.VMEM((MODEL, INNER), LOW),
            pltpu.VMEM((MODEL, INNER), LOW),
            pltpu.VMEM((ROWS, MODEL), LOW),
            pltpu.VMEM((2, ROWS, INNER), LOW),
            pltpu.SemaphoreType.DMA((6,)),
            pltpu.SemaphoreType.DMA((3,)),
            pltpu.SemaphoreType.DMA((2 * SLOTS,)),
        ],
        4 * ROWS * MODEL * INNER,
        12 << 20,
        vmem=60,
    )(ids, index, tokens, w_key, w_value)


def project_queries_kernel(low, grad_update, w_query, w_out, queries, grad_mixed):
    product = dot(low[...], w_query[...]).astype(LOW)
    queries[...] = product * jnp.asarray(0.125, LOW)
    grad_mixed[...] = dot_t(grad_update[...], w_out[...]).astype(LOW)


def project_queries(low, grad_update, w_query, w_out):
    width = 384
    out = pl.BlockSpec((ROWS, width), lambda j: (0, j))
    return call(
        project_queries_kernel,
        INNER // width,
        0,
        [
            whole((ROWS, MODEL)),
            whole((ROWS, MODEL)),
            pl.BlockSpec((MODEL, width), lambda j: (0, j)),
            pl.BlockSpec((width, MODEL), lambda j: (j, 0)),
        ],
        [out, out],
        [array((ROWS, INNER), LOW)] * 2,
        [],
        4 * ROWS * MODEL * INNER,
        10 << 20,
    )(low, grad_update, w_query, w_out)


def parts_of(frame):
    return frame // 8, lax.rem(frame // 2, 4), lax.rem(frame, 2)


def source_of(offsets, frame, read):
    source = frame - offsets[read, frame]
    return jnp.maximum(source, 0), source >= 0


def back_to(frame, source):
    z_here, x_here, core_here = parts_of(frame)
    z_at, x_at, core_at = parts_of(source)
    return lax.rem(z_here - z_at + 4, 4), lax.rem(x_here - x_at + 4, 4), core_at == core_here


def pick_kernel(ids, offsets, held_0, held_1, held_2, held_3, picked, sem):
    frame = ids[1]
    partner = frame + 1 - 2 * lax.rem(frame, 2)
    held = (held_0, held_1, held_2, held_3)
    wanted = []
    for read in range(READS):
        source, live = source_of(offsets, partner, read)
        back_z, back_x, same = back_to(frame, source)
        wanted.append(jnp.logical_and(live, same))
        for shift in range(4):

            @pl.when(jnp.logical_and(wanted[read], back_x == shift))
            def _():
                pltpu.make_async_copy(held[shift].at[back_z], picked.at[read], sem.at[read]).start()

        @pl.when(jnp.logical_not(wanted[read]))
        def _():
            picked[read] = jnp.zeros((MEM, 2 * INNER), LOW)

    for read in range(READS):

        @pl.when(wanted[read])
        def _():
            pltpu.make_async_copy(held_0.at[0], picked.at[read], sem.at[read]).wait()


def pick(ids, offsets, held):
    return call(
        pick_kernel,
        1,
        2,
        [IN_PLACE] * 4,
        whole((READS, MEM, 2 * INNER)),
        array((READS, MEM, 2 * INNER), LOW),
        [pltpu.SemaphoreType.DMA((READS,))],
        0,
        1 << 20,
        vmem=2,
    )(ids, offsets, *held)


def shift_z(by):
    return [(f, (f + 8 * by) % 32) for f in range(32)]


def shift_x(by):
    return [(f, f // 8 * 8 + (f % 8 + 2 * by) % 8) for f in range(32)]


SWAP_CORE = [(f, f ^ 1) for f in range(32)]


def shift_cam(by):
    return [(s, (s + by) % 4) for s in range(4)]


def attention_kernel(ids, offsets, count, queries, grads, keys_own, values_own, *rest):
    mem_in, far_in, rest = (rest[:5], rest[5:10]), rest[10:13], rest[13:]
    mixed, grad_query, grad_keys, grad_values, grad_mem, grad_mem_low = rest[:6]
    far_out, rest = rest[6:9], rest[9:]
    keys, values, keys_t, values_t, scores, grad_w, weights, grad_s, two_q, two_g, rest_k, rest_v = rest
    camera, frame = ids[0], ids[1]

    slot_live, slot_at, live_total = [], [], 0
    for slot in range(SLOTS):
        sender = lax.rem(camera + 4 - (slot // 2 + 1), 4)
        live = count[sender, camera] > slot % 2
        slot_live.append(jnp.logical_and(live, live_total < LIVE_MAX))
        slot_at.append(jnp.minimum(live_total, LIVE_MAX - 1))
        live_total = live_total + live.astype(jnp.int32)

    keys[0:ROWS, :] = keys_own[...]
    values[0:ROWS, :] = values_own[...]
    for read in range(READS):
        source, live = source_of(offsets, frame, read)
        back_z, back_x, same = back_to(frame, source)
        mine = jnp.logical_and(live, same)
        at = slice(MEM_AT + read * MEM, MEM_AT + (read + 1) * MEM)
        for shift in range(4):

            @pl.when(jnp.logical_and(mine, back_x == shift))
            def _():
                keys[at, :] = mem_in[0][shift][back_z]
                values[at, :] = mem_in[1][shift][back_z]

        @pl.when(jnp.logical_not(mine))
        def _():
            keys[at, :] = mem_in[0][4][read]
            values[at, :] = mem_in[1][4][read]

    for place in range(LIVE_MAX):

        @pl.when(live_total <= place)
        def _():
            at = slice(FAR_AT + place * STRIP, FAR_AT + (place + 1) * STRIP)
            keys[at, :] = jnp.zeros((STRIP, PAIR), LOW)
            values[at, :] = jnp.zeros((STRIP, PAIR), LOW)

    for slot in range(SLOTS):

        @pl.when(slot_live[slot])
        def _():
            at = pl.ds(pl.multiple_of(FAR_AT + slot_at[slot] * STRIP, STRIP), STRIP)
            keys[at, :] = far_in[slot // 2][0, slot % 2]
            values[at, :] = far_in[slot // 2][1, slot % 2]

    keys_t[...] = keys[...].T
    values_t[...] = values[...].T
    lane = lax.broadcasted_iota(jnp.int32, (ROWS, PAIR), 1)
    for head in range(2):
        keep = (lane >= 64) if head else (lane < 64)
        at = slice(head * ROWS, (head + 1) * ROWS)
        two_q[at, :] = jnp.where(keep, queries[...], jnp.zeros((ROWS, PAIR), LOW))
        two_g[at, :] = jnp.where(keep, grads[...], jnp.zeros((ROWS, PAIR), LOW))

    pieces = [(0, ROWS, None)]
    for read in range(READS):
        start = MEM_AT + read * MEM
        pieces.append((start, start + MEM, offsets[read, frame] <= frame))
    for place in range(LIVE_MAX):
        start = FAR_AT + place * STRIP
        pieces.append((start, start + STRIP, place < live_total))

    def pieces_of(base):
        for start, end, live in pieces:
            low, high = max(start, base), min(end, base + CHUNK)
            if low < high:
                yield low, high, live

    def folded(block):
        return block.reshape(block.shape[0] // 8, 8, ROWS)

    bases = range(0, KEYS, CHUNK)
    highest = [jnp.full((8, ROWS), MASKED, WIDE)] * 2
    total, inner = [jnp.zeros((8, ROWS), WIDE)] * 2, [jnp.zeros((8, ROWS), WIDE)] * 2
    share = [None, None]

    def score(head, base):
        cols = slice(head * ROWS, (head + 1) * ROWS)
        block = dot_t(keys[base : base + CHUNK, :], two_q[cols, :])
        scores[head, base : base + CHUNK, :] = block
        for low, high, live in pieces_of(base):
            top = jnp.max(folded(block[low - base : high - base]), axis=0)
            top = jnp.maximum(highest[head], top)
            highest[head] = top if live is None else jnp.where(live, top, highest[head])
        if base == bases[-1]:
            highest[head] = jnp.max(highest[head], axis=0, keepdims=True)

    def lift(head, base):
        cols = slice(head * ROWS, (head + 1) * ROWS)
        block = dot_t(values[base : base + CHUNK, :], two_g[cols, :])
        grad_w[head, base : base + CHUNK, :] = block
        for low, high, live in pieces_of(base):
            top = highest[head] if live is None else jnp.where(live, highest[head], -MASKED)
            lifted = jnp.exp(scores[head, low:high, :] - top)
            scores[head, low:high, :] = lifted
            total[head] = total[head] + jnp.sum(folded(lifted), axis=0)
            inner[head] = inner[head] + jnp.sum(folded(lifted * block[low - base : high - base]), axis=0)
        if base == bases[-1]:
            share[head] = 1.0 / jnp.sum(total[head], axis=0, keepdims=True)
            inner[head] = jnp.sum(inner[head], axis=0, keepdims=True) * share[head]

    def settle(head, base):
        cols, at = slice(head * ROWS, (head + 1) * ROWS), slice(base, base + CHUNK)
        part = scores[head, at, :] * share[head]
        weights[at, cols] = part.astype(LOW)
        grad_s[at, cols] = (part * (grad_w[head, at, :] - inner[head])).astype(LOW)

    def row_grads(head, base):
        cols, at = slice(head * ROWS, (head + 1) * ROWS), slice(base, base + CHUNK)
        for_value = dot(weights[at, cols], two_g[cols, :])
        for_key = dot(grad_s[at, cols], two_q[cols, :])
        for made, own, far in ((for_key, grad_keys, rest_k), (for_value, grad_values, rest_v)):
            for start, end, ref, shift in ((0, ROWS, own, 0), (ROWS, KEYS, far, ROWS)):
                first, last = max(start, base), min(end, base + CHUNK)
                if first < last:
                    there = slice(first - shift, last - shift)
                    block = made[first - base : last - base]
                    ref[there, :] = block if head == 0 else ref[there, :] + block

    mixed_t, grad_query_t = [None, None], [None, None]

    def query_side(head):
        cols, dims = slice(head * ROWS, (head + 1) * ROWS), slice(head * 64, (head + 1) * 64)
        mixed_t[head] = dot(values_t[dims, :], weights[:, cols])
        grad_query_t[head] = dot(keys_t[dims, :], grad_s[:, cols])

    for base in bases:
        score(0, base)
    for base in bases:
        lift(0, base)
        score(1, base)
    for base in bases:
        settle(0, base)
        lift(1, base)
    for base in bases:
        row_grads(0, base)
        settle(1, base)
    query_side(0)
    for base in bases:
        row_grads(1, base)
    query_side(1)
    mixed[...] = jnp.concatenate(mixed_t, axis=0).T.astype(LOW)
    grad_query[...] = (jnp.concatenate(grad_query_t, axis=0).T * 0.125).astype(LOW)

    grad_mem[0] = rest_k[0 : READS * MEM, :]
    grad_mem[1] = rest_v[0 : READS * MEM, :]
    grad_mem_low[0] = rest_k[0 : READS * MEM, :].astype(LOW)
    grad_mem_low[1] = rest_v[0 : READS * MEM, :].astype(LOW)
    for slot in range(SLOTS):

        @pl.when(slot_live[slot])
        def _():
            start = FAR_AT - ROWS + slot_at[slot] * STRIP
            at = pl.ds(pl.multiple_of(start, STRIP), STRIP)
            far_out[slot // 2][0, slot % 2] = rest_k[at, :].astype(LOW)
            far_out[slot // 2][1, slot % 2] = rest_v[at, :].astype(LOW)


def attention(group, ids, offsets, count, queries, grads, keys_own, values_own, mem, far):
    first, pairs = group
    width = pairs * PAIR

    def taken(rows):
        return pl.BlockSpec((rows, PAIR), lambda p, *_: (0, first + p))

    def made(rows):
        return pl.BlockSpec((rows, PAIR), lambda p, *_: (0, p))

    far_in = pl.BlockSpec((2, 2, STRIP, PAIR), lambda p, *_: (0, 0, 0, first + p))
    far_out = pl.BlockSpec((2, 2, STRIP, PAIR), lambda p, *_: (0, 0, 0, p))
    mem_k = pl.BlockSpec((4, MEM, PAIR), lambda p, *_: (0, 0, first + p))
    mem_v = pl.BlockSpec((4, MEM, PAIR), lambda p, *_: (0, 0, INNER // PAIR + first + p))
    mem_out = pl.BlockSpec((2, READS * MEM, PAIR), lambda p, *_: (0, 0, p))
    return call(
        attention_kernel,
        pairs,
        3,
        [taken(ROWS)] * 4 + [mem_k] * 5 + [mem_v] * 5 + [far_in] * 3,
        [made(ROWS)] * 4 + [mem_out] * 2 + [far_out] * 3,
        [array((ROWS, width), LOW)] * 2
        + [array((ROWS, width), WIDE)] * 2
        + [array((2, READS * MEM, width), WIDE), array((2, READS * MEM, width), LOW)]
        + [array((2, 2, STRIP, width), LOW)] * 3,
        [pltpu.VMEM((KEYS, PAIR), LOW)] * 2
        + [pltpu.VMEM((PAIR, KEYS), LOW)] * 2
        + [pltpu.VMEM((2, KEYS, ROWS), WIDE)] * 2
        + [pltpu.VMEM((KEYS, 2 * ROWS), LOW)] * 2
        + [pltpu.VMEM((2 * ROWS, PAIR), LOW)] * 2
        + [pltpu.VMEM((KEYS - ROWS, PAIR), WIDE)] * 2,
        pairs * 12 * KEYS * 2 * ROWS * 256,
        pairs * (3 << 20),
    )(ids, offsets, count, queries, grads, keys_own, values_own, *mem, *mem, *far)


def sort_kernel(ids, offsets, own, given, out_0, out_1, out_2, out_3, total):
    outs = (out_0, out_1, out_2, out_3)
    frame = ids[1]
    z_here, x_here, core_here = parts_of(frame)
    partner = frame + 1 - 2 * core_here
    total[...] = jnp.zeros_like(total)
    for reader, part in ((frame, own), (partner, given)):
        for read in range(READS):
            source, live = source_of(offsets, reader, read)
            z_at, x_at, core_at = parts_of(source)
            to = lax.rem(x_at - x_here + 4, 4) * 4 + lax.rem(z_at - z_here + 4, 4)

            @pl.when(jnp.logical_and(live, core_at == core_here))
            def _():
                for kind in range(2):
                    added = part[kind, read * MEM : (read + 1) * MEM, :].astype(WIDE)
                    total[to, kind] = total[to, kind] + added

    for shift in range(4):
        outs[shift][...] = total[4 * shift : 4 * shift + 4].astype(LOW)


def sort_reads(ids, offsets, own, given):
    width = own.shape[2]
    shape = (4, 2, MEM, width)
    return call(
        sort_kernel,
        1,
        2,
        [whole(own.shape)] * 2,
        [whole(shape)] * 4,
        [array(shape, LOW)] * 4,
        [pltpu.VMEM((16, 2, MEM, width), WIDE)],
        0,
        2 << 20,
        vmem=12,
    )(ids, offsets, own, given)


def add_kernel(*refs):
    for group, (first, pairs) in enumerate(GROUPS):
        parts, cols = refs[4 * group : 4 * group + 4], slice(first * PAIR, (first + pairs) * PAIR)
        for shift in range(4):
            total = parts[0][shift].astype(WIDE) + parts[1][shift].astype(WIDE)
            total = total + parts[2][shift].astype(WIDE) + parts[3][shift].astype(WIDE)
            refs[4 * len(GROUPS) + shift][:, :, cols] = total.astype(LOW)


def add_reads(parts):
    return call(
        add_kernel,
        1,
        0,
        [whole(part.shape) for part in parts],
        [whole((2, MEM, INNER))] * 4,
        [array((2, MEM, INNER), LOW)] * 4,
        [],
        0,
        2 << 20,
        vmem=8,
    )(*parts)


def outward_kernel(*refs):
    count = len(GROUPS)
    mixed, grad_query = refs[:count], refs[count : 2 * count]
    w_out, w_query, update, grad_normed = refs[2 * count :]
    total, part = 0.0, 0.0
    for (first, pairs), mixed_ref, grad_ref in zip(GROUPS, mixed, grad_query):
        cols = slice(first * PAIR, (first + pairs) * PAIR)
        total = total + dot(mixed_ref[...], w_out[cols, :])
        part = part + dot_t(grad_ref[...], w_query[:, cols])
    update[...] = total.astype(LOW)
    grad_normed[...] = part


def outward(mixed, grad_query, w_out, w_query):
    width = 512
    out = pl.BlockSpec((ROWS, width), lambda j: (0, j))
    parts = [whole((ROWS, pairs * PAIR)) for _, pairs in GROUPS]
    return call(
        outward_kernel,
        MODEL // width,
        0,
        parts
        + parts
        + [
            pl.BlockSpec((INNER, width), lambda j: (0, j)),
            pl.BlockSpec((width, INNER), lambda j: (j, 0)),
        ],
        [out, out],
        [array((ROWS, MODEL), LOW), array((ROWS, MODEL), WIDE)],
        [],
        4 * ROWS * MODEL * INNER,
        11 << 20,
    )(*mixed, *grad_query, w_out, w_query)


def token_grads_kernel(ids, count, index, *refs):
    groups = len(GROUPS)
    own = (refs[:groups], refs[groups : 2 * groups])
    back, refs = refs[2 * groups : 5 * groups], refs[5 * groups :]
    kept, (tokens, grad_part, w_key, w_value, grad_tokens), refs = refs[:4], refs[4:9], refs[9:]
    total, grad_normed, low, made, out_sem = refs
    camera = ids[0]

    row = lax.broadcasted_iota(jnp.int32, (ROWS, 4 * MEM), 0)
    col = lax.broadcasted_iota(jnp.int32, (ROWS, 4 * MEM), 1)
    hit = row == (col % MEM) * (ROWS // MEM)
    spread = jnp.where(hit, 1.0, 0.0).astype(LOW)
    for kind in range(2):
        stacked = jnp.concatenate([part[kind] for part in kept], axis=0)
        for group, (first, pairs) in enumerate(GROUPS):
            cols = slice(first * PAIR, (first + pairs) * PAIR)
            total[kind, :, cols] = own[kind][group][...] + dot(spread, stacked[:, cols])
    for shift in (1, 2, 3):
        other = lax.rem(camera + shift, 4)
        for slot in range(2):

            @pl.when(slot < count[camera, other])
            def _():
                start = index[camera, slot, other] * STRIP
                at = pl.ds(pl.multiple_of(start, STRIP), STRIP)
                for kind in range(2):
                    for group, (first, pairs) in enumerate(GROUPS):
                        cols = slice(first * PAIR, (first + pairs) * PAIR)
                        given = back[3 * group + shift - 1][kind, slot]
                        total[kind, at, cols] = total[kind, at, cols] + given.astype(WIDE)

    half = ROWS // 2
    stores = []
    for start in range(0, ROWS, half):
        at = slice(start, start + half)
        for kind in range(2):
            low[kind, at, :] = total[kind, at, :].astype(LOW)
        for first in range(0, MODEL, 512):
            cols = slice(first, first + 512)
            grad_normed[at, cols] = (
                grad_part[at, cols]
                + dot_t(low[0, at, :], w_key[cols, :])
                + dot_t(low[1, at, :], w_value[cols, :])
            )
        for begin in range(start, start + half, 64):
            at = slice(begin, begin + 64)
            normed, inverse = normalize(tokens[at, :])
            grad = grad_normed[at, :]
            first_mean = jnp.mean(grad, axis=-1, keepdims=True)
            second_mean = jnp.mean(grad * normed, axis=-1, keepdims=True)
            made[at, :] = (inverse * (grad - first_mean - normed * second_mean)).astype(LOW)
        block = pl.ds(start, half)
        stores.append(
            pltpu.make_async_copy(made.at[block], grad_tokens.at[block], out_sem.at[start // half])
        )
        stores[-1].start()
    for store in stores:
        store.wait()


def token_grads(ids, count, index, own_keys, own_values, back, kept, tokens, grad_part, w_key, w_value):
    operands = (*own_keys, *own_values, *back, *kept, tokens, grad_part, w_key, w_value)
    return pl.pallas_call(
        token_grads_kernel,
        in_specs=[pl.BlockSpec(memory_space=pltpu.SMEM)] * 3
        + [pl.BlockSpec(memory_space=pltpu.VMEM)] * len(operands),
        out_specs=IN_PLACE,
        out_shape=array((ROWS, MODEL), LOW),
        scratch_shapes=[
            pltpu.VMEM((2, ROWS, INNER), WIDE),
            pltpu.VMEM((ROWS, MODEL), WIDE),
            pltpu.VMEM((2, ROWS, INNER), LOW),
            pltpu.VMEM((ROWS, MODEL), LOW),
            pltpu.SemaphoreType.DMA((2,)),
        ],
        compiler_params=pltpu.CompilerParams(vmem_limit_bytes=36 << 20),
        cost_estimate=pl.CostEstimate(
            flops=4 * ROWS * MODEL * INNER, bytes_accessed=16 << 20, transcendentals=0
        ),
        name="token_grads",
    )(ids, count, index, *operands)


def send(value, axis, pairs):
    return lax.ppermute(value, axis, pairs)


def local(tokens, w_query, w_key, w_value, w_out, grad_update, offsets, count, index):
    tokens = tokens.reshape(ROWS, MODEL)
    grad_update = grad_update.reshape(ROWS, MODEL)
    ids = jnp.stack([lax.axis_index("cam"), lax.axis_index("tm")]).astype(jnp.int32)
    index, offsets = jnp.transpose(index, (0, 2, 1)), offsets.T
    others = (1, 2, 3)

    low, keys, values, kept, *sends = project_keys(ids, index, tokens, w_key, w_value)
    far = [send(sends[k - 1], "cam", shift_cam(k)) for k in others]
    along_z = jnp.stack([kept] + [send(kept, "tm", shift_z(k)) for k in others])
    held = [along_z] + [send(along_z, "tm", shift_x(k)) for k in others]
    queries, grads = project_queries(low, grad_update, w_query, w_out)
    given = send(pick(ids, offsets, held), "tm", SWAP_CORE)
    made, back, parts = [], [], []
    for group in GROUPS:
        args = (queries, grads, keys, values, [*held, given], far)
        made.append(attention(group, ids, offsets, count, *args))
        back += [send(made[-1][5 + k], "cam", shift_cam(-k)) for k in others]
        mem_given = send(made[-1][5], "tm", SWAP_CORE)
        to_x = sort_reads(ids, offsets, made[-1][4], mem_given)
        parts += [to_x[0]] + [send(to_x[k], "tm", shift_x(k)) for k in others]
    mixed, grad_query, own_keys, own_values = [[m[k] for m in made] for k in range(4)]

    update, grad_part = outward(mixed, grad_query, w_out, w_query)
    sorted_z = add_reads(parts)
    kept_grads = [sorted_z[0]] + [send(sorted_z[k], "tm", shift_z(k)) for k in others]
    args = (own_keys, own_values, back, kept_grads, tokens, grad_part, w_key, w_value)
    grad_tokens = token_grads(ids, count, index, *args)
    shape = (1, 1, ROWS, MODEL)
    return update.reshape(shape), grad_tokens.reshape(shape)


def solution(mesh):
    frames = P("cam", "tm", None, None)
    return jax.shard_map(
        local,
        mesh=mesh,
        in_specs=(frames, P(), P(), P(), P(), frames, P(), P(), P()),
        out_specs=(frames, frames),
        check_vma=False,
    )
```

```python
import jax
import jax.numpy as jnp
from jax import lax
from jax.experimental import pallas as pl
from jax.experimental.pallas import tpu as pltpu
from jax.sharding import PartitionSpec as P


LOW = jnp.bfloat16
WIDE = jnp.float32
ROWS = 512
MODEL = 1536
INNER = 768
STRIP = 128
MEM = 32
POOL = ROWS // MEM
READS = 4
SLOTS = 6
LIVE_MAX = 4
MEM_AT = ROWS
FAR_AT = ROWS + READS * MEM
KEYS = FAR_AT + LIVE_MAX * STRIP
PAIR = 128
CHUNK = 384
EPS = 1e-05
MASKED = -1e30
NT = (((1,), (1,)), ((), ()))
GROUPS = ((0, 4), (4, 2))


def dot(left, right):
    return jnp.dot(left, right, preferred_element_type=WIDE)


def dot_t(left, right):
    return lax.dot_general(left, right, NT, preferred_element_type=WIDE)


def whole(shape):
    return pl.BlockSpec(shape, lambda *_: (0,) * len(shape))


def call(kernel, grid, scalars, in_specs, out_specs, out_shape, scratch, flops, moved, vmem=24):
    return pl.pallas_call(
        kernel,
        grid_spec=pltpu.PrefetchScalarGridSpec(
            num_scalar_prefetch=scalars,
            grid=(grid,),
            in_specs=in_specs,
            out_specs=out_specs,
            scratch_shapes=scratch,
        ),
        out_shape=out_shape,
        compiler_params=pltpu.CompilerParams(
            dimension_semantics=("arbitrary",), vmem_limit_bytes=vmem << 20
        ),
        cost_estimate=pl.CostEstimate(flops=flops, bytes_accessed=moved, transcendentals=0),
    )


IN_PLACE = pl.BlockSpec(memory_space=pl.ANY)
IN_HBM = pl.BlockSpec(memory_space=pltpu.HBM)


def array(shape, dtype):
    return jax.ShapeDtypeStruct(shape, dtype)


def normalize(rows):
    widened = rows.astype(WIDE)
    average = jnp.mean(widened, axis=-1, keepdims=True)
    centred = widened - average
    spread = jnp.mean(centred * centred, axis=-1, keepdims=True)
    inverse = lax.rsqrt(spread + EPS)
    return centred * inverse, inverse


def project_keys_kernel(ids, index, tokens, w_key, w_value, low, keys, values, kept, *rest):
    sends, rest = rest[:3], rest[3:]
    rows, key_w, value_w, normed_low, made, kept_wide, kept_low, in_sem, out_sem, send_sem = rest
    camera = ids[0]
    loads = []
    for step, start in enumerate(range(0, ROWS, STRIP)):
        at = pl.ds(start, STRIP)
        loads.append(pltpu.make_async_copy(tokens.at[at], rows.at[at], in_sem.at[step]))
    loads.append(pltpu.make_async_copy(w_key, key_w, in_sem.at[4]))
    loads.append(pltpu.make_async_copy(w_value, value_w, in_sem.at[5]))
    for load in loads:
        load.start()

    def norm(first, last):
        for start in range(first, last, 64):
            normed = normalize(rows[start : start + 64, :])[0]
            normed_low[start : start + 64, :] = normed.astype(LOW)
            picked = normed.reshape(64 // POOL, POOL, MODEL)[:, 0, :]
            kept_wide[start // POOL : (start + 64) // POOL, :] = picked

    def product(kind, weight, first, last):
        for start in range(0, INNER, 256):
            cols = slice(start, start + 256)
            made[kind, first:last, cols] = dot(normed_low[first:last, :], weight[:, cols]).astype(LOW)

    def product_kept(kind, weight):
        for start in range(0, INNER, 256):
            cols = slice(kind * INNER + start, kind * INNER + start + 256)
            kept[:, cols] = dot(kept_low[...], weight[:, start : start + 256]).astype(LOW)

    stores = []

    def store(source, target, sem):
        stores.append(pltpu.make_async_copy(source, target, sem))
        stores[-1].start()

    def publish(kind, out):
        for shift in (1, 2, 3):
            for slot in range(2):
                strip = index[camera, slot, lax.rem(camera + shift, 4)]
                at = pl.ds(pl.multiple_of(strip * STRIP, STRIP), STRIP)
                sem = send_sem.at[kind * SLOTS + 2 * (shift - 1) + slot]
                store(made.at[kind, at], sends[shift - 1].at[kind, slot], sem)
        store(made.at[kind], out, out_sem.at[1 + kind])

    half = ROWS // 2
    loads[0].wait()
    loads[1].wait()
    norm(0, half)
    for load in loads[2:5]:
        load.wait()
    product(0, key_w, 0, half)
    norm(half, ROWS)
    store(normed_low, low, out_sem.at[0])
    product(0, key_w, half, ROWS)
    kept_low[...] = kept_wide[...].astype(LOW)
    product_kept(0, key_w)
    publish(0, keys)
    loads[5].wait()
    product_kept(1, value_w)
    product(1, value_w, 0, ROWS)
    publish(1, values)
    for copy in stores:
        copy.wait()


def project_keys(ids, index, tokens, w_key, w_value):
    return call(
        project_keys_kernel,
        1,
        2,
        [IN_HBM] * 3,
        [IN_PLACE] * 3 + [whole((MEM, 2 * INNER))] + [IN_PLACE] * 3,
        [array((ROWS, MODEL), LOW), array((ROWS, INNER), LOW), array((ROWS, INNER), LOW)]
        + [array((MEM, 2 * INNER), LOW)]
        + [array((2, 2, STRIP, INNER), LOW)] * 3,
        [
            pltpu.VMEM((ROWS, MODEL), LOW),
            pltpu.VMEM((MODEL, INNER), LOW),
            pltpu.VMEM((MODEL, INNER), LOW),
            pltpu.VMEM((ROWS, MODEL), LOW),
            pltpu.VMEM((2, ROWS, INNER), LOW),
            pltpu.VMEM((MEM, MODEL), WIDE),
            pltpu.VMEM((MEM, MODEL), LOW),
            pltpu.SemaphoreType.DMA((6,)),
            pltpu.SemaphoreType.DMA((3,)),
            pltpu.SemaphoreType.DMA((2 * SLOTS,)),
        ],
        4 * ROWS * MODEL * INNER,
        12 << 20,
        vmem=60,
    )(ids, index, tokens, w_key, w_value)


def project_queries_kernel(low, grad_update, w_query, w_out, queries, grad_mixed):
    product = dot(low[...], w_query[...]).astype(LOW)
    queries[...] = product * jnp.asarray(0.125, LOW)
    grad_mixed[...] = dot_t(grad_update[...], w_out[...]).astype(LOW)


def project_queries(low, grad_update, w_query, w_out):
    width = 384
    out = pl.BlockSpec((ROWS, width), lambda j: (0, j))
    return call(
        project_queries_kernel,
        INNER // width,
        0,
        [
            whole((ROWS, MODEL)),
            whole((ROWS, MODEL)),
            pl.BlockSpec((MODEL, width), lambda j: (0, j)),
            pl.BlockSpec((width, MODEL), lambda j: (j, 0)),
        ],
        [out, out],
        [array((ROWS, INNER), LOW)] * 2,
        [],
        4 * ROWS * MODEL * INNER,
        10 << 20,
    )(low, grad_update, w_query, w_out)


def parts_of(frame):
    return frame // 8, lax.rem(frame // 2, 4), lax.rem(frame, 2)


def source_of(offsets, frame, read):
    source = frame - offsets[read, frame]
    return jnp.maximum(source, 0), source >= 0


def back_to(frame, source):
    z_here, x_here, core_here = parts_of(frame)
    z_at, x_at, core_at = parts_of(source)
    return lax.rem(z_here - z_at + 4, 4), lax.rem(x_here - x_at + 4, 4), core_at == core_here


def pick_kernel(ids, offsets, held_0, held_1, held_2, held_3, for_partner, for_me, sem):
    frame = ids[1]
    partner = frame + 1 - 2 * lax.rem(frame, 2)
    held = (held_0, held_1, held_2, held_3)
    wanted = []
    for at, (reader, picked) in enumerate(((partner, for_partner), (frame, for_me))):
        for read in range(READS):
            source, live = source_of(offsets, reader, read)
            back_z, back_x, same = back_to(frame, source)
            wanted.append(jnp.logical_and(live, same))
            slot = at * READS + read
            for shift in range(4):

                @pl.when(jnp.logical_and(wanted[-1], back_x == shift))
                def _():
                    pltpu.make_async_copy(
                        held[shift].at[back_z], picked.at[read], sem.at[slot]
                    ).start()

            @pl.when(jnp.logical_not(wanted[-1]))
            def _():
                picked[read] = jnp.zeros((MEM, 2 * INNER), LOW)

    for slot in range(2 * READS):
        picked = (for_partner, for_me)[slot // READS]

        @pl.when(wanted[slot])
        def _():
            pltpu.make_async_copy(held_0.at[0], picked.at[slot % READS], sem.at[slot]).wait()


def pick(ids, offsets, held):
    shape = (READS, MEM, 2 * INNER)
    return call(
        pick_kernel,
        1,
        2,
        [IN_PLACE] * 4,
        [whole(shape)] * 2,
        [array(shape, LOW)] * 2,
        [pltpu.SemaphoreType.DMA((2 * READS,))],
        0,
        1 << 20,
        vmem=4,
    )(ids, offsets, *held)


def shift_z(by):
    return [(f, (f + 8 * by) % 32) for f in range(32)]


def shift_x(by):
    return [(f, f // 8 * 8 + (f % 8 + 2 * by) % 8) for f in range(32)]


SWAP_CORE = [(f, f ^ 1) for f in range(32)]


def shift_cam(by):
    return [(s, (s + by) % 4) for s in range(4)]


def attention_kernel(ids, offsets, count, queries, grads, keys_own, values_own, *rest):
    mem_in, far_in, rest = (rest[:2], rest[2:4]), rest[4:7], rest[7:]
    mixed, grad_query, grad_keys, grad_values, grad_mem, grad_mem_low = rest[:6]
    far_out, rest = rest[6:9], rest[9:]
    keys, values, keys_t, values_t, scores, grad_w, weights, grad_s, two_q, two_g, rest_k, rest_v = rest
    camera, frame = ids[0], ids[1]

    slot_live, slot_at, live_total = [], [], 0
    for slot in range(SLOTS):
        sender = lax.rem(camera + 4 - (slot // 2 + 1), 4)
        live = count[sender, camera] > slot % 2
        slot_live.append(jnp.logical_and(live, live_total < LIVE_MAX))
        slot_at.append(jnp.minimum(live_total, LIVE_MAX - 1))
        live_total = live_total + live.astype(jnp.int32)

    keys[0:ROWS, :] = keys_own[...]
    values[0:ROWS, :] = values_own[...]
    for read in range(READS):
        source, live = source_of(offsets, frame, read)
        _, _, same = back_to(frame, source)
        mine = jnp.logical_and(live, same)
        at = slice(MEM_AT + read * MEM, MEM_AT + (read + 1) * MEM)
        for kind, target in enumerate((keys, values)):
            picked, given = mem_in[kind]
            target[at, :] = jnp.where(mine, picked[read], given[read])

    for place in range(LIVE_MAX):

        @pl.when(live_total <= place)
        def _():
            at = slice(FAR_AT + place * STRIP, FAR_AT + (place + 1) * STRIP)
            keys[at, :] = jnp.zeros((STRIP, PAIR), LOW)
            values[at, :] = jnp.zeros((STRIP, PAIR), LOW)

    for slot in range(SLOTS):

        @pl.when(slot_live[slot])
        def _():
            at = pl.ds(pl.multiple_of(FAR_AT + slot_at[slot] * STRIP, STRIP), STRIP)
            keys[at, :] = far_in[slot // 2][0, slot % 2]
            values[at, :] = far_in[slot // 2][1, slot % 2]

    keys_t[...] = keys[...].T
    values_t[...] = values[...].T
    lane = lax.broadcasted_iota(jnp.int32, (ROWS, PAIR), 1)
    for head in range(2):
        keep = (lane >= 64) if head else (lane < 64)
        at = slice(head * ROWS, (head + 1) * ROWS)
        two_q[at, :] = jnp.where(keep, queries[...], jnp.zeros((ROWS, PAIR), LOW))
        two_g[at, :] = jnp.where(keep, grads[...], jnp.zeros((ROWS, PAIR), LOW))

    pieces = [(0, ROWS, None)]
    for read in range(READS):
        start = MEM_AT + read * MEM
        pieces.append((start, start + MEM, offsets[read, frame] <= frame))
    for place in range(LIVE_MAX):
        start = FAR_AT + place * STRIP
        pieces.append((start, start + STRIP, place < live_total))

    def pieces_of(base):
        for start, end, live in pieces:
            low, high = max(start, base), min(end, base + CHUNK)
            if low < high:
                yield low, high, live

    def folded(block):
        return block.reshape(block.shape[0] // 8, 8, ROWS)

    bases = range(0, KEYS, CHUNK)
    highest = [jnp.full((8, ROWS), MASKED, WIDE)] * 2
    total, inner = [jnp.zeros((8, ROWS), WIDE)] * 2, [jnp.zeros((8, ROWS), WIDE)] * 2
    share = [None, None]

    def score(head, base):
        cols = slice(head * ROWS, (head + 1) * ROWS)
        block = dot_t(keys[base : base + CHUNK, :], two_q[cols, :])
        scores[head, base : base + CHUNK, :] = block
        for low, high, live in pieces_of(base):
            top = jnp.max(folded(block[low - base : high - base]), axis=0)
            top = jnp.maximum(highest[head], top)
            highest[head] = top if live is None else jnp.where(live, top, highest[head])
        if base == bases[-1]:
            highest[head] = jnp.max(highest[head], axis=0, keepdims=True)

    def lift(head, base):
        cols = slice(head * ROWS, (head + 1) * ROWS)
        block = dot_t(values[base : base + CHUNK, :], two_g[cols, :])
        grad_w[head, base : base + CHUNK, :] = block
        for low, high, live in pieces_of(base):
            top = highest[head] if live is None else jnp.where(live, highest[head], -MASKED)
            lifted = jnp.exp(scores[head, low:high, :] - top)
            scores[head, low:high, :] = lifted
            total[head] = total[head] + jnp.sum(folded(lifted), axis=0)
            inner[head] = inner[head] + jnp.sum(folded(lifted * block[low - base : high - base]), axis=0)
        if base == bases[-1]:
            share[head] = 1.0 / jnp.sum(total[head], axis=0, keepdims=True)
            inner[head] = jnp.sum(inner[head], axis=0, keepdims=True) * share[head]

    def settle(head, base):
        cols, at = slice(head * ROWS, (head + 1) * ROWS), slice(base, base + CHUNK)
        part = scores[head, at, :] * share[head]
        weights[at, cols] = part.astype(LOW)
        grad_s[at, cols] = (part * (grad_w[head, at, :] - inner[head])).astype(LOW)

    def row_grads(head, base):
        cols, at = slice(head * ROWS, (head + 1) * ROWS), slice(base, base + CHUNK)
        for_value = dot(weights[at, cols], two_g[cols, :])
        for_key = dot(grad_s[at, cols], two_q[cols, :])
        for made, own, far in ((for_key, grad_keys, rest_k), (for_value, grad_values, rest_v)):
            for start, end, ref, shift in ((0, ROWS, own, 0), (ROWS, KEYS, far, ROWS)):
                first, last = max(start, base), min(end, base + CHUNK)
                if first < last:
                    there = slice(first - shift, last - shift)
                    block = made[first - base : last - base]
                    ref[there, :] = block if head == 0 else ref[there, :] + block

    mixed_t, grad_query_t = [None, None], [None, None]

    def query_side(head):
        cols, dims = slice(head * ROWS, (head + 1) * ROWS), slice(head * 64, (head + 1) * 64)
        mixed_t[head] = dot(values_t[dims, :], weights[:, cols])
        grad_query_t[head] = dot(keys_t[dims, :], grad_s[:, cols])

    for base in bases:
        score(0, base)
    for base in bases:
        lift(0, base)
        score(1, base)
    for base in bases:
        settle(0, base)
        lift(1, base)
    for base in bases:
        row_grads(0, base)
        settle(1, base)
    query_side(0)
    for base in bases:
        row_grads(1, base)
    query_side(1)
    mixed[...] = jnp.concatenate(mixed_t, axis=0).T.astype(LOW)
    grad_query[...] = (jnp.concatenate(grad_query_t, axis=0).T * 0.125).astype(LOW)

    grad_mem[0] = rest_k[0 : READS * MEM, :]
    grad_mem[1] = rest_v[0 : READS * MEM, :]
    grad_mem_low[0] = rest_k[0 : READS * MEM, :].astype(LOW)
    grad_mem_low[1] = rest_v[0 : READS * MEM, :].astype(LOW)
    for slot in range(SLOTS):

        @pl.when(slot_live[slot])
        def _():
            start = FAR_AT - ROWS + slot_at[slot] * STRIP
            at = pl.ds(pl.multiple_of(start, STRIP), STRIP)
            far_out[slot // 2][0, slot % 2] = rest_k[at, :].astype(LOW)
            far_out[slot // 2][1, slot % 2] = rest_v[at, :].astype(LOW)


def attention(group, ids, offsets, count, queries, grads, keys_own, values_own, mem, far):
    first, pairs = group
    width = pairs * PAIR

    def taken(rows):
        return pl.BlockSpec((rows, PAIR), lambda p, *_: (0, first + p))

    def made(rows):
        return pl.BlockSpec((rows, PAIR), lambda p, *_: (0, p))

    far_in = pl.BlockSpec((2, 2, STRIP, PAIR), lambda p, *_: (0, 0, 0, first + p))
    far_out = pl.BlockSpec((2, 2, STRIP, PAIR), lambda p, *_: (0, 0, 0, p))
    mem_k = pl.BlockSpec((4, MEM, PAIR), lambda p, *_: (0, 0, first + p))
    mem_v = pl.BlockSpec((4, MEM, PAIR), lambda p, *_: (0, 0, INNER // PAIR + first + p))
    mem_out = pl.BlockSpec((2, READS * MEM, PAIR), lambda p, *_: (0, 0, p))
    return call(
        attention_kernel,
        pairs,
        3,
        [taken(ROWS)] * 4 + [mem_k] * 2 + [mem_v] * 2 + [far_in] * 3,
        [made(ROWS)] * 4 + [mem_out] * 2 + [far_out] * 3,
        [array((ROWS, width), LOW)] * 2
        + [array((ROWS, width), WIDE)] * 2
        + [array((2, READS * MEM, width), WIDE), array((2, READS * MEM, width), LOW)]
        + [array((2, 2, STRIP, width), LOW)] * 3,
        [pltpu.VMEM((KEYS, PAIR), LOW)] * 2
        + [pltpu.VMEM((PAIR, KEYS), LOW)] * 2
        + [pltpu.VMEM((2, KEYS, ROWS), WIDE)] * 2
        + [pltpu.VMEM((KEYS, 2 * ROWS), LOW)] * 2
        + [pltpu.VMEM((2 * ROWS, PAIR), LOW)] * 2
        + [pltpu.VMEM((KEYS - ROWS, PAIR), WIDE)] * 2,
        pairs * 12 * KEYS * 2 * ROWS * 256,
        pairs * (3 << 20),
    )(ids, offsets, count, queries, grads, keys_own, values_own, *mem, *mem, *far)


def sort_kernel(ids, offsets, own, given, out_0, out_1, out_2, out_3, total):
    outs = (out_0, out_1, out_2, out_3)
    frame = ids[1]
    z_here, x_here, core_here = parts_of(frame)
    partner = frame + 1 - 2 * core_here
    total[...] = jnp.zeros_like(total)
    for reader, part in ((frame, own), (partner, given)):
        for read in range(READS):
            source, live = source_of(offsets, reader, read)
            z_at, x_at, core_at = parts_of(source)
            to = lax.rem(x_at - x_here + 4, 4) * 4 + lax.rem(z_at - z_here + 4, 4)

            @pl.when(jnp.logical_and(live, core_at == core_here))
            def _():
                for kind in range(2):
                    added = part[kind, read * MEM : (read + 1) * MEM, :].astype(WIDE)
                    total[to, kind] = total[to, kind] + added

    for shift in range(4):
        outs[shift][...] = total[4 * shift : 4 * shift + 4].astype(LOW)


def sort_reads(ids, offsets, own, given):
    width = own.shape[2]
    shape = (4, 2, MEM, width)
    return call(
        sort_kernel,
        1,
        2,
        [whole(own.shape)] * 2,
        [whole(shape)] * 4,
        [array(shape, LOW)] * 4,
        [pltpu.VMEM((16, 2, MEM, width), WIDE)],
        0,
        2 << 20,
        vmem=12,
    )(ids, offsets, own, given)


def add_kernel(*refs):
    for group, (first, pairs) in enumerate(GROUPS):
        parts, cols = refs[4 * group : 4 * group + 4], slice(first * PAIR, (first + pairs) * PAIR)
        for shift in range(4):
            total = parts[0][shift].astype(WIDE) + parts[1][shift].astype(WIDE)
            total = total + parts[2][shift].astype(WIDE) + parts[3][shift].astype(WIDE)
            refs[4 * len(GROUPS) + shift][:, :, cols] = total.astype(LOW)


def add_reads(parts):
    return call(
        add_kernel,
        1,
        0,
        [whole(part.shape) for part in parts],
        [whole((2, MEM, INNER))] * 4,
        [array((2, MEM, INNER), LOW)] * 4,
        [],
        0,
        2 << 20,
        vmem=8,
    )(*parts)


def outward_kernel(*refs):
    count = len(GROUPS)
    mixed, grad_query = refs[:count], refs[count : 2 * count]
    w_out, w_query, update, grad_normed = refs[2 * count :]
    total, part = 0.0, 0.0
    for (first, pairs), mixed_ref, grad_ref in zip(GROUPS, mixed, grad_query):
        cols = slice(first * PAIR, (first + pairs) * PAIR)
        total = total + dot(mixed_ref[...], w_out[cols, :])
        part = part + dot_t(grad_ref[...], w_query[:, cols])
    update[...] = total.astype(LOW)
    grad_normed[...] = part


def outward(mixed, grad_query, w_out, w_query):
    width = 512
    out = pl.BlockSpec((ROWS, width), lambda j: (0, j))
    parts = [whole((ROWS, pairs * PAIR)) for _, pairs in GROUPS]
    return call(
        outward_kernel,
        MODEL // width,
        0,
        parts
        + parts
        + [
            pl.BlockSpec((INNER, width), lambda j: (0, j)),
            pl.BlockSpec((width, INNER), lambda j: (j, 0)),
        ],
        [out, out],
        [array((ROWS, MODEL), LOW), array((ROWS, MODEL), WIDE)],
        [],
        4 * ROWS * MODEL * INNER,
        11 << 20,
    )(*mixed, *grad_query, w_out, w_query)


def token_grads_kernel(ids, count, index, *refs):
    groups = len(GROUPS)
    own = (refs[:groups], refs[groups : 2 * groups])
    back, refs = refs[2 * groups : 5 * groups], refs[5 * groups :]
    kept, (tokens, grad_part, w_key, w_value, grad_tokens), refs = refs[:4], refs[4:9], refs[9:]
    total, grad_normed, low, made, out_sem = refs
    camera = ids[0]

    row = lax.broadcasted_iota(jnp.int32, (ROWS, 4 * MEM), 0)
    col = lax.broadcasted_iota(jnp.int32, (ROWS, 4 * MEM), 1)
    hit = row == (col % MEM) * (ROWS // MEM)
    spread = jnp.where(hit, 1.0, 0.0).astype(LOW)
    for kind in range(2):
        stacked = jnp.concatenate([part[kind] for part in kept], axis=0)
        for group, (first, pairs) in enumerate(GROUPS):
            cols = slice(first * PAIR, (first + pairs) * PAIR)
            total[kind, :, cols] = own[kind][group][...] + dot(spread, stacked[:, cols])
    for shift in (1, 2, 3):
        other = lax.rem(camera + shift, 4)
        for slot in range(2):

            @pl.when(slot < count[camera, other])
            def _():
                start = index[camera, slot, other] * STRIP
                at = pl.ds(pl.multiple_of(start, STRIP), STRIP)
                for kind in range(2):
                    for group, (first, pairs) in enumerate(GROUPS):
                        cols = slice(first * PAIR, (first + pairs) * PAIR)
                        given = back[3 * group + shift - 1][kind, slot]
                        total[kind, at, cols] = total[kind, at, cols] + given.astype(WIDE)

    half = ROWS // 2
    stores = []
    for start in range(0, ROWS, half):
        at = slice(start, start + half)
        for kind in range(2):
            low[kind, at, :] = total[kind, at, :].astype(LOW)
        for first in range(0, MODEL, 512):
            cols = slice(first, first + 512)
            grad_normed[at, cols] = (
                grad_part[at, cols]
                + dot_t(low[0, at, :], w_key[cols, :])
                + dot_t(low[1, at, :], w_value[cols, :])
            )
        for begin in range(start, start + half, 64):
            at = slice(begin, begin + 64)
            normed, inverse = normalize(tokens[at, :])
            grad = grad_normed[at, :]
            first_mean = jnp.mean(grad, axis=-1, keepdims=True)
            second_mean = jnp.mean(grad * normed, axis=-1, keepdims=True)
            made[at, :] = (inverse * (grad - first_mean - normed * second_mean)).astype(LOW)
        block = pl.ds(start, half)
        stores.append(
            pltpu.make_async_copy(made.at[block], grad_tokens.at[block], out_sem.at[start // half])
        )
        stores[-1].start()
    for store in stores:
        store.wait()


def token_grads(ids, count, index, own_keys, own_values, back, kept, tokens, grad_part, w_key, w_value):
    operands = (*own_keys, *own_values, *back, *kept, tokens, grad_part, w_key, w_value)
    return pl.pallas_call(
        token_grads_kernel,
        in_specs=[pl.BlockSpec(memory_space=pltpu.SMEM)] * 3
        + [pl.BlockSpec(memory_space=pltpu.VMEM)] * len(operands),
        out_specs=IN_PLACE,
        out_shape=array((ROWS, MODEL), LOW),
        scratch_shapes=[
            pltpu.VMEM((2, ROWS, INNER), WIDE),
            pltpu.VMEM((ROWS, MODEL), WIDE),
            pltpu.VMEM((2, ROWS, INNER), LOW),
            pltpu.VMEM((ROWS, MODEL), LOW),
            pltpu.SemaphoreType.DMA((2,)),
        ],
        compiler_params=pltpu.CompilerParams(vmem_limit_bytes=36 << 20),
        cost_estimate=pl.CostEstimate(
            flops=4 * ROWS * MODEL * INNER, bytes_accessed=16 << 20, transcendentals=0
        ),
        name="token_grads",
    )(ids, count, index, *operands)


def send(value, axis, pairs):
    return lax.ppermute(value, axis, pairs)


def local(tokens, w_query, w_key, w_value, w_out, grad_update, offsets, count, index):
    tokens = tokens.reshape(ROWS, MODEL)
    grad_update = grad_update.reshape(ROWS, MODEL)
    ids = jnp.stack([lax.axis_index("cam"), lax.axis_index("tm")]).astype(jnp.int32)
    index, offsets = jnp.transpose(index, (0, 2, 1)), offsets.T
    others = (1, 2, 3)

    low, keys, values, kept, *sends = project_keys(ids, index, tokens, w_key, w_value)
    far = [send(sends[k - 1], "cam", shift_cam(k)) for k in others]
    along_z = jnp.stack([kept] + [send(kept, "tm", shift_z(k)) for k in others])
    held = [along_z] + [send(along_z, "tm", shift_x(k)) for k in others]
    queries, grads = project_queries(low, grad_update, w_query, w_out)
    for_partner, for_me = pick(ids, offsets, held)
    given = send(for_partner, "tm", SWAP_CORE)
    made, back, parts = [], [], []
    for group in GROUPS:
        args = (queries, grads, keys, values, (for_me, given), far)
        made.append(attention(group, ids, offsets, count, *args))
        for k in others:
            back.append(send(made[-1][5 + k], "cam", shift_cam(-k)))
        mem_given = send(made[-1][5], "tm", SWAP_CORE)
        to_x = sort_reads(ids, offsets, made[-1][4], mem_given)
        parts += [to_x[0]] + [send(to_x[k], "tm", shift_x(k)) for k in others]
    mixed, grad_query, own_keys, own_values = [[m[k] for m in made] for k in range(4)]

    update, grad_part = outward(mixed, grad_query, w_out, w_query)
    sorted_z = add_reads(parts)
    kept_grads = [sorted_z[0]] + [send(sorted_z[k], "tm", shift_z(k)) for k in others]
    args = (own_keys, own_values, back, kept_grads, tokens, grad_part, w_key, w_value)
    grad_tokens = token_grads(ids, count, index, *args)
    shape = (1, 1, ROWS, MODEL)
    return update.reshape(shape), grad_tokens.reshape(shape)


def solution(mesh):
    frames = P("cam", "tm", None, None)
    return jax.shard_map(
        local,
        mesh=mesh,
        in_specs=(frames, P(), P(), P(), P(), frames, P(), P(), P()),
        out_specs=(frames, frames),
        check_vma=False,
    )
```

```python
import jax
import jax.numpy as jnp
from jax import lax
from jax.experimental import pallas as pl
from jax.experimental.pallas import tpu as pltpu
from jax.sharding import PartitionSpec as P


LOW = jnp.bfloat16
WIDE = jnp.float32
ROWS = 512
MODEL = 1536
INNER = 768
STRIP = 128
MEM = 32
POOL = ROWS // MEM
READS = 4
SLOTS = 6
LIVE_MAX = 4
MEM_AT = ROWS
FAR_AT = ROWS + READS * MEM
KEYS = FAR_AT + LIVE_MAX * STRIP
PAIR = 128
CHUNK = 384
EPS = 1e-05
MASKED = -1e30
NT = (((1,), (1,)), ((), ()))
GROUPS = ((0, 4), (4, 2))


def dot(left, right):
    return jnp.dot(left, right, preferred_element_type=WIDE)


def dot_t(left, right):
    return lax.dot_general(left, right, NT, preferred_element_type=WIDE)


def whole(shape):
    return pl.BlockSpec(shape, lambda *_: (0,) * len(shape))


def call(kernel, grid, scalars, in_specs, out_specs, out_shape, scratch, flops, moved, vmem=24):
    return pl.pallas_call(
        kernel,
        grid_spec=pltpu.PrefetchScalarGridSpec(
            num_scalar_prefetch=scalars,
            grid=(grid,),
            in_specs=in_specs,
            out_specs=out_specs,
            scratch_shapes=scratch,
        ),
        out_shape=out_shape,
        compiler_params=pltpu.CompilerParams(
            dimension_semantics=("arbitrary",), vmem_limit_bytes=vmem << 20
        ),
        cost_estimate=pl.CostEstimate(flops=flops, bytes_accessed=moved, transcendentals=0),
    )


IN_PLACE = pl.BlockSpec(memory_space=pl.ANY)
IN_HBM = pl.BlockSpec(memory_space=pltpu.HBM)


def array(shape, dtype):
    return jax.ShapeDtypeStruct(shape, dtype)


def normalize(rows):
    widened = rows.astype(WIDE)
    average = jnp.mean(widened, axis=-1, keepdims=True)
    centred = widened - average
    spread = jnp.mean(centred * centred, axis=-1, keepdims=True)
    inverse = lax.rsqrt(spread + EPS)
    return centred * inverse, inverse


def project_keys_kernel(ids, index, tokens, w_key, w_value, low, keys, values, kept, *rest):
    sends, rest = rest[:3], rest[3:]
    rows, key_w, value_w, normed_low, made, kept_wide, in_sem, out_sem, send_sem = rest
    camera = ids[0]
    loads = []
    for step, start in enumerate(range(0, ROWS, STRIP)):
        at = pl.ds(start, STRIP)
        loads.append(pltpu.make_async_copy(tokens.at[at], rows.at[at], in_sem.at[step]))
    loads.append(pltpu.make_async_copy(w_key, key_w, in_sem.at[4]))
    loads.append(pltpu.make_async_copy(w_value, value_w, in_sem.at[5]))
    for load in loads:
        load.start()

    def norm(first, last):
        for start in range(first, last, 64):
            normed = normalize(rows[start : start + 64, :])[0]
            normed_low[start : start + 64, :] = normed.astype(LOW)
            picked = normed.reshape(64 // POOL, POOL, MODEL)[:, 0, :]
            kept_wide[start // POOL : (start + 64) // POOL, :] = picked

    def product(kind, weight, first, last):
        for start in range(0, INNER, 256):
            cols = slice(start, start + 256)
            made[kind, first:last, cols] = dot(normed_low[first:last, :], weight[:, cols]).astype(LOW)

    stores = []

    def store(source, target, sem):
        stores.append(pltpu.make_async_copy(source, target, sem))
        stores[-1].start()

    def publish(kind, out):
        for shift in (1, 2, 3):
            for slot in range(2):
                strip = index[camera, slot, lax.rem(camera + shift, 4)]
                at = pl.ds(pl.multiple_of(strip * STRIP, STRIP), STRIP)
                sem = send_sem.at[kind * SLOTS + 2 * (shift - 1) + slot]
                store(made.at[kind, at], sends[shift - 1].at[kind, slot], sem)
        store(made.at[kind, pl.ds(0, ROWS)], out, out_sem.at[1 + kind])
        kept[:, kind * INNER : (kind + 1) * INNER] = made[kind, ROWS:, :]

    half = ROWS // 2
    loads[0].wait()
    loads[1].wait()
    norm(0, half)
    for load in loads[2:5]:
        load.wait()
    product(0, key_w, 0, half)
    norm(half, ROWS)
    store(normed_low.at[pl.ds(0, ROWS)], low, out_sem.at[0])
    normed_low[ROWS:, :] = kept_wide[...].astype(LOW)
    product(0, key_w, half, ROWS + MEM)
    publish(0, keys)
    loads[5].wait()
    product(1, value_w, 0, ROWS + MEM)
    publish(1, values)
    for copy in stores:
        copy.wait()


def project_keys(ids, index, tokens, w_key, w_value):
    return pl.pallas_call(
        project_keys_kernel,
        in_specs=[pl.BlockSpec(memory_space=pltpu.SMEM)] * 2 + [IN_HBM] * 3,
        out_specs=[IN_HBM] * 3 + [pl.BlockSpec(memory_space=pltpu.VMEM)] + [IN_HBM] * 3,
        out_shape=[array((ROWS, MODEL), LOW), array((ROWS, INNER), LOW), array((ROWS, INNER), LOW)]
        + [array((MEM, 2 * INNER), LOW)]
        + [array((2, 2, STRIP, INNER), LOW)] * 3,
        scratch_shapes=[
            pltpu.VMEM((ROWS, MODEL), LOW),
            pltpu.VMEM((MODEL, INNER), LOW),
            pltpu.VMEM((MODEL, INNER), LOW),
            pltpu.VMEM((ROWS + MEM, MODEL), LOW),
            pltpu.VMEM((2, ROWS + MEM, INNER), LOW),
            pltpu.VMEM((MEM, MODEL), WIDE),
            pltpu.SemaphoreType.DMA((6,)),
            pltpu.SemaphoreType.DMA((3,)),
            pltpu.SemaphoreType.DMA((2 * SLOTS,)),
        ],
        compiler_params=pltpu.CompilerParams(vmem_limit_bytes=48 << 20),
        cost_estimate=pl.CostEstimate(
            flops=4 * ROWS * MODEL * INNER, bytes_accessed=12 << 20, transcendentals=0
        ),
        name="project_keys",
    )(ids, index, tokens, w_key, w_value)


def project_queries_kernel(low, grad_update, w_query, w_out, queries, grad_mixed):
    product = dot(low[...], w_query[...]).astype(LOW)
    queries[...] = product * jnp.asarray(0.125, LOW)
    grad_mixed[...] = dot_t(grad_update[...], w_out[...]).astype(LOW)


def project_queries(low, grad_update, w_query, w_out):
    width = 384
    out = pl.BlockSpec((ROWS, width), lambda j: (0, j))
    return call(
        project_queries_kernel,
        INNER // width,
        0,
        [
            whole((ROWS, MODEL)),
            whole((ROWS, MODEL)),
            pl.BlockSpec((MODEL, width), lambda j: (0, j)),
            pl.BlockSpec((width, MODEL), lambda j: (j, 0)),
        ],
        [out, out],
        [array((ROWS, INNER), LOW)] * 2,
        [],
        4 * ROWS * MODEL * INNER,
        10 << 20,
    )(low, grad_update, w_query, w_out)


def parts_of(frame):
    return frame // 8, lax.rem(frame // 2, 4), lax.rem(frame, 2)


def source_of(offsets, frame, read):
    source = frame - offsets[read, frame]
    return jnp.maximum(source, 0), source >= 0


def back_to(frame, source):
    z_here, x_here, core_here = parts_of(frame)
    z_at, x_at, core_at = parts_of(source)
    return lax.rem(z_here - z_at + 4, 4), lax.rem(x_here - x_at + 4, 4), core_at == core_here


def pick_kernel(ids, offsets, held_0, held_1, held_2, held_3, for_partner, for_me, sem):
    frame = ids[1]
    partner = frame + 1 - 2 * lax.rem(frame, 2)
    held = (held_0, held_1, held_2, held_3)
    wanted = []
    for at, (reader, picked) in enumerate(((partner, for_partner), (frame, for_me))):
        for read in range(READS):
            source, live = source_of(offsets, reader, read)
            back_z, back_x, same = back_to(frame, source)
            wanted.append(jnp.logical_and(live, same))
            slot = at * READS + read
            for shift in range(4):

                @pl.when(jnp.logical_and(wanted[-1], back_x == shift))
                def _():
                    pltpu.make_async_copy(
                        held[shift].at[back_z], picked.at[read], sem.at[slot]
                    ).start()

            @pl.when(jnp.logical_not(wanted[-1]))
            def _():
                picked[read] = jnp.zeros((MEM, 2 * INNER), LOW)

    for slot in range(2 * READS):
        picked = (for_partner, for_me)[slot // READS]

        @pl.when(wanted[slot])
        def _():
            pltpu.make_async_copy(held_0.at[0], picked.at[slot % READS], sem.at[slot]).wait()


def pick(ids, offsets, held):
    shape = (READS, MEM, 2 * INNER)
    return call(
        pick_kernel,
        1,
        2,
        [IN_PLACE] * 4,
        [whole(shape)] * 2,
        [array(shape, LOW)] * 2,
        [pltpu.SemaphoreType.DMA((2 * READS,))],
        0,
        1 << 20,
        vmem=4,
    )(ids, offsets, *held)


def shift_z(by):
    return [(f, (f + 8 * by) % 32) for f in range(32)]


def shift_x(by):
    return [(f, f // 8 * 8 + (f % 8 + 2 * by) % 8) for f in range(32)]


SWAP_CORE = [(f, f ^ 1) for f in range(32)]


def shift_cam(by):
    return [(s, (s + by) % 4) for s in range(4)]


def attention_kernel(ids, offsets, count, queries, grads, keys_own, values_own, *rest):
    mem_in, far_in, rest = (rest[:2], rest[2:4]), rest[4:7], rest[7:]
    mixed, grad_query, grad_keys, grad_values, grad_mem, grad_mem_low = rest[:6]
    far_out, rest = rest[6:9], rest[9:]
    keys, values, keys_t, values_t, scores, grad_w, weights, grad_s, two_q, two_g, rest_k, rest_v = rest
    camera, frame = ids[0], ids[1]

    slot_live, slot_at, live_total = [], [], 0
    for slot in range(SLOTS):
        sender = lax.rem(camera + 4 - (slot // 2 + 1), 4)
        live = count[sender, camera] > slot % 2
        slot_live.append(jnp.logical_and(live, live_total < LIVE_MAX))
        slot_at.append(jnp.minimum(live_total, LIVE_MAX - 1))
        live_total = live_total + live.astype(jnp.int32)

    keys[0:ROWS, :] = keys_own[...]
    values[0:ROWS, :] = values_own[...]
    for read in range(READS):
        source, live = source_of(offsets, frame, read)
        _, _, same = back_to(frame, source)
        mine = jnp.logical_and(live, same)
        at = slice(MEM_AT + read * MEM, MEM_AT + (read + 1) * MEM)
        for kind, target in enumerate((keys, values)):
            picked, given = mem_in[kind]
            target[at, :] = jnp.where(mine, picked[read], given[read])

    for place in range(LIVE_MAX):

        @pl.when(live_total <= place)
        def _():
            at = slice(FAR_AT + place * STRIP, FAR_AT + (place + 1) * STRIP)
            keys[at, :] = jnp.zeros((STRIP, PAIR), LOW)
            values[at, :] = jnp.zeros((STRIP, PAIR), LOW)

    for slot in range(SLOTS):

        @pl.when(slot_live[slot])
        def _():
            at = pl.ds(pl.multiple_of(FAR_AT + slot_at[slot] * STRIP, STRIP), STRIP)
            keys[at, :] = far_in[slot // 2][0, slot % 2]
            values[at, :] = far_in[slot // 2][1, slot % 2]

    keys_t[...] = keys[...].T
    values_t[...] = values[...].T
    lane = lax.broadcasted_iota(jnp.int32, (ROWS, PAIR), 1)
    for head in range(2):
        keep = (lane >= 64) if head else (lane < 64)
        at = slice(head * ROWS, (head + 1) * ROWS)
        two_q[at, :] = jnp.where(keep, queries[...], jnp.zeros((ROWS, PAIR), LOW))
        two_g[at, :] = jnp.where(keep, grads[...], jnp.zeros((ROWS, PAIR), LOW))

    pieces = [(0, ROWS, None)]
    for read in range(READS):
        start = MEM_AT + read * MEM
        pieces.append((start, start + MEM, offsets[read, frame] <= frame))
    for place in range(LIVE_MAX):
        start = FAR_AT + place * STRIP
        pieces.append((start, start + STRIP, place < live_total))

    def pieces_of(base):
        for start, end, live in pieces:
            low, high = max(start, base), min(end, base + CHUNK)
            if low < high:
                yield low, high, live

    def folded(block):
        return block.reshape(block.shape[0] // 8, 8, ROWS)

    bases = range(0, KEYS, CHUNK)
    highest = [jnp.full((8, ROWS), MASKED, WIDE)] * 2
    total, inner = [jnp.zeros((8, ROWS), WIDE)] * 2, [jnp.zeros((8, ROWS), WIDE)] * 2
    share = [None, None]

    def score(head, base):
        cols = slice(head * ROWS, (head + 1) * ROWS)
        block = dot_t(keys[base : base + CHUNK, :], two_q[cols, :])
        scores[head, base : base + CHUNK, :] = block
        for low, high, live in pieces_of(base):
            top = jnp.max(folded(block[low - base : high - base]), axis=0)
            top = jnp.maximum(highest[head], top)
            highest[head] = top if live is None else jnp.where(live, top, highest[head])
        if base == bases[-1]:
            highest[head] = jnp.max(highest[head], axis=0, keepdims=True)

    def lift(head, base):
        cols = slice(head * ROWS, (head + 1) * ROWS)
        block = dot_t(values[base : base + CHUNK, :], two_g[cols, :])
        grad_w[head, base : base + CHUNK, :] = block
        for low, high, live in pieces_of(base):
            top = highest[head] if live is None else jnp.where(live, highest[head], -MASKED)
            lifted = jnp.exp(scores[head, low:high, :] - top)
            scores[head, low:high, :] = lifted
            total[head] = total[head] + jnp.sum(folded(lifted), axis=0)
            inner[head] = inner[head] + jnp.sum(folded(lifted * block[low - base : high - base]), axis=0)
        if base == bases[-1]:
            share[head] = 1.0 / jnp.sum(total[head], axis=0, keepdims=True)
            inner[head] = jnp.sum(inner[head], axis=0, keepdims=True) * share[head]

    def settle(head, base):
        cols, at = slice(head * ROWS, (head + 1) * ROWS), slice(base, base + CHUNK)
        part = scores[head, at, :] * share[head]
        weights[at, cols] = part.astype(LOW)
        grad_s[at, cols] = (part * (grad_w[head, at, :] - inner[head])).astype(LOW)

    def row_grads(head, base):
        cols, at = slice(head * ROWS, (head + 1) * ROWS), slice(base, base + CHUNK)
        for_value = dot(weights[at, cols], two_g[cols, :])
        for_key = dot(grad_s[at, cols], two_q[cols, :])
        for made, own, far in ((for_key, grad_keys, rest_k), (for_value, grad_values, rest_v)):
            for start, end, ref, shift in ((0, ROWS, own, 0), (ROWS, KEYS, far, ROWS)):
                first, last = max(start, base), min(end, base + CHUNK)
                if first < last:
                    there = slice(first - shift, last - shift)
                    block = made[first - base : last - base]
                    ref[there, :] = block if head == 0 else ref[there, :] + block

    mixed_t, grad_query_t = [None, None], [None, None]

    def query_side(head):
        cols, dims = slice(head * ROWS, (head + 1) * ROWS), slice(head * 64, (head + 1) * 64)
        mixed_t[head] = dot(values_t[dims, :], weights[:, cols])
        grad_query_t[head] = dot(keys_t[dims, :], grad_s[:, cols])

    for base in bases:
        score(0, base)
    for base in bases:
        lift(0, base)
        score(1, base)
    for base in bases:
        settle(0, base)
        lift(1, base)
    for base in bases:
        row_grads(0, base)
        settle(1, base)
    query_side(0)
    for base in bases:
        row_grads(1, base)
    query_side(1)
    mixed[...] = jnp.concatenate(mixed_t, axis=0).T.astype(LOW)
    grad_query[...] = (jnp.concatenate(grad_query_t, axis=0).T * 0.125).astype(LOW)

    grad_mem[0] = rest_k[0 : READS * MEM, :]
    grad_mem[1] = rest_v[0 : READS * MEM, :]
    grad_mem_low[0] = rest_k[0 : READS * MEM, :].astype(LOW)
    grad_mem_low[1] = rest_v[0 : READS * MEM, :].astype(LOW)
    for slot in range(SLOTS):

        @pl.when(slot_live[slot])
        def _():
            start = FAR_AT - ROWS + slot_at[slot] * STRIP
            at = pl.ds(pl.multiple_of(start, STRIP), STRIP)
            far_out[slot // 2][0, slot % 2] = rest_k[at, :].astype(LOW)
            far_out[slot // 2][1, slot % 2] = rest_v[at, :].astype(LOW)


def attention(group, ids, offsets, count, queries, grads, keys_own, values_own, mem, far):
    first, pairs = group
    width = pairs * PAIR

    def taken(rows):
        return pl.BlockSpec((rows, PAIR), lambda p, *_: (0, first + p))

    def made(rows):
        return pl.BlockSpec((rows, PAIR), lambda p, *_: (0, p))

    far_in = pl.BlockSpec((2, 2, STRIP, PAIR), lambda p, *_: (0, 0, 0, first + p))
    far_out = pl.BlockSpec((2, 2, STRIP, PAIR), lambda p, *_: (0, 0, 0, p))
    mem_k = pl.BlockSpec((4, MEM, PAIR), lambda p, *_: (0, 0, first + p))
    mem_v = pl.BlockSpec((4, MEM, PAIR), lambda p, *_: (0, 0, INNER // PAIR + first + p))
    mem_out = pl.BlockSpec((2, READS * MEM, PAIR), lambda p, *_: (0, 0, p))
    return call(
        attention_kernel,
        pairs,
        3,
        [taken(ROWS)] * 4 + [mem_k] * 2 + [mem_v] * 2 + [far_in] * 3,
        [made(ROWS)] * 4 + [mem_out] * 2 + [far_out] * 3,
        [array((ROWS, width), LOW)] * 2
        + [array((ROWS, width), WIDE)] * 2
        + [array((2, READS * MEM, width), WIDE), array((2, READS * MEM, width), LOW)]
        + [array((2, 2, STRIP, width), LOW)] * 3,
        [pltpu.VMEM((KEYS, PAIR), LOW)] * 2
        + [pltpu.VMEM((PAIR, KEYS), LOW)] * 2
        + [pltpu.VMEM((2, KEYS, ROWS), WIDE)] * 2
        + [pltpu.VMEM((KEYS, 2 * ROWS), LOW)] * 2
        + [pltpu.VMEM((2 * ROWS, PAIR), LOW)] * 2
        + [pltpu.VMEM((KEYS - ROWS, PAIR), WIDE)] * 2,
        pairs * 12 * KEYS * 2 * ROWS * 256,
        pairs * (3 << 20),
    )(ids, offsets, count, queries, grads, keys_own, values_own, *mem, *mem, *far)


def sort_kernel(ids, offsets, own, given, out_0, out_1, out_2, out_3, total):
    outs = (out_0, out_1, out_2, out_3)
    frame = ids[1]
    z_here, x_here, core_here = parts_of(frame)
    partner = frame + 1 - 2 * core_here
    total[...] = jnp.zeros_like(total)
    for reader, part in ((frame, own), (partner, given)):
        for read in range(READS):
            source, live = source_of(offsets, reader, read)
            z_at, x_at, core_at = parts_of(source)
            to = lax.rem(x_at - x_here + 4, 4) * 4 + lax.rem(z_at - z_here + 4, 4)

            @pl.when(jnp.logical_and(live, core_at == core_here))
            def _():
                for kind in range(2):
                    added = part[kind, read * MEM : (read + 1) * MEM, :].astype(WIDE)
                    total[to, kind] = total[to, kind] + added

    for shift in range(4):
        outs[shift][...] = total[4 * shift : 4 * shift + 4].astype(LOW)


def sort_reads(ids, offsets, own, given):
    width = own.shape[2]
    shape = (4, 2, MEM, width)
    return call(
        sort_kernel,
        1,
        2,
        [whole(own.shape)] * 2,
        [whole(shape)] * 4,
        [array(shape, LOW)] * 4,
        [pltpu.VMEM((16, 2, MEM, width), WIDE)],
        0,
        2 << 20,
        vmem=12,
    )(ids, offsets, own, given)


def add_kernel(*refs):
    for group, (first, pairs) in enumerate(GROUPS):
        parts, cols = refs[4 * group : 4 * group + 4], slice(first * PAIR, (first + pairs) * PAIR)
        for shift in range(4):
            total = parts[0][shift].astype(WIDE) + parts[1][shift].astype(WIDE)
            total = total + parts[2][shift].astype(WIDE) + parts[3][shift].astype(WIDE)
            refs[4 * len(GROUPS) + shift][:, :, cols] = total.astype(LOW)


def add_reads(parts):
    return call(
        add_kernel,
        1,
        0,
        [whole(part.shape) for part in parts],
        [whole((2, MEM, INNER))] * 4,
        [array((2, MEM, INNER), LOW)] * 4,
        [],
        0,
        2 << 20,
        vmem=8,
    )(*parts)


def outward_kernel(*refs):
    count = len(GROUPS)
    mixed, grad_query = refs[:count], refs[count : 2 * count]
    w_out, w_query, update, grad_normed = refs[2 * count :]
    total, part = 0.0, 0.0
    for (first, pairs), mixed_ref, grad_ref in zip(GROUPS, mixed, grad_query):
        cols = slice(first * PAIR, (first + pairs) * PAIR)
        total = total + dot(mixed_ref[...], w_out[cols, :])
        part = part + dot_t(grad_ref[...], w_query[:, cols])
    update[...] = total.astype(LOW)
    grad_normed[...] = part


def outward(mixed, grad_query, w_out, w_query):
    width = 512
    out = pl.BlockSpec((ROWS, width), lambda j: (0, j))
    parts = [whole((ROWS, pairs * PAIR)) for _, pairs in GROUPS]
    return call(
        outward_kernel,
        MODEL // width,
        0,
        parts
        + parts
        + [
            pl.BlockSpec((INNER, width), lambda j: (0, j)),
            pl.BlockSpec((width, INNER), lambda j: (j, 0)),
        ],
        [out, out],
        [array((ROWS, MODEL), LOW), array((ROWS, MODEL), WIDE)],
        [],
        4 * ROWS * MODEL * INNER,
        11 << 20,
    )(*mixed, *grad_query, w_out, w_query)


def token_grads_kernel(ids, count, index, *refs):
    groups = len(GROUPS)
    own = (refs[:groups], refs[groups : 2 * groups])
    back, refs = refs[2 * groups : 5 * groups], refs[5 * groups :]
    kept, (tokens, grad_part, w_key, w_value, grad_tokens), refs = refs[:4], refs[4:9], refs[9:]
    total, grad_normed, low, made, out_sem = refs
    camera = ids[0]

    row = lax.broadcasted_iota(jnp.int32, (ROWS, 4 * MEM), 0)
    col = lax.broadcasted_iota(jnp.int32, (ROWS, 4 * MEM), 1)
    hit = row == (col % MEM) * (ROWS // MEM)
    spread = jnp.where(hit, 1.0, 0.0).astype(LOW)
    for kind in range(2):
        stacked = jnp.concatenate([part[kind] for part in kept], axis=0)
        for group, (first, pairs) in enumerate(GROUPS):
            cols = slice(first * PAIR, (first + pairs) * PAIR)
            total[kind, :, cols] = own[kind][group][...] + dot(spread, stacked[:, cols])
    for shift in (1, 2, 3):
        other = lax.rem(camera + shift, 4)
        for slot in range(2):

            @pl.when(slot < count[camera, other])
            def _():
                start = index[camera, slot, other] * STRIP
                at = pl.ds(pl.multiple_of(start, STRIP), STRIP)
                for kind in range(2):
                    for group, (first, pairs) in enumerate(GROUPS):
                        cols = slice(first * PAIR, (first + pairs) * PAIR)
                        given = back[3 * group + shift - 1][kind, slot]
                        total[kind, at, cols] = total[kind, at, cols] + given.astype(WIDE)

    half = ROWS // 2
    stores = []
    for start in range(0, ROWS, half):
        at = slice(start, start + half)
        for kind in range(2):
            low[kind, at, :] = total[kind, at, :].astype(LOW)
        for first in range(0, MODEL, 512):
            cols = slice(first, first + 512)
            grad_normed[at, cols] = (
                grad_part[at, cols]
                + dot_t(low[0, at, :], w_key[cols, :])
                + dot_t(low[1, at, :], w_value[cols, :])
            )
        for begin in range(start, start + half, 64):
            at = slice(begin, begin + 64)
            normed, inverse = normalize(tokens[at, :])
            grad = grad_normed[at, :]
            first_mean = jnp.mean(grad, axis=-1, keepdims=True)
            second_mean = jnp.mean(grad * normed, axis=-1, keepdims=True)
            made[at, :] = (inverse * (grad - first_mean - normed * second_mean)).astype(LOW)
        block = pl.ds(start, half)
        stores.append(
            pltpu.make_async_copy(made.at[block], grad_tokens.at[block], out_sem.at[start // half])
        )
        stores[-1].start()
    for store in stores:
        store.wait()


def token_grads(ids, count, index, own_keys, own_values, back, kept, tokens, grad_part, w_key, w_value):
    operands = (*own_keys, *own_values, *back, *kept, tokens, grad_part, w_key, w_value)
    return pl.pallas_call(
        token_grads_kernel,
        in_specs=[pl.BlockSpec(memory_space=pltpu.SMEM)] * 3
        + [pl.BlockSpec(memory_space=pltpu.VMEM)] * len(operands),
        out_specs=IN_PLACE,
        out_shape=array((ROWS, MODEL), LOW),
        scratch_shapes=[
            pltpu.VMEM((2, ROWS, INNER), WIDE),
            pltpu.VMEM((ROWS, MODEL), WIDE),
            pltpu.VMEM((2, ROWS, INNER), LOW),
            pltpu.VMEM((ROWS, MODEL), LOW),
            pltpu.SemaphoreType.DMA((2,)),
        ],
        compiler_params=pltpu.CompilerParams(vmem_limit_bytes=36 << 20),
        cost_estimate=pl.CostEstimate(
            flops=4 * ROWS * MODEL * INNER, bytes_accessed=16 << 20, transcendentals=0
        ),
        name="token_grads",
    )(ids, count, index, *operands)


def send(value, axis, pairs):
    return lax.ppermute(value, axis, pairs)


def local(tokens, w_query, w_key, w_value, w_out, grad_update, offsets, count, index):
    tokens = tokens.reshape(ROWS, MODEL)
    grad_update = grad_update.reshape(ROWS, MODEL)
    ids = jnp.stack([lax.axis_index("cam"), lax.axis_index("tm")]).astype(jnp.int32)
    index, offsets = jnp.transpose(index, (0, 2, 1)), offsets.T
    others = (1, 2, 3)

    low, keys, values, kept, *sends = project_keys(ids, index, tokens, w_key, w_value)
    far = [send(sends[k - 1], "cam", shift_cam(k)) for k in others]
    along_z = jnp.stack([kept] + [send(kept, "tm", shift_z(k)) for k in others])
    held = [along_z] + [send(along_z, "tm", shift_x(k)) for k in others]
    queries, grads = project_queries(low, grad_update, w_query, w_out)
    for_partner, for_me = pick(ids, offsets, held)
    given = send(for_partner, "tm", SWAP_CORE)
    made, back, parts = [], [], []
    for group in GROUPS:
        args = (queries, grads, keys, values, (for_me, given), far)
        made.append(attention(group, ids, offsets, count, *args))
        for k in others:
            back.append(send(made[-1][5 + k], "cam", shift_cam(-k)))
        mem_given = send(made[-1][5], "tm", SWAP_CORE)
        to_x = sort_reads(ids, offsets, made[-1][4], mem_given)
        parts += [to_x[0]] + [send(to_x[k], "tm", shift_x(k)) for k in others]
    mixed, grad_query, own_keys, own_values = [[m[k] for m in made] for k in range(4)]

    update, grad_part = outward(mixed, grad_query, w_out, w_query)
    sorted_z = add_reads(parts)
    kept_grads = [sorted_z[0]] + [send(sorted_z[k], "tm", shift_z(k)) for k in others]
    args = (own_keys, own_values, back, kept_grads, tokens, grad_part, w_key, w_value)
    grad_tokens = token_grads(ids, count, index, *args)
    shape = (1, 1, ROWS, MODEL)
    return update.reshape(shape), grad_tokens.reshape(shape)


def solution(mesh):
    frames = P("cam", "tm", None, None)
    return jax.shard_map(
        local,
        mesh=mesh,
        in_specs=(frames, P(), P(), P(), P(), frames, P(), P(), P()),
        out_specs=(frames, frames),
        check_vma=False,
    )
```
